32 devices in a mesh: dp: 2 (over x), rows: 16 (over z, y, core).
Axes of the slice: x: 2, y: 2, z: 4, core: 2. Of those that a mesh axis runs over, the one named last changes fastest.
Arguments:
- tokens: bfloat16 [16384, 512], P(('dp', 'rows')), may hold values from -6 to 6
- segment_ids: int32 [1024], P(('dp', 'rows')), may hold values from 0 to 169, never falling along the last dimension, each value on 1 to 8 neighbouring positions
- first_gain: float32 [512], replicated, may hold values from 0.1 to 1.9
- first_shift: float32 [512], replicated, may hold values from -4 to 4
- triple_weight: bfloat16 [512, 1536], replicated, may hold values from -0.25 to 0.25
- output_weight: bfloat16 [512, 512], replicated, may hold values from -0.75 to 0.75
- output_bias: float32 [512], replicated, may hold values from -4 to 4
- second_gain: float32 [512], replicated, may hold values from 0.1 to 1.9
- second_shift: float32 [512], replicated, may hold values from -4 to 4
- expand_weight: bfloat16 [512, 2048], replicated, may hold values from -0.25 to 0.25
- expand_bias: float32 [2048], replicated, may hold values from -6 to 6
- reduce_weight: bfloat16 [2048, 512], replicated, may hold values from -0.1875 to 0.1875
- reduce_bias: float32 [512], replicated, may hold values from -4 to 4
- cotangent: bfloat16 [16384, 512], P(('dp', 'rows')), may hold values from -6 to 6
Outputs:
- layer_out: bfloat16 [16384, 512], P(('dp', 'rows'))
- input_grad: bfloat16 [16384, 512], P(('dp', 'rows'))
- grad_first_gain: float32 [512], replicated
- grad_first_shift: float32 [512], replicated
- grad_triple: float32 [512, 1536], replicated
- grad_output: float32 [512, 512], replicated
- grad_output_bias: float32 [512], replicated
- grad_second_gain: float32 [512], replicated
- grad_second_shift: float32 [512], replicated
- grad_expand: float32 [512, 2048], replicated
- grad_expand_bias: float32 [2048], replicated
- grad_reduce: float32 [2048, 512], replicated
- grad_reduce_bias: float32 [512], replicated
The draws below stay inside these ranges and needn't reach their ends.
Inputs may be any that keep to these rules, and one draw needn't show every extreme that they name: `segment_ids`: sample numbers never fall along the rows and rise by one at each new sample; each sample covers 1 to 8 consecutive rows, and some sample covers exactly 8.
All inputs are finite; a program needn't handle non-finite values.
Results may differ from the reference program's by a relative error of at most 0.011.
Values may be sent and summed in bfloat16 or wider, within the bound.
A program may use at most 128 MiB of HBM per device.

```python
import math
import jax
import jax.numpy as jnp
import numpy as np
from jax import lax

D = 512
HEADS = 16
HEAD_DIM = 32
FF = 2048
LON = 16
SAMPLE_ROWS = 8
BLOCK_ROWS = 32
GROUP_ROWS = 512
TOTAL_ROWS = 1024
TOKENS = 16384
SAMPLES = 170
N_DP = 2


def level_of(rng, extent, cuts, smallest, top_value):
    loudness, own = 1.0, jax.random.fold_in(rng, 6)
    for dim, shards_of in cuts:
        draws = jnp.exp(jax.random.uniform(jax.random.fold_in(own, dim), (shards_of,), jnp.float32, smallest / len(cuts), top_value / len(cuts)))
        loudness = loudness * jnp.repeat(draws, extent[dim] // shards_of).reshape([-1 if axis == dim else 1 for axis in range(len(extent))])
    return loudness


def length_profile(amount, total, limit, lean):
    loads = [(1 << 20) // math.isqrt(standing ** lean) + 1 for standing in range(2, amount + 1)]
    spare, counts = total - limit - (amount - 1), [1] * (amount - 1)
    while spare > 0:
        candidates = [i for i in range(amount - 1) if counts[i] < limit]
        pool, left = sum([loads[i] for i in candidates]), spare
        for i in candidates:
            extra = min(limit - counts[i], max(1, left * loads[i] // pool), spare)
            counts[i] = counts[i] + extra
            spare = spare - extra
    return np.array([limit] + counts)


def ragged_sizes(own_key, amount, total, reach, skew):
    if amount == 2:
        one = jax.random.randint(own_key, (), max(1, total - reach), min(reach, total - 1) + 1)
        return jnp.stack([one, total - one])
    sizes = jnp.asarray(length_profile(amount, total, reach, skew), jnp.int32)
    couples = (amount - 1) // 2
    source_of, sink = sizes[1:1 + 2 * couples:2], sizes[2:2 + 2 * couples:2]
    slack = jnp.minimum(source_of - 1, reach - sink)
    shifted = jax.random.randint(jax.random.fold_in(own_key, 1), (couples,), 0, 1 << 20) % (slack + 1)
    sizes = sizes.at[1:1 + 2 * couples:2].set(source_of - shifted).at[2:2 + 2 * couples:2].set(sink + shifted)
    return sizes[jax.random.permutation(jax.random.fold_in(own_key, 2), amount)]


def bell_draw(rng, extent, deviation, bound, split=(), kind=jnp.bfloat16):
    loudness = level_of(rng, extent, split, -0.22, 0.18) if split else 1.0
    drawn = jax.random.normal(rng, extent, jnp.float32) * deviation * loudness
    return jnp.minimum(jnp.maximum(drawn, -bound), bound).astype(kind)


def setup_inputs(seed: int = 0) -> dict:
    key_list = jax.random.split(jax.random.key(seed), 15)
    return {
        "tokens": bell_draw(key_list[0], (TOKENS, D), 1.0, 6.0, ((0, 32),)),
        "segment_ids": jnp.searchsorted(jnp.cumsum(ragged_sizes(key_list[1], SAMPLES, TOTAL_ROWS, SAMPLE_ROWS, 0)), jnp.arange(TOTAL_ROWS), side="right").astype(jnp.int32),
        "first_gain": jnp.clip(1.0 + 0.18 * jax.random.normal(key_list[2], (D,), jnp.float32), 0.1, 1.9),
        "first_shift": bell_draw(key_list[3], (D,), 0.3, 4.0, (), jnp.float32),
        "triple_weight": bell_draw(key_list[4], (D, 3 * D), D ** -0.5, 0.25),
        "output_weight": bell_draw(key_list[5], (D, D), (D // 8) ** -0.5, 0.75),
        "output_bias": bell_draw(key_list[6], (D,), 0.3, 4.0, (), jnp.float32),
        "second_gain": jnp.clip(1.0 + 0.18 * jax.random.normal(key_list[7], (D,), jnp.float32), 0.1, 1.9),
        "second_shift": bell_draw(key_list[8], (D,), 0.3, 4.0, (), jnp.float32),
        "expand_weight": bell_draw(key_list[9], (D, FF), D ** -0.5, 0.25),
        "expand_bias": bell_draw(key_list[10], (FF,), 0.5, 6.0, (), jnp.float32),
        "reduce_weight": bell_draw(key_list[11], (FF, D), (FF // 2) ** -0.5, 0.1875),
        "reduce_bias": bell_draw(key_list[12], (D,), 0.3, 4.0, (), jnp.float32),
        "cotangent": bell_draw(key_list[13], (TOKENS, D), 1.0, 6.0, ((0, 32),)),
    }


EPSILON = 1e-06
NEGATIVE = -1e+30
TOP_PREC = lax.Precision.HIGHEST

@jax.custom_vjp
def low(v):
    return lax.optimization_barrier(v.astype(jnp.bfloat16)).astype(jnp.float32)

@jax.custom_vjp
def low_back(v):
    return v

def low_keep(v):
    return (low(v), None)

def low_pass(kept, grad):
    return (grad,)

def back_keep(v):
    return (v, None)

def back_low(kept, grad):
    return (low(grad),)
low.defvjp(low_keep, low_pass)
low_back.defvjp(back_keep, back_low)

def layer_norm(values, norm_gain, norm_shift):
    average = lax.optimization_barrier(jnp.mean(values, axis=-1, keepdims=True))
    centred = values - average
    spread = lax.optimization_barrier(jnp.mean(centred * centred, axis=-1, keepdims=True))
    return centred * lax.rsqrt(spread + EPSILON) * norm_gain + norm_shift

def window_mask(query_seg, key_seg):
    query_row = jnp.repeat(jnp.arange(BLOCK_ROWS, dtype=jnp.int32) + 1, LON)
    key_row = jnp.repeat(jnp.arange(BLOCK_ROWS + 2, dtype=jnp.int32), LON)
    query_lon = jnp.tile(jnp.arange(LON, dtype=jnp.int32), BLOCK_ROWS)
    key_lon = jnp.tile(jnp.arange(LON, dtype=jnp.int32), BLOCK_ROWS + 2)
    lon_gap = (query_lon[:, None] - key_lon[None, :]) % LON
    circle = jnp.minimum(lon_gap, LON - lon_gap)
    nearby = (jnp.abs(query_row[:, None] - key_row[None, :]) <= 1) & (circle <= 2)
    same_sample = jnp.repeat(query_seg, LON)[:, None] == jnp.repeat(key_seg, LON)[None, :]
    return nearby & same_sample

def attend_block(queries, key_rows, value_rows, allowed):
    head_scale = HEAD_DIM ** (-0.5)
    query_heads = queries.reshape(-1, HEADS, HEAD_DIM)
    key_heads = key_rows.reshape(-1, HEADS, HEAD_DIM)
    value_heads = value_rows.reshape(-1, HEADS, HEAD_DIM)
    scores = low_back(jnp.einsum('qhd,khd->hqk', query_heads, key_heads, precision=TOP_PREC) * head_scale)
    logits = jnp.where(allowed[None], scores, NEGATIVE)
    largest = lax.optimization_barrier(jnp.max(logits, axis=-1, keepdims=True))
    raised = jnp.exp(logits - largest)
    weights = low(raised / lax.optimization_barrier(jnp.sum(raised, axis=-1, keepdims=True)))
    mixed = jnp.einsum('hqk,khd->qhd', weights, value_heads, precision=TOP_PREC)
    return mixed.reshape(-1, HEADS * HEAD_DIM)

def group_forward(inputs, seg_rows, params):
    first_gain, first_shift, triple_weight, output_weight, output_bias, second_gain, second_shift, expand_weight, expand_bias, reduce_weight, reduce_bias = params
    normed = low(layer_norm(inputs, first_gain, first_shift))
    triple = low_back(low(jnp.dot(normed, triple_weight, precision=TOP_PREC)))
    row_count = seg_rows.shape[0]
    queries = triple[:, :D]
    pairs = jnp.pad(triple[:, D:].reshape(row_count, LON, 2 * D), ((1, 1), (0, 0), (0, 0)))
    seg_padded = jnp.pad(seg_rows, 1, constant_values=-1)
    block_count = row_count // BLOCK_ROWS
    query_blocks = queries.reshape(block_count, BLOCK_ROWS * LON, D)

    def one_block(element):
        block_index, query_block = element
        first_row = block_index * BLOCK_ROWS
        pair_block = lax.dynamic_slice_in_dim(pairs, first_row, BLOCK_ROWS + 2, 0).reshape(-1, 2 * D)
        allowed = window_mask(lax.dynamic_slice_in_dim(seg_rows, first_row, BLOCK_ROWS, 0), lax.dynamic_slice_in_dim(seg_padded, first_row, BLOCK_ROWS + 2, 0))
        return attend_block(query_block, pair_block[:, :D], pair_block[:, D:], allowed)
    attended = lax.map(jax.checkpoint(one_block), (jnp.arange(block_count, dtype=jnp.int32), query_blocks))
    attended = low_back(low(attended.reshape(-1, D)))
    hidden_state = inputs + low_back(jnp.dot(attended, output_weight, precision=TOP_PREC) + output_bias)

    def feed_forward(state_rows):
        second = low(layer_norm(state_rows, second_gain, second_shift))
        expanded = low_back(jnp.dot(second, expand_weight, precision=TOP_PREC) + expand_bias)
        activated = low(jax.nn.gelu(expanded, approximate=False))
        return state_rows + low_back(jnp.dot(activated, reduce_weight, precision=TOP_PREC) + reduce_bias)
    token_count = hidden_state.shape[0]
    piece_rows = math.gcd(token_count, 4096)
    result = lax.map(jax.checkpoint(feed_forward), hidden_state.reshape(token_count // piece_rows, piece_rows, D))
    return result.reshape(token_count, D)

def reference(tokens, segment_ids, first_gain, first_shift, triple_weight, output_weight, output_bias, second_gain, second_shift, expand_weight, expand_bias, reduce_weight, reduce_bias, cotangent):
    params = tuple((element.astype(jnp.float32) for element in (first_gain, first_shift, triple_weight, output_weight, output_bias, second_gain, second_shift, expand_weight, expand_bias, reduce_weight, reduce_bias)))
    inputs = tokens.astype(jnp.float32).reshape(N_DP, GROUP_ROWS * LON, D)
    seg_groups = segment_ids.reshape(N_DP, GROUP_ROWS)

    def forward(all_inputs, weights_all):

        def per_group(element):
            return jax.checkpoint(group_forward)(element[0], element[1], weights_all)
        return lax.map(per_group, (all_inputs, seg_groups))
    outputs, pullback = jax.vjp(forward, inputs, params)
    input_grad, weight_grads = pullback(cotangent.astype(jnp.float32).reshape(N_DP, GROUP_ROWS * LON, D))
    factor = TOKENS ** (-0.5)
    scaled = [gradient * factor for gradient in weight_grads]
    return (outputs.reshape(TOKENS, D).astype(jnp.bfloat16), input_grad.reshape(TOKENS, D).astype(jnp.bfloat16), scaled[0], scaled[1], scaled[2], scaled[3], scaled[4], scaled[5], scaled[6], scaled[7], scaled[8], scaled[9], scaled[10])
```

```python
from functools import partial

import jax
import jax.numpy as jnp
from jax import lax
from jax.experimental import pallas as pl
from jax.experimental.pallas import tpu as pltpu
from jax.sharding import PartitionSpec as P

HEADS = 16
HEAD_DIM = 32
LON = 16
BLOCK_ROWS = 32


EPSILON = 1e-06
NEGATIVE = -1e30


def extended(x, sides, width):
    for axis, dim in sides:
        size, length = (lax.axis_size(axis), x.shape[dim])
        up = [(i, (i + 1) % size) for i in range(size - 1)]
        down = [(j, i) for i, j in up]
        last = lax.slice_in_dim(x, length - width, length, axis=dim)
        initial = lax.slice_in_dim(x, 0, width, axis=dim)
        before = lax.ppermute(last, axis, up)
        after = lax.ppermute(initial, axis, down)
        x = jnp.concatenate([before, x, after], axis=dim)
    return x


def norm_forward(values, norm_gain, norm_shift):
    average = jnp.mean(values, axis=-1, keepdims=True)
    centred = values - average
    inv_dev = lax.rsqrt(jnp.mean(centred * centred, axis=-1, keepdims=True) + EPSILON)
    standard = centred * inv_dev
    return (standard * norm_gain + norm_shift, standard, inv_dev)


def norm_backward(incoming, standard, inv_dev, norm_gain):
    scaled = incoming * norm_gain
    bracket = (
        scaled
        - jnp.mean(scaled, axis=-1, keepdims=True)
        - standard * jnp.mean(scaled * standard, axis=-1, keepdims=True)
    )
    return (inv_dev * bracket, jnp.sum(incoming * standard, axis=0), jnp.sum(incoming, axis=0))


def window_mask(query_seg, key_seg):
    query_row = jnp.repeat(jnp.arange(BLOCK_ROWS, dtype=jnp.int32) + 1, LON)
    key_row = jnp.repeat(jnp.arange(BLOCK_ROWS + 2, dtype=jnp.int32), LON)
    query_lon = jnp.tile(jnp.arange(LON, dtype=jnp.int32), BLOCK_ROWS)
    key_lon = jnp.tile(jnp.arange(LON, dtype=jnp.int32), BLOCK_ROWS + 2)
    lon_gap = (query_lon[:, None] - key_lon[None, :]) % LON
    circle = jnp.minimum(lon_gap, LON - lon_gap)
    nearby = (jnp.abs(query_row[:, None] - key_row[None, :]) <= 1) & (circle <= 2)
    same_sample = jnp.repeat(query_seg, LON)[:, None] == jnp.repeat(key_seg, LON)[None, :]
    return nearby & same_sample


def outer_sum(left, right):
    return lax.dot_general(
        left, right, (((0,), (0,)), ((), ())), preferred_element_type=jnp.float32
    )


def times_transposed(left, right):
    return lax.dot_general(
        left, right, (((1,), (1,)), ((), ())), preferred_element_type=jnp.float32
    )


def head_split(values):
    return values.reshape(values.shape[0], HEADS, HEAD_DIM)


def block_logits(queries, key_rows, allowed):
    scores = jnp.einsum(
        "qhd,khd->hqk",
        head_split(queries),
        head_split(key_rows),
        preferred_element_type=jnp.float32,
    ) * HEAD_DIM ** (-0.5)
    return jnp.where(allowed[None], scores, NEGATIVE)


MESH_ID = pl.DeviceIdType.MESH


def span_of(start, size, unit):
    if isinstance(start, int):
        return pl.ds(start, size)
    return pl.ds(pl.multiple_of(start, unit), size)


class Link:
    def __init__(self, dp_count, row_count):
        self.dp, self.row = lax.axis_index("dp"), lax.axis_index("rows")
        self.sizes = {"core": 2, "x": dp_count, "y": 2, "z": row_count // 4}
        core, y, z = self.row % 2, (self.row // 2) % 2, self.row // 4
        self.place = {"core": core, "x": self.dp, "y": y, "z": z}
        self.row_count = row_count

    def peer(self, dim, step):
        n, here = self.sizes[dim], self.place[dim]
        there = lax.rem(here + step, n)
        if dim == "x":
            return (there, self.row)
        stride = {"core": 1, "y": 2, "z": 4}[dim]
        return (self.dp, self.row + (there - here) * stride)

    def beside(self, step):
        return (self.dp, lax.rem(self.row + step + self.row_count, self.row_count))

    def greet(self):
        barrier = pltpu.get_barrier_semaphore()
        peers = [self.peer(d, s) for d in self.sizes for s in range(1, self.sizes[d])]
        peers += [self.beside(1), self.beside(-1)]
        for device in peers:
            pl.semaphore_signal(barrier, inc=1, device_id=device, device_id_type=MESH_ID)
        pl.semaphore_wait(barrier, len(peers))


def piece_grid(dim, n, rows, columns):
    if dim != "z":
        return n, 1
    across = min(n, columns // 128)
    return n // across, across


def phase_shapes(shape, order, sizes):
    shapes, (rows, columns) = [], shape
    for dim in order:
        down, across = piece_grid(dim, sizes[dim], rows, columns)
        rows, columns = rows // down, columns // across
        shapes.append((sizes[dim] - 1, rows, columns))
    return shapes


class Part:
    def __init__(self, link, source, result, shape, order, boxes, send_sems, recv_sems):
        self.link, self.source, self.result, self.order = link, source, result, order
        self.boxes, self.send_sems, self.recv_sems = boxes, send_sems, recv_sems
        self.shape = shape
        self.regions = [(0, shape[0], 0, shape[1])]
        self.next_sem = 0
        self.pending = []

    def copy(self, source, target, device):
        i = self.next_sem
        self.next_sem += 1
        made = pltpu.make_async_remote_copy(
            src_ref=source, dst_ref=target, send_sem=self.send_sems.at[i],
            recv_sem=self.recv_sems.at[i], device_id=device, device_id_type=MESH_ID)
        made.start()
        self.pending.append(made)

    def wait(self):
        for made in self.pending:
            made.wait()
        self.pending = []

    def cut(self, phase, which):
        dim = self.order[phase]
        _, rows, _, columns = self.regions[phase]
        down, across = piece_grid(dim, self.link.sizes[dim], rows, columns)
        height, width = rows // down, columns // across
        if across == 1:
            return which * height, height, 0, width
        return (which // across) * height, height, lax.rem(which, across) * width, width

    def view(self, ref, place):
        top, height, left, width = place
        if width == ref.shape[1]:
            return ref.at[span_of(top, height, 16), :]
        return ref.at[span_of(top, height, 16), span_of(left, width, 128)]

    def scatter(self, phase):
        dim = self.order[phase]
        n, here = self.link.sizes[dim], self.link.place[dim]
        for step in range(1, n):
            place = self.cut(phase, lax.rem(here + step, n))
            self.copy(self.view(self.source, place), self.boxes[phase].at[step - 1], self.link.peer(dim, step))

    def gain(self, phase):
        self.wait()
        dim = self.order[phase]
        n = self.link.sizes[dim]
        own = self.cut(phase, self.link.place[dim])
        box = self.boxes[phase]
        last = phase == len(self.order) - 1
        top, height, left, width = own
        base_top, _, base_left, _ = self.regions[phase]
        self.regions.append((base_top + top, height, base_left + left, width))
        mine = self.view(self.source, own)
        target = self.view(self.result, self.regions[-1]) if last else box.at[0]
        rows = min(height, 32)

        @pl.loop(0, height // rows)
        def _(i):
            span = pl.ds(pl.multiple_of(i * rows, rows), rows)
            total = mine[span, :].astype(jnp.float32)
            for slot in range(n - 1):
                total += box[slot, span, :].astype(jnp.float32)
            target[span, :] = total.astype(jnp.bfloat16)

        self.source = box.at[0]

    def spread(self, phase):
        dim = self.order[phase]
        for step in range(1, self.link.sizes[dim]):
            where = self.view(self.result, self.regions[phase + 1])
            self.copy(where, where, self.link.peer(dim, step))


def part_scratch(shape, order, sizes):
    copies = 2 * sum(sizes[d] - 1 for d in order)
    boxes = [pltpu.VMEM(s, jnp.bfloat16) for s in phase_shapes(shape, order, sizes)]
    return boxes + [pltpu.SemaphoreType.DMA((copies,)), pltpu.SemaphoreType.DMA((copies,))]


def vector_scratch(shape, sizes):
    order = ("core", "x", "y", "z")
    boxes = [pltpu.VMEM((sizes[d] - 1,) + shape, jnp.float32) for d in order]
    copies = sum(sizes[d] - 1 for d in order)
    return boxes + [pltpu.SemaphoreType.DMA((copies,)), pltpu.SemaphoreType.DMA((copies,))]


class Vectors:
    def __init__(self, link, work, boxes, send_sems, recv_sems):
        self.link, self.work, self.boxes = link, work, boxes
        self.send_sems, self.recv_sems = send_sems, recv_sems
        self.order = ("core", "x", "y", "z")
        self.next_sem, self.pending = 0, []

    def send(self, phase):
        dim = self.order[phase]
        for step in range(1, self.link.sizes[dim]):
            i = self.next_sem
            self.next_sem += 1
            made = pltpu.make_async_remote_copy(
                src_ref=self.work.at[phase], dst_ref=self.boxes[phase].at[step - 1],
                send_sem=self.send_sems.at[i], recv_sem=self.recv_sems.at[i],
                device_id=self.link.peer(dim, step), device_id_type=MESH_ID)
            made.start()
            self.pending.append(made)

    def gain(self, phase):
        for made in self.pending:
            made.wait()
        self.pending = []
        total = self.work[phase]
        for slot in range(self.link.sizes[self.order[phase]] - 1):
            total = total + self.boxes[phase][slot]
        self.work[phase + 1] = total


def sum_parts(width, ff):
    half = ff // 2
    return [
        ("reduce", (half, width), ("core", "x", "y", "z")),
        ("reduce", (half, width), ("core", "y", "x", "z")),
        ("expand", (width, half), ("core", "x", "y", "z")),
        ("expand", (width, half), ("core", "y", "x", "z")),
        ("mixed", (width, 2 * width), ("core", "x", "y", "z")),
        ("mixed", (width, 2 * width), ("core", "y", "x", "z")),
    ]


def sum_kernel(sizes, counts, width, ff, reduce_ref, expand_ref, mixed_ref, vectors_ref,
               reduce_out, expand_out, mixed_out, vectors_out, work, *scratch):
    link = Link(sizes["x"], counts)
    link.greet()
    half = ff // 2
    at = {}
    scratch = list(scratch)
    parts = []
    for name, shape, order in sum_parts(width, ff):
        source, result = {"reduce": (reduce_ref, reduce_out), "expand": (expand_ref, expand_out),
                          "mixed": (mixed_ref, mixed_out)}[name]
        turn = at.get(name, 0)
        at[name] = turn + 1
        spot = pl.ds(turn * shape[0], shape[0]) if name == "reduce" else pl.ds(turn * shape[1], shape[1])
        where = (spot, slice(None)) if name == "reduce" else (slice(None), spot)
        boxes, scratch = scratch[:4], scratch[4:]
        send_sems, recv_sems = scratch[:2]
        scratch = scratch[2:]
        parts.append(Part(link, source.at[where], result.at[where], shape, order, boxes, send_sems, recv_sems))
    vectors = Vectors(link, work, scratch[:4], scratch[4], scratch[5])
    work[0] = vectors_ref[...]
    vectors.send(0)
    for phase in range(4):
        for part in parts:
            if phase:
                part.gain(phase - 1)
            part.scatter(phase)
        vectors.gain(phase)
        if phase < 3:
            vectors.send(phase + 1)
    vectors_out[...] = work[4]
    for part in parts:
        part.gain(3)
        part.spread(3)
    for phase in (2, 1, 0):
        for part in parts:
            part.wait()
            part.spread(phase)
    for part in parts:
        part.wait()


def sum_over_devices(reduce_grad, expand_grad, mixed_grad, vectors, dp_count, row_count):
    ff, width = reduce_grad.shape
    sizes = {"core": 2, "x": dp_count, "y": 2, "z": row_count // 4}
    scratch = [pltpu.VMEM((5,) + vectors.shape, jnp.float32)]
    for _, shape, order in sum_parts(width, ff):
        scratch += part_scratch(shape, order, sizes)
    scratch += vector_scratch(vectors.shape, sizes)
    arrays = (reduce_grad, expand_grad, mixed_grad, vectors)
    return pl.pallas_call(
        partial(sum_kernel, sizes, row_count, width, ff),
        out_shape=[jax.ShapeDtypeStruct(a.shape, a.dtype) for a in arrays],
        in_specs=[pl.BlockSpec(memory_space=pltpu.VMEM)] * 4,
        out_specs=[pl.BlockSpec(memory_space=pltpu.VMEM)] * 4,
        scratch_shapes=scratch,
        compiler_params=pltpu.CompilerParams(collective_id=1, has_side_effects=True, vmem_limit_bytes=48 << 20),
        name="sum_over_devices",
    )(*arrays)


def body(
    tokens,
    segment_ids,
    first_gain,
    first_shift,
    triple_weight,
    output_weight,
    output_bias,
    second_gain,
    second_shift,
    expand_weight,
    expand_bias,
    reduce_weight,
    reduce_bias,
    cotangent,
):
    model_width = output_weight.shape[0]
    row_count = segment_ids.shape[0]
    token_count = tokens.shape[0]
    block_count = row_count // BLOCK_ROWS
    query_span = BLOCK_ROWS * LON
    key_span = (BLOCK_ROWS + 2) * LON
    head_scale = HEAD_DIM ** (-0.5)
    inputs = tokens.astype(jnp.float32)
    band_index = lax.axis_index("rows")
    band_count = lax.axis_size("rows")
    seg_ext = extended(segment_ids, (("rows", 0),), 1)
    ext_row = jnp.arange(row_count + 2, dtype=jnp.int32)
    inside = ((ext_row > 0) | (band_index > 0)) & (
        (ext_row < row_count + 1) | (band_index < band_count - 1)
    )
    seg_ext = jnp.where(inside, seg_ext, -1)
    first_out, first_std, first_inv = norm_forward(inputs, first_gain, first_shift)
    first_low = first_out.astype(jnp.bfloat16)
    triple = jnp.dot(first_low, triple_weight, preferred_element_type=jnp.float32).astype(
        jnp.bfloat16
    )
    queries = triple[:, :model_width]
    pair_ext = extended(
        triple[:, model_width:].reshape(row_count, LON, 2 * model_width), (("rows", 0),), 1
    )

    def block_inputs(block_index):
        first_row = block_index * BLOCK_ROWS
        pair_block = pair_ext.reshape(key_span, 2 * model_width)
        allowed = window_mask(
            lax.dynamic_slice_in_dim(seg_ext, first_row + 1, BLOCK_ROWS, 0), seg_ext
        )
        key_rows = pair_block[:, :model_width]
        value_rows = pair_block[:, model_width:]
        return (first_row, queries, key_rows, value_rows, block_logits(queries, key_rows, allowed))

    def forward_block(block_index):
        pieces = block_inputs(block_index)
        logits = pieces[4]
        largest = jnp.max(logits, axis=-1, keepdims=True)
        raised = jnp.exp(logits - largest)
        denominator = jnp.sum(raised, axis=-1, keepdims=True)
        weights = (raised / denominator).astype(jnp.bfloat16)
        mixed = jnp.einsum(
            "hqk,khd->qhd", weights, head_split(pieces[3]), preferred_element_type=jnp.float32
        )
        return (
            mixed.reshape(query_span, model_width).astype(jnp.bfloat16),
            (largest + jnp.log(denominator))[..., 0],
        )

    attended, log_totals = lax.map(forward_block, jnp.arange(block_count, dtype=jnp.int32))
    attended = attended.reshape(token_count, model_width)
    hidden_state = (
        inputs + jnp.dot(attended, output_weight, preferred_element_type=jnp.float32) + output_bias
    )
    second_out, second_std, second_inv = norm_forward(hidden_state, second_gain, second_shift)
    second_low = second_out.astype(jnp.bfloat16)
    expanded = jnp.dot(second_low, expand_weight, preferred_element_type=jnp.float32) + expand_bias
    activated, gelu_back = jax.vjp(partial(jax.nn.gelu, approximate=False), expanded)
    activated_low = activated.astype(jnp.bfloat16)
    layer_out = (
        hidden_state
        + jnp.dot(activated_low, reduce_weight, preferred_element_type=jnp.float32)
        + reduce_bias
    ).astype(jnp.bfloat16)
    upstream = cotangent.astype(jnp.float32)
    grad_reduce = outer_sum(activated_low, cotangent)
    grad_reduce_bias = jnp.sum(upstream, axis=0)
    expanded_grad = gelu_back(times_transposed(cotangent, reduce_weight))[0].astype(jnp.bfloat16)
    grad_expand = outer_sum(second_low, expanded_grad)
    grad_expand_bias = jnp.sum(expanded_grad.astype(jnp.float32), axis=0)
    second_grad = times_transposed(expanded_grad, expand_weight)
    state_part, grad_second_gain, grad_second_shift = norm_backward(
        second_grad, second_std, second_inv, second_gain
    )
    state_grad = upstream + state_part
    branch_grad = state_grad.astype(jnp.bfloat16)
    grad_output = outer_sum(attended, branch_grad)
    grad_output_bias = jnp.sum(branch_grad.astype(jnp.float32), axis=0)
    attended_grad = times_transposed(branch_grad, output_weight).astype(jnp.bfloat16)

    def backward_block(block_index, state_pair):
        query_grads, pair_grads = state_pair
        first_row, query_block, key_rows, value_rows, logits = block_inputs(block_index)
        weights = jnp.exp(logits - log_totals[block_index][..., None])
        upstream_block = head_split(attended_grad)
        weight_grads = jnp.einsum(
            "qhd,khd->hqk",
            upstream_block,
            head_split(value_rows),
            preferred_element_type=jnp.float32,
        )
        centre = jnp.sum(weights * weight_grads, axis=-1, keepdims=True)
        score_grads = (weights * (weight_grads - centre)).astype(jnp.bfloat16)
        query_part = (
            jnp.einsum(
                "hqk,khd->qhd",
                score_grads,
                head_split(key_rows),
                preferred_element_type=jnp.float32,
            )
            * head_scale
        )
        key_part = (
            jnp.einsum(
                "hqk,qhd->khd",
                score_grads,
                head_split(query_block),
                preferred_element_type=jnp.float32,
            )
            * head_scale
        )
        value_part = jnp.einsum(
            "hqk,qhd->khd",
            weights.astype(jnp.bfloat16),
            upstream_block,
            preferred_element_type=jnp.float32,
        )
        query_grads = query_part.reshape(query_span, model_width)
        pair_part = jnp.concatenate(
            [
                key_part.reshape(BLOCK_ROWS + 2, LON, model_width),
                value_part.reshape(BLOCK_ROWS + 2, LON, model_width),
            ],
            axis=-1,
        )
        current = pair_grads
        pair_grads = current + pair_part
        return (query_grads, pair_grads)

    start_state = (
        jnp.zeros((token_count, model_width), jnp.float32),
        jnp.zeros((row_count + 2, LON, 2 * model_width), jnp.float32),
    )
    query_grads, pair_grads = lax.fori_loop(0, block_count, backward_block, start_state)
    rim_grads = extended(
        jnp.stack([pair_grads[0], pair_grads[row_count + 1]]).astype(jnp.bfloat16),
        (("rows", 0),),
        1,
    ).astype(jnp.float32)
    own_grads = pair_grads[1 : row_count + 1]
    own_grads = own_grads.at[0].add(rim_grads[0]).at[row_count - 1].add(rim_grads[3])
    triple_grad = jnp.concatenate(
        [query_grads, own_grads.reshape(token_count, 2 * model_width)], axis=1
    ).astype(jnp.bfloat16)
    grad_triple = outer_sum(first_low, triple_grad)
    first_grad = times_transposed(triple_grad, triple_weight)
    input_part, grad_first_gain, grad_first_shift = norm_backward(
        first_grad, first_std, first_inv, first_gain
    )
    input_grad = (state_grad + input_part).astype(jnp.bfloat16)
    small = [grad_first_gain, grad_first_shift, grad_output_bias, grad_second_gain, grad_second_shift]
    small = jnp.concatenate(
        [jnp.stack(small), grad_expand_bias.reshape(-1, model_width), grad_reduce_bias[None]]
    )
    small = jnp.pad(small, ((0, -small.shape[0] % 8), (0, 0)))
    low = jnp.bfloat16
    total_reduce, total_expand, total_mixed, total_small = sum_over_devices(
        grad_reduce.astype(low),
        grad_expand.astype(low),
        jnp.concatenate([grad_triple.astype(low), grad_output.astype(low)], axis=1),
        small,
        lax.axis_size("dp"),
        band_count,
    )
    factor = (token_count * lax.axis_size("dp") * band_count) ** (-0.5)
    total_small = total_small * factor
    bias_rows = grad_expand_bias.shape[0] // model_width
    wide = jnp.float32
    return (
        layer_out,
        input_grad,
        total_small[0],
        total_small[1],
        total_mixed[:, : 3 * model_width].astype(wide) * factor,
        total_mixed[:, 3 * model_width :].astype(wide) * factor,
        total_small[2],
        total_small[3],
        total_small[4],
        total_expand.astype(wide) * factor,
        total_small[5 : 5 + bias_rows].reshape(-1),
        total_reduce.astype(wide) * factor,
        total_small[5 + bias_rows],
    )


def solution(mesh):
    placed = (
        P(("dp", "rows"), None),
        P(("dp", "rows")),
        P(),
        P(),
        P(),
        P(),
        P(),
        P(),
        P(),
        P(),
        P(),
        P(),
        P(),
        P(("dp", "rows"), None),
    )
    return jax.shard_map(
        body,
        mesh=mesh,
        in_specs=placed,
        out_specs=(
            P(("dp", "rows"), None),
            P(("dp", "rows"), None),
            P(),
            P(),
            P(),
            P(),
            P(),
            P(),
            P(),
            P(),
            P(),
            P(),
            P(),
        ),
        check_vma=False,
    )
```

```python
from functools import partial

import jax
import jax.numpy as jnp
from jax import lax
from jax.experimental import pallas as pl
from jax.experimental.pallas import tpu as pltpu
from jax.sharding import PartitionSpec as P

HEAD_DIM = 32
LON = 16
EPSILON = 1e-06
NEGATIVE = -1e30

MESH_ID = pl.DeviceIdType.MESH


def span_of(start, size, unit):
    if isinstance(start, int):
        return pl.ds(start, size)
    return pl.ds(pl.multiple_of(start, unit), size)


class Link:
    def __init__(self, dp_count, row_count):
        self.dp, self.row = lax.axis_index("dp"), lax.axis_index("rows")
        self.sizes = {"core": 2, "x": dp_count, "y": 2, "z": row_count // 4}
        core, y, z = self.row % 2, (self.row // 2) % 2, self.row // 4
        self.place = {"core": core, "x": self.dp, "y": y, "z": z}
        self.row_count = row_count

    def peer(self, dim, step):
        n, here = self.sizes[dim], self.place[dim]
        there = lax.rem(here + step, n)
        if dim == "x":
            return (there, self.row)
        stride = {"core": 1, "y": 2, "z": 4}[dim]
        return (self.dp, self.row + (there - here) * stride)

    def beside(self, step):
        return (self.dp, lax.rem(self.row + step + self.row_count, self.row_count))

    def peers(self):
        found = [self.peer(d, s) for d in self.sizes for s in range(1, self.sizes[d])]
        return found + [self.beside(1), self.beside(-1)]

    def signal(self):
        barrier = pltpu.get_barrier_semaphore()
        for device in self.peers():
            pl.semaphore_signal(barrier, inc=1, device_id=device, device_id_type=MESH_ID)

    def await_all(self):
        pl.semaphore_wait(pltpu.get_barrier_semaphore(), len(self.peers()))


def piece_grid(dim, n, rows, columns):
    if dim != "z":
        return n, 1
    across = min(n, columns // 128)
    return n // across, across


def phase_shapes(shape, order, sizes):
    shapes, (rows, columns) = [], shape
    for dim in order:
        down, across = piece_grid(dim, sizes[dim], rows, columns)
        rows, columns = rows // down, columns // across
        shapes.append((sizes[dim] - 1, rows, columns))
    return shapes


class Part:
    def __init__(self, link, source, result, shape, order, boxes, send_sems, recv_sems):
        self.link, self.source, self.result, self.order = link, source, result, order
        self.boxes, self.send_sems, self.recv_sems = boxes, send_sems, recv_sems
        self.shape = shape
        self.regions = [(0, shape[0], 0, shape[1])]
        self.next_sem = 0
        self.pending = []

    def copy(self, source, target, device):
        i = self.next_sem
        self.next_sem += 1
        made = pltpu.make_async_remote_copy(
            src_ref=source, dst_ref=target, send_sem=self.send_sems.at[i],
            recv_sem=self.recv_sems.at[i], device_id=device, device_id_type=MESH_ID)
        made.start()
        self.pending.append(made)

    def wait(self):
        for made in self.pending:
            made.wait()
        self.pending = []

    def cut(self, phase, which):
        dim = self.order[phase]
        _, rows, _, columns = self.regions[phase]
        down, across = piece_grid(dim, self.link.sizes[dim], rows, columns)
        height, width = rows // down, columns // across
        if across == 1:
            return which * height, height, 0, width
        return (which // across) * height, height, lax.rem(which, across) * width, width

    def view(self, ref, place):
        top, height, left, width = place
        if width == ref.shape[1]:
            return ref.at[span_of(top, height, 16), :]
        return ref.at[span_of(top, height, 16), span_of(left, width, 128)]

    def scatter(self, phase):
        dim = self.order[phase]
        n, here = self.link.sizes[dim], self.link.place[dim]
        for step in range(1, n):
            place = self.cut(phase, lax.rem(here + step, n))
            self.copy(self.view(self.source, place), self.boxes[phase].at[step - 1], self.link.peer(dim, step))

    def gain(self, phase):
        self.wait()
        dim = self.order[phase]
        n = self.link.sizes[dim]
        own = self.cut(phase, self.link.place[dim])
        box = self.boxes[phase]
        last = phase == len(self.order) - 1
        top, height, left, width = own
        base_top, _, base_left, _ = self.regions[phase]
        self.regions.append((base_top + top, height, base_left + left, width))
        mine = self.view(self.source, own)
        target = self.view(self.result, self.regions[-1]) if last else box.at[0]
        rows = min(height, 32)

        @pl.loop(0, height // rows)
        def _(i):
            span = pl.ds(pl.multiple_of(i * rows, rows), rows)
            total = mine[span, :].astype(jnp.float32)
            for slot in range(n - 1):
                total += box[slot, span, :].astype(jnp.float32)
            target[span, :] = total.astype(jnp.bfloat16)

        self.source = box.at[0]

    def spread(self, phase):
        dim = self.order[phase]
        for step in range(1, self.link.sizes[dim]):
            where = self.view(self.result, self.regions[phase + 1])
            self.copy(where, where, self.link.peer(dim, step))


def part_scratch(shape, order, sizes):
    copies = 2 * sum(sizes[d] - 1 for d in order)
    boxes = [pltpu.VMEM(s, jnp.bfloat16) for s in phase_shapes(shape, order, sizes)]
    return boxes + [pltpu.SemaphoreType.DMA((copies,)), pltpu.SemaphoreType.DMA((copies,))]


def vector_scratch(shape, sizes):
    order = ("core", "x", "y", "z")
    boxes = [pltpu.VMEM((sizes[d] - 1,) + shape, jnp.float32) for d in order]
    copies = sum(sizes[d] - 1 for d in order)
    return boxes + [pltpu.SemaphoreType.DMA((copies,)), pltpu.SemaphoreType.DMA((copies,))]


class Vectors:
    def __init__(self, link, work, boxes, send_sems, recv_sems):
        self.link, self.work, self.boxes = link, work, boxes
        self.send_sems, self.recv_sems = send_sems, recv_sems
        self.order = ("core", "x", "y", "z")
        self.next_sem, self.pending = 0, []

    def send(self, phase):
        dim = self.order[phase]
        for step in range(1, self.link.sizes[dim]):
            i = self.next_sem
            self.next_sem += 1
            made = pltpu.make_async_remote_copy(
                src_ref=self.work.at[phase], dst_ref=self.boxes[phase].at[step - 1],
                send_sem=self.send_sems.at[i], recv_sem=self.recv_sems.at[i],
                device_id=self.link.peer(dim, step), device_id_type=MESH_ID)
            made.start()
            self.pending.append(made)

    def gain(self, phase):
        for made in self.pending:
            made.wait()
        self.pending = []
        total = self.work[phase]
        for slot in range(self.link.sizes[self.order[phase]] - 1):
            total = total + self.boxes[phase][slot]
        self.work[phase + 1] = total


def nn(left, right):
    return lax.dot_general(left, right, (((1,), (0,)), ((), ())), preferred_element_type=jnp.float32)


def nt(left, right):
    return lax.dot_general(left, right, (((1,), (1,)), ((), ())), preferred_element_type=jnp.float32)


def tn(left, right):
    return lax.dot_general(left, right, (((0,), (0,)), ((), ())), preferred_element_type=jnp.float32)


def aligned(index, size):
    if isinstance(index, int):
        return pl.ds(index * size, size)
    return pl.ds(pl.multiple_of(index * size, size), size)


def column_sum(values):
    return jnp.sum(values, axis=0, keepdims=True)


def row_mean(values):
    return jnp.mean(values, axis=-1, keepdims=True)


ROWS = 64
KEYS = 96
GROUP = 128
STACK = 256
SQRT_HALF = 0.5 ** 0.5
DENSITY = (2.0 * 3.141592653589793) ** (-0.5)


def part_list(width, ff):
    half = ff // 2
    xyz, yxz = ("core", "x", "y", "z"), ("core", "y", "x", "z")
    wide = [(half, width), (width, half)]
    square = [(width, width), (width, width)]
    return [(s, o) for pair in (wide, wide, square, square) for s, o in zip(pair, (xyz, yxz))]


class Group:
    def __init__(self, parts):
        self.parts, self.step = parts, 0

    def go(self):
        step = self.step
        self.step += 1
        for part in self.parts:
            if step == 0:
                part.scatter(0)
            elif step <= 3:
                part.gain(step - 1)
                part.scatter(step)
            elif step == 4:
                part.gain(3)
                part.spread(3)
            elif step <= 7:
                part.wait()
                part.spread(7 - step)
            else:
                part.wait()


def layer_kernel(sizes, row_count, width, ff, *refs):
    refs = list(refs)

    def take(n):
        taken = refs[:n]
        del refs[:n]
        return taken

    (tok_hbm, cot_hbm, wqkv_hbm, wo_hbm, w1_hbm, w2_hbm) = take(6)
    (seg_ref, gain1, shift1, bias_o, gain2, shift2, bias_1, bias_2) = take(8)
    (out_ref, dx_ref, reduce_out, expand_out, low_out, high_out, vec_out) = take(7)
    (tok, cot, wqkv, wo, w1, w2, load_sems) = take(7)
    (a1, hat1, inv1, q, kv, prob, att, hid, hat2, inv2, a2) = take(11)
    (pre, dact, act, dpre, outacc, da, dhid, db, dout, dkv, dqkv) = take(11)
    (p_reduce, p_expand, p_low, p_high, vec, bias, head_mask) = take(7)
    (seg_box, rim_send, rim_box, rim_sems) = take(4)
    low = jnp.bfloat16
    wide = jnp.float32
    tokens = tok.shape[0]
    rows_here = seg_ref.shape[1]
    blocks = tokens // ROWS
    groups = width // GROUP
    scale = HEAD_DIM ** (-0.5)

    loads = []
    for i, (source, target) in enumerate(
        ((tok_hbm, tok), (wqkv_hbm, wqkv), (wo_hbm, wo), (cot_hbm, cot), (w1_hbm, w1), (w2_hbm, w2))
    ):
        made = pltpu.make_async_copy(source, target, load_sems.at[i])
        made.start()
        loads.append(made)

    link = Link(sizes["x"], row_count)
    link.signal()

    lane = lax.broadcasted_iota(jnp.int32, (ROWS, GROUP), 1) // HEAD_DIM
    for h in range(4):
        head_mask[pl.ds(h * ROWS, ROWS), :] = jnp.where(lane == h, 1.0, 0.0).astype(low)

    def stack_heads(block):
        return jnp.concatenate([block] * 4, axis=0) * head_mask[...]

    def pick_heads(stacked):
        picked = stacked[3 * ROWS :]
        for h in (2, 1, 0):
            picked = jnp.where(lane == h, stacked[h * ROWS : (h + 1) * ROWS], picked)
        return picked

    loads[0].wait()

    def norm(values, gain, shift, hat_ref, inv_ref, out, span):
        centred = values - row_mean(values)
        inv = lax.rsqrt(row_mean(centred * centred) + EPSILON)
        hat = centred * inv
        hat_ref[span, :] = hat
        inv_ref[span, :] = inv
        out[span, :] = (hat * gain[...] + shift[...]).astype(low)

    @pl.loop(0, blocks)
    def _(i):
        span = aligned(i, ROWS)
        norm(tok[span, :].astype(wide), gain1, shift1, hat1, inv1, a1, span)

    loads[1].wait()

    @pl.loop(0, 2)
    def _(i):
        columns = aligned(i, STACK)
        made = nn(a1[...], wqkv[:, columns])
        q[:, columns] = made.astype(low)

    for which in range(2):

        @pl.loop(0, 2)
        def _(i):
            columns = aligned(i, STACK)
            source = pl.ds(pl.multiple_of((which + 1) * width + i * STACK, STACK), STACK)
            kv[which, LON : LON + tokens, columns] = nn(a1[...], wqkv[:, source]).astype(low)

    link.await_all()
    edge = LON + tokens
    left, right = link.beside(-1), link.beside(1)
    halo = []
    for i, (source, target, device) in enumerate(
        (
            (kv.at[:, pl.ds(LON, LON), :], kv.at[:, pl.ds(edge, LON), :], left),
            (kv.at[:, pl.ds(tokens, LON), :], kv.at[:, pl.ds(0, LON), :], right),
            (seg_ref, seg_box.at[1], left),
            (seg_ref, seg_box.at[0], right),
        )
    ):
        made = pltpu.make_async_remote_copy(
            src_ref=source, dst_ref=target, send_sem=rim_sems.at[0, i], recv_sem=rim_sems.at[1, i],
            device_id=device, device_id_type=MESH_ID)
        made.start()
        halo.append(made)
    for made in halo:
        made.wait()

    before = jnp.where(link.row > 0, seg_box[0, :, rows_here - 1 : rows_here], -1)
    after = jnp.where(link.row < row_count - 1, seg_box[1, :, 0:1], -1)
    tall = rows_here + 8
    slot = lax.broadcasted_iota(jnp.int32, (tall, rows_here), 0)
    place = lax.broadcasted_iota(jnp.int32, (tall, rows_here), 1)
    own = jnp.broadcast_to(seg_ref[...].astype(wide), (tall, rows_here))
    seg_column = jnp.sum(jnp.where(slot == place + 1, own, 0.0), axis=1, keepdims=True)
    slot = lax.broadcasted_iota(jnp.int32, (tall, 1), 0)
    seg_column = jnp.where(slot == 0, before.astype(wide), seg_column)
    seg_column = jnp.where(slot == rows_here + 1, after.astype(wide), seg_column)

    key = lax.broadcasted_iota(jnp.int32, (KEYS, STACK), 0)
    query = lax.broadcasted_iota(jnp.int32, (KEYS, STACK), 1) % ROWS
    gap = (query - key + 2 * LON) % LON
    near = (jnp.abs(key // LON - query // LON - 1) <= 1) & (jnp.minimum(gap, LON - gap) <= 2)
    spread_slot = lax.broadcasted_iota(jnp.int32, (tall, STACK), 0)
    spread_query = (lax.broadcasted_iota(jnp.int32, (tall, STACK), 1) % ROWS) // LON
    spread_seg = jnp.broadcast_to(seg_column, (tall, STACK))
    key_slot = lax.broadcasted_iota(jnp.int32, (KEYS, STACK), 0) // LON

    @pl.loop(0, blocks)
    def _(i):
        first = i * (ROWS // LON)
        query_seg = jnp.sum(
            jnp.where(spread_slot == spread_query + (first + 1), spread_seg, 0.0), axis=0, keepdims=True)
        key_seg = jnp.zeros((KEYS, STACK), wide)
        for r in range(KEYS // LON):
            row_seg = jnp.sum(jnp.where(slot == first + r, seg_column, 0.0), axis=0, keepdims=True)
            key_seg = jnp.where(key_slot == r, row_seg, key_seg)
        bias[i] = jnp.where(near & (key_seg == query_seg), 0.0, NEGATIVE)

    @pl.loop(0, blocks)
    def _(i):
        span = aligned(i, ROWS)
        keys = pl.ds(pl.multiple_of(i * ROWS, ROWS), KEYS)
        for g in range(groups):
            lanes = pl.ds(g * GROUP, GROUP)
            scores = nt(kv[0, keys, lanes], stack_heads(q[span, lanes])) * scale + bias[i]
            raised = jnp.exp(scores - jnp.max(scores, axis=0, keepdims=True))
            weights = raised * (1.0 / column_sum(raised))
            prob[i * groups + g] = weights
            mixed = tn(weights.astype(low), kv[1, keys, lanes])
            att[span, lanes] = pick_heads(mixed).astype(low)

    loads[2].wait()
    for i in range(2):
        columns = pl.ds(i * STACK, STACK)
        hid[:, columns] = tok[:, columns].astype(wide) + nn(att[...], wo[:, columns]) + bias_o[:, columns]

    @pl.loop(0, blocks)
    def _(i):
        span = aligned(i, ROWS)
        norm(hid[span, :], gain2, shift2, hat2, inv2, a2, span)

    for made in loads[3:]:
        made.wait()

    shapes = part_list(width, ff)
    half = ff // 2
    spots = [
        (p_reduce.at[pl.ds(0, half)], reduce_out.at[pl.ds(0, half)]),
        (p_expand.at[:, pl.ds(0, half)], expand_out.at[:, pl.ds(0, half)]),
        (p_reduce.at[pl.ds(half, half)], reduce_out.at[pl.ds(half, half)]),
        (p_expand.at[:, pl.ds(half, half)], expand_out.at[:, pl.ds(half, half)]),
        (p_low.at[:, pl.ds(0, width)], low_out.at[:, pl.ds(0, width)]),
        (p_low.at[:, pl.ds(width, width)], low_out.at[:, pl.ds(width, width)]),
        (p_high.at[:, pl.ds(0, width)], high_out.at[:, pl.ds(0, width)]),
        (p_high.at[:, pl.ds(width, width)], high_out.at[:, pl.ds(width, width)]),
    ]
    parts = []
    for (shape, order), (source, result) in zip(shapes, spots):
        scratch = take(6)
        parts.append(Part(link, source, result, shape, order, scratch[:4], scratch[4], scratch[5]))
    flows = [Group(parts[i : i + 2]) for i in range(0, 8, 2)]
    scratch = take(6)
    vectors = Vectors(link, vec, scratch[:4], scratch[4], scratch[5])

    vec[0] = jnp.zeros(vec.shape[1:], wide)
    outacc[...] = jnp.zeros(outacc.shape, wide)
    da[...] = jnp.zeros(da.shape, wide)

    def feed(j):
        columns = aligned(j, STACK)
        w1_part, w2_part = w1[:, columns], w2[columns, :]
        pre[...] = nn(a2[...], w1_part) + bias_1[:, columns]
        dact[...] = nt(cot[...], w2_part)

        def gelu(i, total):
            span = aligned(i, 32)
            x = pre[span, :]
            cdf = 0.5 + 0.5 * lax.erf(x * SQRT_HALF)
            act[span, :] = (x * cdf).astype(low)
            slope = cdf + x * (jnp.exp(x * x * (-0.5)) * DENSITY)
            made = (dact[span, :] * slope).astype(low)
            dpre[span, :] = made
            return total + jnp.sum(made.astype(wide).reshape(4, 8, STACK), axis=0)

        total = lax.fori_loop(0, tokens // 32, gelu, jnp.zeros((8, STACK), wide))
        return total, columns

    def feed_products(columns):
        w1_part, w2_part = w1[:, columns], w2[columns, :]
        outacc[...] += nn(act[...], w2_part)
        da[...] += nt(dpre[...], w1_part)
        p_reduce[columns, :] = tn(act[...], cot[...]).astype(low)
        p_expand[:, columns] = tn(a2[...], dpre[...]).astype(low)

    per_row = width // STACK
    for part in range(2):
        for j in range(half // STACK):
            index = part * (half // STACK) + j
            total, columns = feed(index)
            feed_products(columns)
            vec[0, 5 + index // per_row : 6 + index // per_row, pl.ds((index % per_row) * STACK, STACK)] = column_sum(total)
            if part == 1 and j in (0, 2):
                flows[0].go()
        flows[part].go()

    def norm_back(incoming, hat_ref, inv_ref, gain, span):
        hat = hat_ref[span, :]
        scaled = incoming * gain[...]
        bracket = scaled - row_mean(scaled) - hat * row_mean(scaled * hat)
        return inv_ref[span, :] * bracket, hat

    def fold(values):
        return jnp.sum(values.reshape(values.shape[0] // 8, 8, values.shape[1]), axis=0)

    def second_back(i, totals):
        span = aligned(i, ROWS)
        incoming = da[span, :]
        part, hat = norm_back(incoming, hat2, inv2, gain2, span)
        up = cot[span, :].astype(wide)
        state = up + part
        dhid[span, :] = state
        rounded = state.astype(low)
        db[span, :] = rounded
        out_ref[span, :] = (hid[span, :] + outacc[span, :] + bias_2[...]).astype(low)
        added = (rounded.astype(wide), incoming * hat, incoming, up)
        return tuple(t + fold(a) for t, a in zip(totals, added))

    zero = jnp.zeros((8, width), wide)
    totals = lax.fori_loop(0, blocks, second_back, (zero,) * 4)
    for at, total in zip((2, 3, 4, 9), totals):
        vec[0, at : at + 1, :] = column_sum(total)

    flows[1].go()
    dout[...] = nt(db[...], wo[...]).astype(low)
    for i, target in enumerate((p_low, p_high)):
        target[:, 3 * STACK :] = tn(att[...], db[:, i * STACK : (i + 1) * STACK]).astype(low)
    flows[0].go()

    dkv[...] = jnp.zeros(dkv.shape, wide)

    def attention_back(pair):
        @pl.loop(0, blocks)
        def _(i):
            span = aligned(i, ROWS)
            keys = pl.ds(pl.multiple_of(i * ROWS, ROWS), KEYS)
            for g in (2 * pair, 2 * pair + 1):
                lanes = pl.ds(g * GROUP, GROUP)
                stacked_out = stack_heads(dout[span, lanes])
                stacked_query = stack_heads(q[span, lanes])
                weights = prob[i * groups + g]
                slopes = nt(kv[1, keys, lanes], stacked_out)
                centre = column_sum(weights * slopes)
                ds = (weights * (slopes - centre)).astype(low)
                dkv[0, keys, lanes] += nn(ds, stacked_query) * scale
                dkv[1, keys, lanes] += nn(weights.astype(low), stacked_out)
                dqkv[span, lanes] = (pick_heads(tn(ds, kv[0, keys, lanes])) * scale).astype(low)

    def rim_start(pair):
        lanes = pl.ds(pair * STACK, STACK)
        rim_send[pair, 0] = dkv[:, 0:LON, lanes].astype(low)
        rim_send[pair, 1] = dkv[:, edge : edge + LON, lanes].astype(low)
        made = []
        for side, device in ((0, left), (1, right)):
            copy = pltpu.make_async_remote_copy(
                src_ref=rim_send.at[pair, side], dst_ref=rim_box.at[pair, side],
                send_sem=rim_sems.at[0, 4 + 2 * pair + side], recv_sem=rim_sems.at[1, 4 + 2 * pair + side],
                device_id=device, device_id_type=MESH_ID)
            copy.start()
            made.append(copy)
        return made

    def rim_finish(pair, copies):
        for copy in copies:
            copy.wait()
        lanes = pl.ds(pair * STACK, STACK)
        dkv[:, tokens : tokens + LON, lanes] += rim_box[pair, 0].astype(wide)
        dkv[:, LON : 2 * LON, lanes] += rim_box[pair, 1].astype(wide)

    def triple_products(pair, target):
        for which in range(2):
            columns = pl.ds((which + 1) * width + pair * STACK, STACK)
            dqkv[:, columns] = dkv[which, LON : LON + tokens, pl.ds(pair * STACK, STACK)].astype(low)
        for which in range(3):
            columns = pl.ds(which * width + pair * STACK, STACK)
            target[:, which * STACK : (which + 1) * STACK] = tn(a1[...], dqkv[:, columns]).astype(low)

    attention_back(0)
    copies = rim_start(0)
    flows[1].go()
    flows[0].go()
    attention_back(1)
    rim_finish(0, copies)
    copies = rim_start(1)
    triple_products(0, p_low)
    flows[2].go()
    flows[1].go()
    flows[0].go()
    rim_finish(1, copies)
    triple_products(1, p_high)
    flows[3].go()
    flows[2].go()

    da[...] = nt(dqkv[...], wqkv[...])
    flows[1].go()
    flows[0].go()

    def first_back(i, totals):
        span = aligned(i, ROWS)
        incoming = da[span, :]
        part, hat = norm_back(incoming, hat1, inv1, gain1, span)
        dx_ref[span, :] = (dhid[span, :] + part).astype(low)
        return totals[0] + fold(incoming * hat), totals[1] + fold(incoming)

    totals = lax.fori_loop(0, blocks, first_back, (zero,) * 2)
    for at, total in zip((0, 1), totals):
        vec[0, at : at + 1, :] = column_sum(total)
    vectors.send(0)

    turns = [flow for flow in flows]
    phase = 0
    while any(flow.step < 9 for flow in flows):
        for flow in flows:
            if flow.step < 9 and flow.step <= min(f.step for f in flows) + 3:
                flow.go()
        if phase < 4:
            vectors.gain(phase)
            if phase < 3:
                vectors.send(phase + 1)
            phase += 1
    vec_out[...] = vec[4]


def run_layer(arrays, dp_count, row_count):
    (tokens, cotangent, wqkv, wo, w1, w2, seg, *vectors) = arrays
    count, width = tokens.shape
    ff = w1.shape[1]
    sizes = {"core": 2, "x": dp_count, "y": 2, "z": row_count // 4}
    low, wide = jnp.bfloat16, jnp.float32
    keys = count + 2 * LON
    blocks = count // ROWS
    vm = pltpu.VMEM
    square = (count, width)
    vec_shape = (16, width)
    scratch = [vm(square, low), vm(square, low), vm(wqkv.shape, low), vm(wo.shape, low), vm(w1.shape, low),
               vm(w2.shape, low), pltpu.SemaphoreType.DMA((6,))]
    scratch += [vm(square, low), vm(square, wide), vm((count, 1), wide), vm(square, low), vm((2, keys, width), low),
                vm((blocks * width // GROUP, KEYS, STACK), wide), vm(square, low), vm(square, wide),
                vm(square, wide), vm((count, 1), wide), vm(square, low)]
    scratch += [vm((count, STACK), wide), vm((count, STACK), wide), vm((count, STACK), low), vm((count, STACK), low),
                vm(square, wide), vm(square, wide), vm(square, wide), vm(square, low), vm(square, low),
                vm((2, keys, width), wide), vm((count, 3 * width), low)]
    scratch += [vm((ff, width), low), vm((width, ff), low), vm((width, 2 * width), low), vm((width, 2 * width), low),
                vm((5,) + vec_shape, wide), vm((blocks, KEYS, STACK), wide), vm((STACK, GROUP), low)]
    scratch += [vm((2,) + seg.shape, jnp.int32), vm((2, 2, 2, LON, STACK), low), vm((2, 2, 2, LON, STACK), low),
                pltpu.SemaphoreType.DMA((2, 8))]
    for shape, order in part_list(width, ff):
        scratch += part_scratch(shape, order, sizes)
    scratch += vector_scratch(vec_shape, sizes)
    shapes = [(square, low), (square, low), ((ff, width), low), ((width, ff), low), ((width, 2 * width), low),
              ((width, 2 * width), low), (vec_shape, wide)]
    vmem = pl.BlockSpec(memory_space=pltpu.VMEM)
    return pl.pallas_call(
        partial(layer_kernel, sizes, row_count, width, ff),
        out_shape=[jax.ShapeDtypeStruct(s, t) for s, t in shapes],
        in_specs=[pl.BlockSpec(memory_space=pl.ANY)] * 6 + [vmem] * 8,
        out_specs=[vmem] * 7,
        scratch_shapes=scratch,
        compiler_params=pltpu.CompilerParams(collective_id=1, has_side_effects=True, vmem_limit_bytes=60 << 20),
        name="layer",
    )(*arrays)


def widen_kernel(factor, width, reduce_ref, expand_ref, low_ref, high_ref, vec_ref,
                 triple_out, output_out, expand_out, reduce_out, *vector_outs):
    wide = jnp.float32
    reduce_out[...] = reduce_ref[...].astype(wide) * factor
    expand_out[...] = expand_ref[...].astype(wide) * factor
    for pair, ref in enumerate((low_ref, high_ref)):
        for which in range(3):
            at = which * width + pair * STACK
            triple_out[:, at : at + STACK] = ref[:, which * STACK : (which + 1) * STACK].astype(wide) * factor
        output_out[:, pair * STACK : (pair + 1) * STACK] = ref[:, 3 * STACK :].astype(wide) * factor

    @pl.when(pl.program_id(0) == 0)
    def _():
        values = vec_ref[...] * factor
        for at, ref in zip((0, 1, 2, 3, 4, 9), vector_outs[:5] + vector_outs[6:]):
            ref[...] = values[at : at + 1]
        many = vector_outs[5].shape[1] // width
        for i in range(many):
            vector_outs[5][:, i * width : (i + 1) * width] = values[5 + i : 6 + i]


def widen(sums, factor, steps=8):
    reduce_sum, expand_sum, low_sum, high_sum, vec = sums
    ff, width = reduce_sum.shape

    def spec(shape):
        return pl.BlockSpec((shape[0] // steps, shape[1]), lambda i: (i, 0))

    def whole(shape):
        return pl.BlockSpec(shape, lambda i: (0, 0))

    outs = [(width, 3 * width), (width, width), (width, ff), (ff, width)]
    small = [(1, width)] * 5 + [(1, ff), (1, width)]
    return pl.pallas_call(
        partial(widen_kernel, factor, width),
        grid=(steps,),
        out_shape=[jax.ShapeDtypeStruct(s, jnp.float32) for s in outs + small],
        in_specs=[spec(a.shape) for a in (reduce_sum, expand_sum, low_sum, high_sum)] + [whole(vec.shape)],
        out_specs=[spec(s) for s in outs] + [whole(s) for s in small],
        compiler_params=pltpu.CompilerParams(vmem_limit_bytes=32 << 20),
        name="widen",
    )(reduce_sum, expand_sum, low_sum, high_sum, vec)


def body(
    tokens,
    segment_ids,
    first_gain,
    first_shift,
    triple_weight,
    output_weight,
    output_bias,
    second_gain,
    second_shift,
    expand_weight,
    expand_bias,
    reduce_weight,
    reduce_bias,
    cotangent,
):
    dp_count, row_count = lax.axis_size("dp"), lax.axis_size("rows")
    flat = [
        v.reshape(1, -1)
        for v in (segment_ids, first_gain, first_shift, output_bias, second_gain, second_shift, expand_bias, reduce_bias)
    ]
    layer_out, input_grad, *sums = run_layer(
        (tokens, cotangent, triple_weight, output_weight, expand_weight, reduce_weight, *flat), dp_count, row_count)
    factor = (tokens.shape[0] * dp_count * row_count) ** (-0.5)
    triple, output, expand, reduce, *small = widen(sums, factor)
    small = [v.reshape(-1) for v in small]
    return (
        layer_out, input_grad, small[0], small[1], triple, output, small[2], small[3], small[4],
        expand, small[5], reduce, small[6],
    )


def solution(mesh):
    placed = (
        P(("dp", "rows"), None),
        P(("dp", "rows")),
        P(),
        P(),
        P(),
        P(),
        P(),
        P(),
        P(),
        P(),
        P(),
        P(),
        P(),
        P(("dp", "rows"), None),
    )
    return jax.shard_map(
        body,
        mesh=mesh,
        in_specs=placed,
        out_specs=(
            P(("dp", "rows"), None),
            P(("dp", "rows"), None),
            P(),
            P(),
            P(),
            P(),
            P(),
            P(),
            P(),
            P(),
            P(),
            P(),
            P(),
        ),
        check_vma=False,
    )
```

```python
from functools import partial

import jax
import jax.numpy as jnp
from jax import lax
from jax.experimental import pallas as pl
from jax.experimental.pallas import tpu as pltpu
from jax.sharding import PartitionSpec as P

HEAD_DIM = 32
LON = 16
EPSILON = 1e-06
NEGATIVE = -1e30

MESH_ID = pl.DeviceIdType.MESH


def span_of(start, size, unit):
    if isinstance(start, int):
        return pl.ds(start, size)
    return pl.ds(pl.multiple_of(start, unit), size)


class Link:
    def __init__(self, dp_count, row_count):
        self.dp, self.row = lax.axis_index("dp"), lax.axis_index("rows")
        self.sizes = link_sizes(dp_count, row_count)
        z = self.row // 4
        self.place = {
            "core": self.row % 2, "x": self.dp, "y": (self.row // 2) % 2, "z": z, "zl": z % 2, "zh": z // 2,
            "yz": self.row // 2, "xz": z * dp_count + self.dp}
        self.row_count = row_count

    def peer(self, dim, step):
        n, here = self.sizes[dim], self.place[dim]
        there = lax.rem(here + step, n)
        if dim == "x":
            return (there, self.row)
        if dim == "xz":
            wide = self.sizes["x"]
            return (lax.rem(there, wide), self.row + (there // wide - here // wide) * 4)
        if dim == "yz":
            return (self.dp, self.row + (there - here) * 2)
        stride = {"core": 1, "y": 2, "z": 4, "zl": 4, "zh": 8}[dim]
        return (self.dp, self.row + (there - here) * stride)

    def beside(self, step):
        return (self.dp, lax.rem(self.row + step + self.row_count, self.row_count))

    def peers(self):
        found = [self.peer(d, s) for d in ("core", "x", "yz", "xz") for s in range(1, self.sizes[d])]
        return found + [self.beside(1), self.beside(-1)]

    def signal(self):
        barrier = pltpu.get_barrier_semaphore()
        for device in self.peers():
            pl.semaphore_signal(barrier, inc=1, device_id=device, device_id_type=MESH_ID)

    def await_all(self):
        pl.semaphore_wait(pltpu.get_barrier_semaphore(), len(self.peers()))


def link_sizes(dp_count, row_count):
    deep = row_count // 4
    return {"core": 2, "x": dp_count, "y": 2, "z": deep, "zl": 2, "zh": deep // 2,
            "yz": 2 * deep, "xz": dp_count * deep}


def remote(source, target, sems, i, device):
    return pltpu.make_async_remote_copy(
        src_ref=source, dst_ref=target, send_sem=sems.at[0, i], recv_sem=sems.at[1, i],
        device_id=device, device_id_type=MESH_ID)


def piece_grid(dim, n, columns):
    if "z" not in dim or dim == "zl":
        return n, 1
    across = min(n, columns // 128)
    return n // across, across


def phase_shapes(shape, order, sizes):
    shapes, (rows, columns) = [], shape
    for dim in order:
        down, across = piece_grid(dim, sizes[dim], columns)
        rows, columns = rows // down, columns // across
        shapes.append((sizes[dim] - 1, rows, columns))
    return shapes


class Part:
    def __init__(self, link, source, result, final, order, boxes, sems, final_sem):
        self.link, self.source, self.result, self.order = link, source, result, order
        self.final, self.boxes, self.sems, self.final_sem = final, boxes, sems, final_sem
        self.step = 0
        top, left = 0, 0
        rows, columns = source.shape
        self.cuts, self.regions, self.first_sem = [], [], []
        used = 0
        for dim in order:
            n, here = link.sizes[dim], link.place[dim]
            down, across = piece_grid(dim, n, columns)
            rows, columns = rows // down, columns // across
            places = []
            for step in range(n):
                which = lax.rem(here + step, n)
                if across == 1:
                    places.append((which * rows, rows, 0, columns))
                else:
                    places.append(((which // across) * rows, rows, lax.rem(which, across) * columns, columns))
            self.cuts.append(places)
            top, left = top + places[0][0], left + places[0][2]
            self.regions.append((top, rows, left, columns))
            self.first_sem.append(used)
            used += n - 1
        self.spread_sem = used

    @property
    def last(self):
        return 2 * len(self.order)

    def view(self, ref, place):
        top, height, left, width = place
        rows = span_of(top, height, 16)
        if width == ref.shape[1]:
            return ref.at[rows, :]
        return ref.at[rows, span_of(left, width, 128)]

    def input_of(self, phase):
        return self.source if phase == 0 else self.boxes[phase - 1].at[0]

    def scatter(self, phase):
        dim = self.order[phase]
        return [
            remote(self.view(self.input_of(phase), self.cuts[phase][step]), self.boxes[phase].at[step - 1],
                   self.sems, self.first_sem[phase] + step - 1, self.link.peer(dim, step))
            for step in range(1, self.link.sizes[dim])
        ]

    def spread(self, phase):
        dim = self.order[phase]
        where = self.view(self.result, self.regions[phase])
        return [
            remote(where, where, self.sems, self.spread_sem + self.first_sem[phase] + step - 1,
                   self.link.peer(dim, step))
            for step in range(1, self.link.sizes[dim])
        ]

    def flush(self):
        return pltpu.make_async_copy(self.result, self.final, self.final_sem)

    def gain(self, phase):
        box = self.boxes[phase]
        _, height, _, _ = self.cuts[phase][0]
        mine = self.view(self.input_of(phase), self.cuts[phase][0])
        if phase == len(self.order) - 1:
            target = self.view(self.result, self.regions[phase])
        else:
            target = box.at[0]
        rows = min(height, 32)

        @pl.loop(0, height // rows)
        def _(i):
            span = pl.ds(pl.multiple_of(i * rows, rows), rows)
            if box.shape[0] == 1:
                target[span, :] = mine[span, :] + box[0, span, :]
            else:
                total = mine[span, :].astype(jnp.float32)
                for slot in range(box.shape[0]):
                    total += box[slot, span, :].astype(jnp.float32)
                target[span, :] = total.astype(jnp.bfloat16)

    def moves(self, step):
        depth = len(self.order)
        return self.scatter(step) if step < depth else self.spread(2 * depth - 1 - step)

    def start(self):
        if self.step < 2 * len(self.order):
            for move in self.moves(self.step):
                move.start()
        else:
            self.flush().start()
        self.step += 1

    def finish(self):
        for move in self.moves(self.step - 1):
            move.wait()
        if self.step <= len(self.order):
            self.gain(self.step - 1)


def part_scratch(shape, order, sizes):
    copies = 2 * sum(sizes[d] - 1 for d in order)
    boxes = [pltpu.VMEM(s, jnp.bfloat16) for s in phase_shapes(shape, order, sizes)]
    return boxes + [pltpu.SemaphoreType.DMA((2, copies))]


VECTOR_ORDER = ("core", "x", "y", "z")


def vector_scratch(shape, sizes):
    boxes = [pltpu.VMEM((sizes[d] - 1,) + shape, jnp.float32) for d in VECTOR_ORDER]
    copies = sum(sizes[d] - 1 for d in VECTOR_ORDER)
    return boxes + [pltpu.SemaphoreType.DMA((2, copies))]


class Vectors:
    def __init__(self, link, work, boxes, sems):
        self.link, self.work, self.boxes, self.sems = link, work, boxes, sems
        self.step = 0
        self.last = len(VECTOR_ORDER)

    def moves(self, phase):
        dim = VECTOR_ORDER[phase]
        first = sum(self.link.sizes[d] - 1 for d in VECTOR_ORDER[:phase])
        return [
            remote(self.work.at[phase], self.boxes[phase].at[step - 1], self.sems, first + step - 1,
                   self.link.peer(dim, step))
            for step in range(1, self.link.sizes[dim])
        ]

    def start(self):
        for move in self.moves(self.step):
            move.start()
        self.step += 1

    def finish(self):
        for move in self.moves(self.step - 1):
            move.wait()
        total = self.work[self.step - 1]
        for slot in range(self.boxes[self.step - 1].shape[0]):
            total = total + self.boxes[self.step - 1][slot]
        self.work[self.step] = total


def nn(left, right):
    return lax.dot_general(left, right, (((1,), (0,)), ((), ())), preferred_element_type=jnp.float32)


def nt(left, right):
    return lax.dot_general(left, right, (((1,), (1,)), ((), ())), preferred_element_type=jnp.float32)


def tn(left, right):
    return lax.dot_general(left, right, (((0,), (0,)), ((), ())), preferred_element_type=jnp.float32)


def aligned(index, size):
    if isinstance(index, int):
        return pl.ds(index * size, size)
    return pl.ds(pl.multiple_of(index * size, size), size)


def column_sum(values):
    return jnp.sum(values, axis=0, keepdims=True)


def row_mean(values):
    return jnp.mean(values, axis=-1, keepdims=True)


ROWS = 64
KEYS = 96
GROUP = 128
STACK = 256
UNROLL = 8
SQRT_HALF = 0.5 ** 0.5
DENSITY = (2.0 * 3.141592653589793) ** (-0.5)


ORDERS = (
    ("core", "x", "y", "z"),
    ("core", "y", "x", "z"),
    ("core", "zl", "x", "y", "zh"),
    ("core", "zl", "y", "x", "zh"),
    ("core", "x", "yz"),
    ("core", "y", "xz"),
)
FINISH = 100
KINDS = (2, 3, 0, 1, 2, 3, 0, 1, 0, 1, 0, 1)
PLAN = (
    (),
    (0, 1),
    (),
    (2, 3, 100, 0, 101, 1),
    (102, 2, 103, 3),
    (4, 5),
    (),
    (7, 6, 104, 4, 105, 5, 102, 2, 103, 3),
    (100, 0, 101, 1, 107, 106, 6),
    (),
    (),
    (102, 103),
    (7,),
    (),
    (),
    (2, 3),
    (),
    (),
    (),
    (101, 1),
    (100, 0, 104, 4),
    (105,),
    (5,),
    (),
    (),
    (106,),
    (),
    (104,),
    (4, 108, 8, 105, 5),
    (0,),
    (1,),
    (),
    (),
    (106, 6, 107, 7),
    (101,),
    (4, 105),
    (5, 0, 109, 9),
    (),
    (1,),
    (),
    (),
    (108, 106, 6, 107, 7, 102, 2, 104),
    (8, 6, 107, 7, 102, 2, 103, 3, 101, 100),
    (9, 102, 2, 104, 103, 3, 100),
    (10, 8, 103, 105, 100),
    (11, 4, 5, 0, 101, 1, 110, 10, 109),
    (9, 3, 106, 107, 111, 108, 8),
    (12, 102, 2, 104, 105, 100, 101),
    (5, 11, 112, 108, 8, 102, 2, 7, 0, 109, 9, 103, 3, 4, 110, 105, 103, 3, 10, 108, 12, 111, 11, 5, 109, 9, 104, 4, 107, 100, 0, 8, 112, 110, 10, 7, 109, 9, 105, 111, 11, 104, 108, 8, 6, 4, 110, 10, 109, 9, 107, 7, 100, 0, 111, 11, 106, 6, 107, 7, 100, 0, 108, 8, 1, 110, 5, 108, 8, 10, 109, 9, 111, 11, 12, 104, 4, 101, 1, 109, 9, 106, 6, 104, 4, 110, 10, 106, 6, 112, 12, 111, 11, 105, 5, 105, 5, 101, 1, 110, 10, 112, 101, 1, 111, 11, 110, 10, 111, 11),
)


def layer_kernel(sizes, row_count, width, ff, *refs):
    refs = list(refs)

    def take(n):
        taken = refs[:n]
        del refs[:n]
        return taken

    (tok_hbm, cot_hbm, wqkv_hbm, wo_hbm, w1_hbm, w2_hbm) = take(6)
    small_hbm = take(8)
    (out_hbm, dx_hbm, sums_hbm, vec_out) = take(4)
    (tok, cot, wqkv, wo, w1, w2, load_sems) = take(7)
    small = take(8)
    (seg_ref, gain1, shift1, bias_o, gain2, shift2, bias_1, bias_2) = small
    (a1, hat1, inv1, q, kv, prob, att, hid, hat2, inv2, a2) = take(11)
    (pre, dact, act, dpre, outacc, da, dhid, db, dout, dkv, dqkv) = take(11)
    (grads, sums, out_ref, dx_ref, vec, head_mask) = take(6)
    (seg_box, rim_send, rim_box, rim_sems, store_sems) = take(5)
    low = jnp.bfloat16
    wide = jnp.float32
    tokens = tok.shape[0]
    rows_here = seg_ref.shape[1]
    blocks = tokens // ROWS
    groups = width // GROUP
    scale = HEAD_DIM ** (-0.5)

    link = Link(sizes["x"], row_count)
    link.signal()
    loads = [
        pltpu.make_async_copy(source, target, load_sems.at[i])
        for i, (source, target) in enumerate(
            ((tok_hbm, tok), (wqkv_hbm, wqkv), (wo_hbm, wo), (cot_hbm, cot), (w1_hbm, w1), (w2_hbm, w2)))
    ]
    small_loads = [
        pltpu.make_async_copy(source, target, load_sems.at[6 + i])
        for i, (source, target) in enumerate(zip(small_hbm, small))
    ]
    loads[0].start()
    for made in small_loads:
        made.start()
    loads[1].start()

    lane = lax.broadcasted_iota(jnp.int32, (ROWS, GROUP), 1) // HEAD_DIM
    for h in range(4):
        head_mask[pl.ds(h * ROWS, ROWS), :] = jnp.where(lane == h, 1.0, 0.0).astype(low)

    def stack_heads(block):
        return jnp.concatenate([block] * 4, axis=0) * head_mask[...]

    def pick_heads(stacked):
        picked = stacked[3 * ROWS :]
        for h in (2, 1, 0):
            picked = jnp.where(lane == h, stacked[h * ROWS : (h + 1) * ROWS], picked)
        return picked

    loads[0].wait()
    for made in small_loads:
        made.wait()

    def norm(values, gain, shift, hat_ref, inv_ref, out, span):
        centred = values - row_mean(values)
        inv = lax.rsqrt(row_mean(centred * centred) + EPSILON)
        hat = centred * inv
        hat_ref[span, :] = hat
        inv_ref[span, :] = inv
        out[span, :] = (hat * gain[...] + shift[...]).astype(low)

    @pl.loop(0, blocks)
    def _(i):
        span = aligned(i, ROWS)
        norm(tok[span, :].astype(wide), gain1, shift1, hat1, inv1, a1, span)

    loads[1].wait()
    for made in loads[2:]:
        made.start()
    for which in range(2):

        @pl.loop(0, 2)
        def _(i):
            columns = aligned(i, STACK)
            source = pl.ds(pl.multiple_of((which + 1) * width + i * STACK, STACK), STACK)
            kv[which, LON : LON + tokens, columns] = nn(a1[...], wqkv[:, source]).astype(low)

    link.await_all()
    edge = LON + tokens
    left, right = link.beside(-1), link.beside(1)
    halo = [
        remote(source, target, rim_sems, i, device)
        for i, (source, target, device) in enumerate(
            (
                (kv.at[:, pl.ds(LON, LON), :], kv.at[:, pl.ds(edge, LON), :], left),
                (kv.at[:, pl.ds(tokens, LON), :], kv.at[:, pl.ds(0, LON), :], right),
                (seg_ref, seg_box.at[1], left),
                (seg_ref, seg_box.at[0], right),
            )
        )
    ]
    for made in halo:
        made.start()

    @pl.loop(0, 2)
    def _(i):
        columns = aligned(i, STACK)
        q[:, columns] = nn(a1[...], wqkv[:, columns]).astype(low)

    tall = rows_here + 8
    slot = lax.broadcasted_iota(jnp.int32, (tall, rows_here), 0)
    place = lax.broadcasted_iota(jnp.int32, (tall, rows_here), 1)
    own = jnp.broadcast_to(seg_ref[...].astype(wide), (tall, rows_here))
    inner_seg = jnp.sum(jnp.where(slot == place + 1, own, 0.0), axis=1, keepdims=True)
    slot = lax.broadcasted_iota(jnp.int32, (tall, 1), 0)
    key = lax.broadcasted_iota(jnp.int32, (KEYS, STACK), 0)
    query = lax.broadcasted_iota(jnp.int32, (KEYS, STACK), 1) % ROWS
    gap = (query - key + 2 * LON) % LON
    near = (jnp.abs(key // LON - query // LON - 1) <= 1) & (jnp.minimum(gap, LON - gap) <= 2)
    spread_slot = lax.broadcasted_iota(jnp.int32, (tall, STACK), 0)
    spread_query = (lax.broadcasted_iota(jnp.int32, (tall, STACK), 1) % ROWS) // LON
    key_slot = key // LON

    def mask(i, seg_column):
        first = i * (ROWS // LON)
        query_seg = jnp.sum(
            jnp.where(spread_slot == spread_query + (first + 1), seg_column, 0.0), axis=0, keepdims=True)
        key_seg = jnp.zeros((KEYS, STACK), wide)
        for r in range(KEYS // LON):
            row_seg = jnp.sum(jnp.where(slot == first + r, seg_column, 0.0), axis=0, keepdims=True)
            key_seg = jnp.where(key_slot == r, row_seg, key_seg)
        return jnp.where(near & (key_seg == query_seg), 0.0, NEGATIVE)

    def attend(i, seg_column):
        span = aligned(i, ROWS)
        keys = pl.ds(i * ROWS if isinstance(i, int) else pl.multiple_of(i * ROWS, ROWS), KEYS)
        bias = mask(i, seg_column)
        for g in range(groups):
            lanes = pl.ds(g * GROUP, GROUP)
            scores = nt(kv[0, keys, lanes], stack_heads(q[span, lanes])) * scale + bias
            raised = jnp.exp(scores - jnp.max(scores, axis=0, keepdims=True))
            weights = raised * (1.0 / column_sum(raised))
            prob[i * groups + g] = weights
            mixed = tn(weights.astype(low), kv[1, keys, lanes])
            att[span, lanes] = pick_heads(mixed).astype(low)

    @pl.loop(0, (blocks - 2) // 2)
    def _(i):
        attend(2 * i + 1, inner_seg)
        attend(2 * i + 2, inner_seg)

    for made in halo:
        made.wait()
    before = jnp.where(link.row > 0, seg_box[0, :, rows_here - 1 : rows_here], -1)
    after = jnp.where(link.row < row_count - 1, seg_box[1, :, 0:1], -1)
    outer_seg = jnp.where(slot == 0, before.astype(wide), inner_seg)
    outer_seg = jnp.where(slot == rows_here + 1, after.astype(wide), outer_seg)
    attend(0, outer_seg)
    attend(blocks - 1, outer_seg)

    loads[2].wait()
    for i in range(2):
        columns = pl.ds(i * STACK, STACK)
        hid[:, columns] = tok[:, columns].astype(wide) + nn(att[...], wo[:, columns]) + bias_o[:, columns]

    @pl.loop(0, blocks)
    def _(i):
        span = aligned(i, ROWS)
        norm(hid[span, :], gain2, shift2, hat2, inv2, a2, span)

    for made in loads[3:]:
        made.wait()

    parts = []
    for i, kind in enumerate(KINDS):
        order = ORDERS[kind]
        scratch = take(len(order) + 1)
        parts.append(Part(link, grads.at[i], sums.at[i], sums_hbm.at[i], order, scratch[:-1], scratch[-1],
                          store_sems.at[i]))
    scratch = take(len(VECTOR_ORDER) + 1)
    vectors = Vectors(link, vec, scratch[:-1], scratch[-1])
    flows = parts + [vectors]
    stores = [pltpu.make_async_copy(a, b, store_sems.at[len(parts) + i])
              for i, (a, b) in enumerate(((out_ref, out_hbm), (dx_ref, dx_hbm)))]

    def turn(at):
        for i in PLAN[at]:
            if i < FINISH:
                flows[i].start()
            else:
                flows[i - FINISH].finish()

    vec[0] = jnp.zeros(vec.shape[1:], wide)
    outacc[...] = jnp.zeros(outacc.shape, wide)
    da[...] = jnp.zeros(da.shape, wide)

    def feed(j):
        columns = aligned(j, STACK)
        w1_part, w2_part = w1[:, columns], w2[columns, :]
        pre[...] = nn(a2[...], w1_part) + bias_1[:, columns]
        dact[...] = nt(cot[...], w2_part)

        def gelu(i, total):
            span = aligned(i, 32)
            x = pre[span, :]
            cdf = 0.5 + 0.5 * lax.erf(x * SQRT_HALF)
            act[span, :] = (x * cdf).astype(low)
            slope = cdf + x * (jnp.exp(x * x * (-0.5)) * DENSITY)
            made = (dact[span, :] * slope).astype(low)
            dpre[span, :] = made
            return total + jnp.sum(made.astype(wide).reshape(4, 8, STACK), axis=0)

        total = lax.fori_loop(0, tokens // 32, gelu, jnp.zeros((8, STACK), wide))
        return total, columns

    def feed_products(j, columns):
        w1_part, w2_part = w1[:, columns], w2[columns, :]
        outacc[...] += nn(act[...], w2_part)
        da[...] += nt(dpre[...], w1_part)
        spot = pl.ds((j % 2) * STACK, STACK)
        grads[j // 2 * 2, spot, :] = tn(act[...], cot[...]).astype(low)
        grads[j // 2 * 2 + 1, :, spot] = tn(a2[...], dpre[...]).astype(low)

    per_row = width // STACK
    for j in range(ff // STACK):
        total, columns = feed(j)
        feed_products(j, columns)
        vec[0, 5 + j // per_row : 6 + j // per_row, pl.ds((j % per_row) * STACK, STACK)] = column_sum(total)
        turn(j)

    def norm_back(incoming, hat_ref, inv_ref, gain, span):
        hat = hat_ref[span, :]
        scaled = incoming * gain[...]
        bracket = scaled - row_mean(scaled) - hat * row_mean(scaled * hat)
        return inv_ref[span, :] * bracket, hat

    def fold(values):
        return jnp.sum(values.reshape(values.shape[0] // 8, 8, values.shape[1]), axis=0)

    def second_back(i, totals):
        span = aligned(i, ROWS)
        incoming = da[span, :]
        part, hat = norm_back(incoming, hat2, inv2, gain2, span)
        up = cot[span, :].astype(wide)
        state = up + part
        dhid[span, :] = state
        rounded = state.astype(low)
        db[span, :] = rounded
        out_ref[span, :] = (hid[span, :] + outacc[span, :] + bias_2[...]).astype(low)
        added = (rounded.astype(wide), incoming * hat, incoming, up)
        return tuple(t + fold(a) for t, a in zip(totals, added))

    zero = jnp.zeros((8, width), wide)
    totals = lax.fori_loop(0, blocks, second_back, (zero,) * 4)
    for at, total in zip((2, 3, 4, 9), totals):
        vec[0, at : at + 1, :] = column_sum(total)

    stores[0].start()
    turn(8)
    dout[...] = nt(db[...], wo[...]).astype(low)
    made = tn(att[...], db[...]).astype(low)
    for g in range(groups):
        grads[8 + g, :, 3 * GROUP :] = made[:, g * GROUP : (g + 1) * GROUP]
    turn(9)

    dkv[...] = jnp.zeros(dkv.shape, wide)

    def attention_back(g):
        lanes = pl.ds(g * GROUP, GROUP)

        def one(i):
            span = aligned(i, ROWS)
            keys = pl.ds(i * ROWS if isinstance(i, int) else pl.multiple_of(i * ROWS, ROWS), KEYS)
            stacked_out = stack_heads(dout[span, lanes])
            stacked_query = stack_heads(q[span, lanes])
            weights = prob[i * groups + g]
            slopes = nt(kv[1, keys, lanes], stacked_out)
            centre = column_sum(weights * slopes)
            ds = (weights * (slopes - centre)).astype(low)
            dkv[0, keys, lanes] += nn(ds, stacked_query) * scale
            dkv[1, keys, lanes] += nn(weights.astype(low), stacked_out)
            dqkv[span, lanes] = (pick_heads(tn(ds, kv[0, keys, lanes])) * scale).astype(low)

        def first_turn(i):
            for at in range(0, blocks, UNROLL):
                if UNROLL == blocks:
                    turn(10 + 8 * g)
                elif PLAN[10 + 8 * g + at]:

                    @pl.when(i == at // UNROLL)
                    def _():
                        turn(10 + 8 * g + at)

        if UNROLL == blocks:
            for i in range(blocks):
                one(i)
                turn(10 + 8 * g + i)
        else:

            @pl.loop(0, blocks // UNROLL)
            def _(i):
                for k in range(UNROLL):
                    one(i * UNROLL + k)
                first_turn(i)

    def rim_copies(g):
        return [remote(rim_send.at[g, side], rim_box.at[g, side], rim_sems, 4 + 2 * g + side, device)
                for side, device in ((0, left), (1, right))]

    def rim_start(g):
        lanes = pl.ds(g * GROUP, GROUP)
        rim_send[g, 0] = dkv[:, 0:LON, lanes].astype(low)
        rim_send[g, 1] = dkv[:, edge : edge + LON, lanes].astype(low)
        for copy in rim_copies(g):
            copy.start()

    def rim_finish(g):
        for copy in rim_copies(g):
            copy.wait()
        lanes = pl.ds(g * GROUP, GROUP)
        dkv[:, tokens : tokens + LON, lanes] += rim_box[g, 0].astype(wide)
        dkv[:, LON : 2 * LON, lanes] += rim_box[g, 1].astype(wide)

    def triple_products(g):
        for which in range(2):
            columns = pl.ds((which + 1) * width + g * GROUP, GROUP)
            dqkv[:, columns] = dkv[which, LON : LON + tokens, pl.ds(g * GROUP, GROUP)].astype(low)
        joined = jnp.concatenate(
            [dqkv[:, pl.ds(which * width + g * GROUP, GROUP)] for which in range(3)], axis=1)
        grads[8 + g, :, : 3 * GROUP] = tn(a1[...], joined).astype(low)
        turn(42 + g)

    for g in range(groups):
        attention_back(g)
        if g:
            rim_finish(g - 1)
        rim_start(g)
        if g:
            triple_products(g - 1)
    rim_finish(groups - 1)
    triple_products(groups - 1)

    da[...] = nt(dqkv[...], wqkv[...])
    turn(46)

    def first_back(i, totals):
        span = aligned(i, ROWS)
        incoming = da[span, :]
        part, hat = norm_back(incoming, hat1, inv1, gain1, span)
        dx_ref[span, :] = (dhid[span, :] + part).astype(low)
        return totals[0] + fold(incoming * hat), totals[1] + fold(incoming)

    totals = lax.fori_loop(0, blocks, first_back, (zero,) * 2)
    for at, total in zip((0, 1), totals):
        vec[0, at : at + 1, :] = column_sum(total)
    stores[1].start()
    turn(47)
    turn(48)
    vec_out[...] = vec[len(VECTOR_ORDER)]
    for store in stores:
        store.wait()
    for part in parts:
        part.flush().wait()


def run_layer(arrays, dp_count, row_count):
    (tokens, cotangent, wqkv, wo, w1, w2, seg, *vectors) = arrays
    count, width = tokens.shape
    ff = w1.shape[1]
    sizes = link_sizes(dp_count, row_count)
    low, wide = jnp.bfloat16, jnp.float32
    keys = count + 2 * LON
    blocks = count // ROWS
    vm = pltpu.VMEM
    square = (count, width)
    vec_shape = (16, width)
    scratch = [vm(square, low), vm(square, low), vm(wqkv.shape, low), vm(wo.shape, low), vm(w1.shape, low),
               vm(w2.shape, low), pltpu.SemaphoreType.DMA((14,))]
    scratch += [vm(v.shape, v.dtype) for v in (seg, *vectors)]
    scratch += [vm(square, low), vm(square, wide), vm((count, 1), wide), vm(square, low), vm((2, keys, width), low),
                vm((blocks * width // GROUP, KEYS, STACK), wide), vm(square, low), vm(square, wide),
                vm(square, wide), vm((count, 1), wide), vm(square, low)]
    scratch += [vm((count, STACK), wide), vm((count, STACK), wide), vm((count, STACK), low), vm((count, STACK), low),
                vm(square, wide), vm(square, wide), vm(square, wide), vm(square, low), vm(square, low),
                vm((2, keys, width), wide), vm((count, 3 * width), low)]
    count_parts = len(KINDS)
    slabs = (count_parts, width, width)
    scratch += [vm(slabs, low), vm(slabs, low), vm(square, low), vm(square, low), vm((5,) + vec_shape, wide),
                vm((STACK, GROUP), low)]
    rims = (width // GROUP, 2, 2, LON, GROUP)
    scratch += [vm((2,) + seg.shape, jnp.int32), vm(rims, low), vm(rims, low),
                pltpu.SemaphoreType.DMA((2, 12)), pltpu.SemaphoreType.DMA((count_parts + 2,))]
    for kind in KINDS:
        scratch += part_scratch((width, width), ORDERS[kind], sizes)
    scratch += vector_scratch(vec_shape, sizes)
    shapes = [(square, low), (square, low), (slabs, low), (vec_shape, wide)]
    vmem = pl.BlockSpec(memory_space=pltpu.VMEM)
    anywhere = pl.BlockSpec(memory_space=pl.ANY)
    return pl.pallas_call(
        partial(layer_kernel, sizes, row_count, width, ff),
        out_shape=[jax.ShapeDtypeStruct(s, t) for s, t in shapes],
        in_specs=[anywhere] * 14,
        out_specs=[anywhere] * 3 + [vmem],
        scratch_shapes=scratch,
        compiler_params=pltpu.CompilerParams(collective_id=1, has_side_effects=True, vmem_limit_bytes=60 << 20),
        name="layer",
    )(*arrays)


def widen_kernel(factor, width, out_in, dx_in, sums_hbm, vec_ref, out_hbm, dx_hbm, triple_hbm, output_hbm,
                 expand_hbm, reduce_hbm, *refs):
    vector_outs, (slabs, triple, output, expand, reduce, passing, in_sems, out_sems) = refs[:7], refs[7:]
    wide = jnp.float32
    count = slabs.shape[0]
    sources = [pltpu.make_async_copy(sums_hbm.at[i], slabs.at[i], in_sems.at[i]) for i in range(count)]
    order = list(range(8, count)) + list(range(8))
    for i in order[:4]:
        sources[i].start()
    passed = [pltpu.make_async_copy(source, passing.at[i], in_sems.at[count + i])
              for i, source in enumerate((out_in, dx_in))]
    for made in passed:
        made.start()
    for i in order[4:]:
        sources[i].start()
    moves = []

    def send(source, target):
        moves.append(pltpu.make_async_copy(source, target, out_sems.at[len(moves)]))
        moves[-1].start()

    def convert(i, store):
        sources[i].wait()

        @pl.loop(0, width // 32)
        def _(at):
            span = pl.ds(pl.multiple_of(at * 32, 32), 32)
            store(span, slabs[i, span, :].astype(wide) * factor)

    for g in range(count - 8):

        def store(span, made):
            for which in range(3):
                triple[span, pl.ds(which * width + g * GROUP, GROUP)] = made[:, which * GROUP : (which + 1) * GROUP]
            output[span, pl.ds(g * GROUP, GROUP)] = made[:, 3 * GROUP :]

        convert(8 + g, store)
    send(triple, triple_hbm)
    send(output, output_hbm)
    for i, target in enumerate((out_hbm, dx_hbm)):
        passed[i].wait()
        send(passing.at[i], target)
    for i in range(4):

        def store_reduce(span, made):
            reduce[i, span, :] = made

        def store_expand(span, made):
            expand[i, span, :] = made

        convert(2 * i, store_reduce)
        send(reduce.at[i], reduce_hbm.at[i])
        convert(2 * i + 1, store_expand)
        send(expand.at[i], expand_hbm.at[:, pl.ds(i * width, width)])
    values = vec_ref[...] * factor
    for at, ref in zip((0, 1, 2, 3, 4, 9), vector_outs[:5] + vector_outs[6:]):
        ref[...] = values[at : at + 1]
    for i in range(vector_outs[5].shape[1] // width):
        vector_outs[5][:, i * width : (i + 1) * width] = values[5 + i : 6 + i]
    for move in moves:
        move.wait()


def widen(layer_out, input_grad, sums, vec, factor):
    count, width, _ = sums.shape
    ff = 4 * width
    square = layer_out.shape
    big = [(width, 3 * width), (width, width), (width, ff), (4, width, width)]
    small = [(1, width)] * 5 + [(1, ff), (1, width)]
    wide = jnp.float32
    vm = pltpu.VMEM
    anywhere = pl.BlockSpec(memory_space=pl.ANY)
    vmem = pl.BlockSpec(memory_space=pltpu.VMEM)
    made = pl.pallas_call(
        partial(widen_kernel, factor, width),
        out_shape=[jax.ShapeDtypeStruct(square, layer_out.dtype)] * 2
        + [jax.ShapeDtypeStruct(s, wide) for s in big + small],
        in_specs=[anywhere] * 3 + [vmem],
        out_specs=[anywhere] * 6 + [vmem] * 7,
        scratch_shapes=[vm(sums.shape, sums.dtype), vm(big[0], wide), vm(big[1], wide), vm(big[3], wide),
                        vm(big[3], wide), vm((2,) + square, layer_out.dtype), pltpu.SemaphoreType.DMA((count + 2,)),
                        pltpu.SemaphoreType.DMA((12,))],
        compiler_params=pltpu.CompilerParams(vmem_limit_bytes=60 << 20),
        name="widen",
    )(layer_out, input_grad, sums, vec)
    return (*made[:5], made[5].reshape(ff, width), *made[6:])


def body(
    tokens,
    segment_ids,
    first_gain,
    first_shift,
    triple_weight,
    output_weight,
    output_bias,
    second_gain,
    second_shift,
    expand_weight,
    expand_bias,
    reduce_weight,
    reduce_bias,
    cotangent,
):
    dp_count, row_count = lax.axis_size("dp"), lax.axis_size("rows")
    flat = [
        v.reshape(1, -1)
        for v in (segment_ids, first_gain, first_shift, output_bias, second_gain, second_shift, expand_bias, reduce_bias)
    ]
    made = run_layer(
        (tokens, cotangent, triple_weight, output_weight, expand_weight, reduce_weight, *flat), dp_count, row_count)
    factor = (tokens.shape[0] * dp_count * row_count) ** (-0.5)
    layer_out, input_grad, triple, output, expand, reduce, *small = widen(*made, factor)
    small = [v.reshape(-1) for v in small]
    return (
        layer_out, input_grad, small[0], small[1], triple, output, small[2], small[3], small[4],
        expand, small[5], reduce, small[6],
    )


def solution(mesh):
    placed = (
        P(("dp", "rows"), None),
        P(("dp", "rows")),
        P(),
        P(),
        P(),
        P(),
        P(),
        P(),
        P(),
        P(),
        P(),
        P(),
        P(),
        P(("dp", "rows"), None),
    )
    return jax.shard_map(
        body,
        mesh=mesh,
        in_specs=placed,
        out_specs=(
            P(("dp", "rows"), None),
            P(("dp", "rows"), None),
            P(),
            P(),
            P(),
            P(),
            P(),
            P(),
            P(),
            P(),
            P(),
            P(),
            P(),
        ),
        check_vma=False,
    )
```

```python
from functools import partial

import jax
import jax.numpy as jnp
from jax import lax
from jax.experimental import pallas as pl
from jax.experimental.pallas import tpu as pltpu
from jax.sharding import PartitionSpec as P

HEAD_DIM = 32
LON = 16
EPSILON = 1e-06
NEGATIVE = -1e30

MESH_ID = pl.DeviceIdType.MESH


def span_of(start, size, unit):
    if isinstance(start, int):
        return pl.ds(start, size)
    return pl.ds(pl.multiple_of(start, unit), size)


class Link:
    def __init__(self, dp_count, row_count):
        self.dp, self.row = lax.axis_index("dp"), lax.axis_index("rows")
        self.sizes = link_sizes(dp_count, row_count)
        z = self.row // 4
        self.place = {
            "core": self.row % 2, "x": self.dp, "y": (self.row // 2) % 2, "z": z, "zl": z % 2, "zh": z // 2,
            "yz": self.row // 2, "xz": z * dp_count + self.dp}
        self.row_count = row_count

    def peer(self, dim, step):
        n, here = self.sizes[dim], self.place[dim]
        there = lax.rem(here + step, n)
        if dim == "x":
            return (there, self.row)
        if dim == "xz":
            wide = self.sizes["x"]
            return (lax.rem(there, wide), self.row + (there // wide - here // wide) * 4)
        if dim == "yz":
            return (self.dp, self.row + (there - here) * 2)
        stride = {"core": 1, "y": 2, "z": 4, "zl": 4, "zh": 8}[dim]
        return (self.dp, self.row + (there - here) * stride)

    def beside(self, step):
        return (self.dp, lax.rem(self.row + step + self.row_count, self.row_count))

    def peers(self):
        found = [self.peer(d, s) for d in ("core", "x", "yz", "xz") for s in range(1, self.sizes[d])]
        return found + [self.beside(1), self.beside(-1)]

    def signal(self):
        barrier = pltpu.get_barrier_semaphore()
        for device in self.peers():
            pl.semaphore_signal(barrier, inc=1, device_id=device, device_id_type=MESH_ID)

    def await_all(self):
        pl.semaphore_wait(pltpu.get_barrier_semaphore(), len(self.peers()))


def link_sizes(dp_count, row_count):
    deep = row_count // 4
    return {"core": 2, "x": dp_count, "y": 2, "z": deep, "zl": 2, "zh": deep // 2,
            "yz": 2 * deep, "xz": dp_count * deep}


def remote(source, target, sems, i, device):
    return pltpu.make_async_remote_copy(
        src_ref=source, dst_ref=target, send_sem=sems.at[0, i], recv_sem=sems.at[1, i],
        device_id=device, device_id_type=MESH_ID)


def piece_grid(dim, n, columns):
    if "z" not in dim or dim == "zl":
        return n, 1
    across = min(n, columns // 128)
    return n // across, across


def phase_shapes(shape, order, sizes):
    shapes, (rows, columns) = [], shape
    for dim in order:
        down, across = piece_grid(dim, sizes[dim], columns)
        rows, columns = rows // down, columns // across
        shapes.append((sizes[dim] - 1, rows, columns))
    return shapes


class Part:
    def __init__(self, link, source, result, final, order, boxes, sems, final_sem):
        self.link, self.source, self.result, self.order = link, source, result, order
        self.final, self.boxes, self.sems, self.final_sem = final, boxes, sems, final_sem
        self.step = 0
        top, left = 0, 0
        rows, columns = source.shape
        self.cuts, self.regions, self.first_sem = [], [], []
        used = 0
        for dim in order:
            n, here = link.sizes[dim], link.place[dim]
            down, across = piece_grid(dim, n, columns)
            rows, columns = rows // down, columns // across
            places = []
            for step in range(n):
                which = lax.rem(here + step, n)
                if across == 1:
                    places.append((which * rows, rows, 0, columns))
                else:
                    places.append(((which // across) * rows, rows, lax.rem(which, across) * columns, columns))
            self.cuts.append(places)
            top, left = top + places[0][0], left + places[0][2]
            self.regions.append((top, rows, left, columns))
            self.first_sem.append(used)
            used += n - 1
        self.spread_sem = used

    @property
    def last(self):
        return 2 * len(self.order)

    def view(self, ref, place):
        top, height, left, width = place
        rows = span_of(top, height, 16)
        if width == ref.shape[1]:
            return ref.at[rows, :]
        return ref.at[rows, span_of(left, width, 128)]

    def input_of(self, phase):
        return self.source if phase == 0 else self.boxes[phase - 1].at[0]

    def scatter(self, phase):
        dim = self.order[phase]
        return [
            remote(self.view(self.input_of(phase), self.cuts[phase][step]), self.boxes[phase].at[step - 1],
                   self.sems, self.first_sem[phase] + step - 1, self.link.peer(dim, step))
            for step in range(1, self.link.sizes[dim])
        ]

    def spread(self, phase):
        dim = self.order[phase]
        where = self.view(self.result, self.regions[phase])
        return [
            remote(where, where, self.sems, self.spread_sem + self.first_sem[phase] + step - 1,
                   self.link.peer(dim, step))
            for step in range(1, self.link.sizes[dim])
        ]

    def flush(self):
        return pltpu.make_async_copy(self.result, self.final, self.final_sem)

    def gain(self, phase):
        box = self.boxes[phase]
        _, height, _, _ = self.cuts[phase][0]
        mine = self.view(self.input_of(phase), self.cuts[phase][0])
        if phase == len(self.order) - 1:
            target = self.view(self.result, self.regions[phase])
        else:
            target = box.at[0]
        rows = min(height, 32)

        @pl.loop(0, height // rows)
        def _(i):
            span = pl.ds(pl.multiple_of(i * rows, rows), rows)
            if box.shape[0] == 1:
                target[span, :] = mine[span, :] + box[0, span, :]
            else:
                total = mine[span, :].astype(jnp.float32)
                for slot in range(box.shape[0]):
                    total += box[slot, span, :].astype(jnp.float32)
                target[span, :] = total.astype(jnp.bfloat16)

    def moves(self, step):
        depth = len(self.order)
        return self.scatter(step) if step < depth else self.spread(2 * depth - 1 - step)

    def start(self):
        if self.step < 2 * len(self.order):
            for move in self.moves(self.step):
                move.start()
        else:
            self.flush().start()
        self.step += 1

    def settle(self):
        for step in range(2 * len(self.order)):
            for move in self.moves(step):
                move.wait_send()
        self.flush().wait()

    def finish(self):
        for move in self.moves(self.step - 1):
            move.wait_recv()
        if self.step <= len(self.order):
            self.gain(self.step - 1)


def part_scratch(shape, order, sizes):
    copies = 2 * sum(sizes[d] - 1 for d in order)
    boxes = [pltpu.VMEM(s, jnp.bfloat16) for s in phase_shapes(shape, order, sizes)]
    return boxes + [pltpu.SemaphoreType.DMA((2, copies))]


VECTOR_ORDER = ("core", "x", "y", "z")


def vector_scratch(shape, sizes):
    boxes = [pltpu.VMEM((sizes[d] - 1,) + shape, jnp.float32) for d in VECTOR_ORDER]
    copies = sum(sizes[d] - 1 for d in VECTOR_ORDER)
    return boxes + [pltpu.SemaphoreType.DMA((2, copies))]


class Vectors:
    def __init__(self, link, work, boxes, sems):
        self.link, self.work, self.boxes, self.sems = link, work, boxes, sems
        self.step = 0
        self.last = len(VECTOR_ORDER)

    def moves(self, phase):
        dim = VECTOR_ORDER[phase]
        first = sum(self.link.sizes[d] - 1 for d in VECTOR_ORDER[:phase])
        return [
            remote(self.work.at[phase], self.boxes[phase].at[step - 1], self.sems, first + step - 1,
                   self.link.peer(dim, step))
            for step in range(1, self.link.sizes[dim])
        ]

    def start(self):
        for move in self.moves(self.step):
            move.start()
        self.step += 1

    def finish(self):
        for move in self.moves(self.step - 1):
            move.wait()
        total = self.work[self.step - 1]
        for slot in range(self.boxes[self.step - 1].shape[0]):
            total = total + self.boxes[self.step - 1][slot]
        self.work[self.step] = total


def nn(left, right):
    return lax.dot_general(left, right, (((1,), (0,)), ((), ())), preferred_element_type=jnp.float32)


def nt(left, right):
    return lax.dot_general(left, right, (((1,), (1,)), ((), ())), preferred_element_type=jnp.float32)


def tn(left, right):
    return lax.dot_general(left, right, (((0,), (0,)), ((), ())), preferred_element_type=jnp.float32)


def aligned(index, size):
    if isinstance(index, int):
        return pl.ds(index * size, size)
    return pl.ds(pl.multiple_of(index * size, size), size)


def column_sum(values):
    return jnp.sum(values, axis=0, keepdims=True)


def row_mean(values):
    return jnp.mean(values, axis=-1, keepdims=True)


ROWS = 64
KEYS = 96
GROUP = 128
STACK = 256
SQRT_HALF = 0.5 ** 0.5
DENSITY = (2.0 * 3.141592653589793) ** (-0.5)


ORDERS = (
    ("core", "x", "y", "z"),
    ("core", "y", "x", "z"),
    ("core", "zl", "x", "y", "zh"),
    ("core", "zl", "y", "x", "zh"),
    ("core", "x", "yz"),
    ("core", "y", "xz"),
)
FINISH = 100
KINDS = (2, 3, 0, 1, 2, 3, 0, 1, 0, 1, 0, 1)
PLAN = (
    (),
    (),
    (),
    (),
    (),
    (0, 1),
    (),
    (),
    (),
    (),
    (),
    (3, 2),
    (),
    (100, 0, 101),
    (),
    (),
    (),
    (5, 4),
    (103, 3, 102, 2),
    (),
    (),
    (),
    (1,),
    (7, 6),
    (105, 104),
    (),
    (),
    (100, 0),
    (5, 107, 7, 106),
    (6, 103, 102, 2),
    (),
    (101,),
    (),
    (4,),
    (100,),
    (),
    (),
    (3,),
    (0, 1),
    (),
    (105,),
    (),
    (5,),
    (),
    (106,),
    (102, 2, 107, 7, 6),
    (),
    (8, 103, 3, 104, 100, 4),
    (),
    (),
    (0,),
    (101,),
    (1, 108),
    (102, 2),
    (8, 105, 107),
    (106,),
    (9, 7, 103, 100, 104, 4),
    (),
    (),
    (0, 101),
    (5, 3),
    (102, 2, 109, 9),
    (),
    (1,),
    (),
    (10, 6, 104, 107, 108, 100),
    (0, 11, 4, 105, 103, 3, 101, 8, 110, 5),
    (7, 102, 106, 10),
    (1, 12, 111, 11, 109, 104, 4, 105, 100),
    (103, 3, 108, 5, 112, 0, 107, 8, 101, 6, 9, 104, 110, 105, 5, 108, 8, 100, 7, 10, 106, 0, 109, 1, 4, 105, 12, 111, 108, 11, 5, 8, 107, 103, 3, 9, 101, 2, 104, 112, 103, 3, 110, 10, 100, 0, 7, 1, 111, 11, 109, 100, 0, 4, 9, 105, 108, 110, 10, 8, 6, 102, 2, 111, 11, 109, 104, 102, 2, 101, 5, 12, 9, 110, 10, 111, 11, 107, 7, 108, 8, 106, 4, 6, 112, 107, 7, 109, 9, 108, 8, 110, 105, 5, 111, 11, 1, 105, 5, 10, 104, 4, 106, 6, 12, 104, 4, 106, 6, 109, 9, 101, 1, 110, 10, 111, 11, 109, 9, 101, 1, 112, 110, 10, 111, 11),
)


def layer_kernel(sizes, row_count, width, ff, *refs):
    refs = list(refs)

    def take(n):
        taken = refs[:n]
        del refs[:n]
        return taken

    (tok_hbm, cot_hbm, wqkv_hbm, wo_hbm, w1_hbm, w2_hbm) = take(6)
    small_hbm = take(8)
    (out_hbm, dx_hbm, sums_hbm, vec_out) = take(4)
    (tok, cot, wqkv, wo, w1, w2, load_sems) = take(7)
    small = take(8)
    (seg_ref, gain1, shift1, bias_o, gain2, shift2, bias_1, bias_2) = small
    (a1, hat1, inv1, q, kv, prob, att, hid, hat2, inv2, a2) = take(11)
    (pre, dact, act, dpre, outacc, da, dhid, db, dout, dkv, dqkv) = take(11)
    (grads, sums, out_ref, dx_ref, vec, head_mask) = take(6)
    (seg_box, rim_send, rim_box, rim_sems, store_sems) = take(5)
    low = jnp.bfloat16
    wide = jnp.float32
    tokens = tok.shape[0]
    rows_here = seg_ref.shape[1]
    blocks = tokens // ROWS
    groups = width // GROUP
    scale = HEAD_DIM ** (-0.5)

    link = Link(sizes["x"], row_count)
    link.signal()
    loads = [
        pltpu.make_async_copy(source, target, load_sems.at[i])
        for i, (source, target) in enumerate(
            ((tok_hbm, tok), (wqkv_hbm, wqkv), (wo_hbm, wo), (cot_hbm, cot), (w1_hbm, w1), (w2_hbm, w2)))
    ]
    small_loads = [
        pltpu.make_async_copy(source, target, load_sems.at[6 + i])
        for i, (source, target) in enumerate(zip(small_hbm, small))
    ]
    loads[0].start()
    for made in small_loads:
        made.start()
    loads[1].start()

    lane = lax.broadcasted_iota(jnp.int32, (ROWS, GROUP), 1) // HEAD_DIM
    for h in range(4):
        head_mask[pl.ds(h * ROWS, ROWS), :] = jnp.where(lane == h, 1.0, 0.0).astype(low)

    def stack_heads(block):
        return jnp.concatenate([block] * 4, axis=0) * head_mask[...]

    def pick_heads(stacked):
        picked = stacked[3 * ROWS :]
        for h in (2, 1, 0):
            picked = jnp.where(lane == h, stacked[h * ROWS : (h + 1) * ROWS], picked)
        return picked

    loads[0].wait()
    for made in small_loads:
        made.wait()

    def norm(values, gain, shift, hat_ref, inv_ref, out, span):
        centred = values - row_mean(values)
        inv = lax.rsqrt(row_mean(centred * centred) + EPSILON)
        hat = centred * inv
        hat_ref[span, :] = hat
        inv_ref[span, :] = inv
        out[span, :] = (hat * gain[...] + shift[...]).astype(low)

    @pl.loop(0, blocks)
    def _(i):
        span = aligned(i, ROWS)
        norm(tok[span, :].astype(wide), gain1, shift1, hat1, inv1, a1, span)

    loads[1].wait()
    for made in loads[2:]:
        made.start()
    for which in range(2):

        @pl.loop(0, 2)
        def _(i):
            columns = aligned(i, STACK)
            source = pl.ds(pl.multiple_of((which + 1) * width + i * STACK, STACK), STACK)
            kv[which, LON : LON + tokens, columns] = nn(a1[...], wqkv[:, source]).astype(low)

    link.await_all()
    edge = LON + tokens
    left, right = link.beside(-1), link.beside(1)
    halo = [
        remote(source, target, rim_sems, i, device)
        for i, (source, target, device) in enumerate(
            (
                (kv.at[:, pl.ds(LON, LON), :], kv.at[:, pl.ds(edge, LON), :], left),
                (kv.at[:, pl.ds(tokens, LON), :], kv.at[:, pl.ds(0, LON), :], right),
                (seg_ref, seg_box.at[1], left),
                (seg_ref, seg_box.at[0], right),
            )
        )
    ]
    for made in halo:
        made.start()

    @pl.loop(0, 2)
    def _(i):
        columns = aligned(i, STACK)
        q[:, columns] = nn(a1[...], wqkv[:, columns]).astype(low)

    tall = rows_here + 8
    slot = lax.broadcasted_iota(jnp.int32, (tall, rows_here), 0)
    place = lax.broadcasted_iota(jnp.int32, (tall, rows_here), 1)
    own = jnp.broadcast_to(seg_ref[...].astype(wide), (tall, rows_here))
    inner_seg = jnp.sum(jnp.where(slot == place + 1, own, 0.0), axis=1, keepdims=True)
    slot = lax.broadcasted_iota(jnp.int32, (tall, 1), 0)
    key = lax.broadcasted_iota(jnp.int32, (KEYS, STACK), 0)
    query = lax.broadcasted_iota(jnp.int32, (KEYS, STACK), 1) % ROWS
    gap = (query - key + 2 * LON) % LON
    near = (jnp.abs(key // LON - query // LON - 1) <= 1) & (jnp.minimum(gap, LON - gap) <= 2)
    spread_slot = lax.broadcasted_iota(jnp.int32, (tall, STACK), 0)
    spread_query = (lax.broadcasted_iota(jnp.int32, (tall, STACK), 1) % ROWS) // LON
    key_slot = key // LON

    def mask(i, seg_column):
        first = i * (ROWS // LON)
        query_seg = jnp.sum(
            jnp.where(spread_slot == spread_query + (first + 1), seg_column, 0.0), axis=0, keepdims=True)
        key_seg = jnp.zeros((KEYS, STACK), wide)
        for r in range(KEYS // LON):
            row_seg = jnp.sum(jnp.where(slot == first + r, seg_column, 0.0), axis=0, keepdims=True)
            key_seg = jnp.where(key_slot == r, row_seg, key_seg)
        return jnp.where(near & (key_seg == query_seg), 0.0, NEGATIVE)

    def attend(i, seg_column):
        span = aligned(i, ROWS)
        keys = pl.ds(i * ROWS if isinstance(i, int) else pl.multiple_of(i * ROWS, ROWS), KEYS)
        bias = mask(i, seg_column)
        for g in range(groups):
            lanes = pl.ds(g * GROUP, GROUP)
            scores = nt(kv[0, keys, lanes], stack_heads(q[span, lanes])) * scale + bias
            raised = jnp.exp(scores - jnp.max(scores, axis=0, keepdims=True))
            weights = raised * (1.0 / column_sum(raised))
            prob[i * groups + g] = weights
            mixed = tn(weights.astype(low), kv[1, keys, lanes])
            att[span, lanes] = pick_heads(mixed).astype(low)

    @pl.loop(0, (blocks - 2) // 2)
    def _(i):
        attend(2 * i + 1, inner_seg)
        attend(2 * i + 2, inner_seg)

    for made in halo:
        made.wait()
    before = jnp.where(link.row > 0, seg_box[0, :, rows_here - 1 : rows_here], -1)
    after = jnp.where(link.row < row_count - 1, seg_box[1, :, 0:1], -1)
    outer_seg = jnp.where(slot == 0, before.astype(wide), inner_seg)
    outer_seg = jnp.where(slot == rows_here + 1, after.astype(wide), outer_seg)
    attend(0, outer_seg)
    attend(blocks - 1, outer_seg)

    loads[2].wait()
    for i in range(2):
        columns = pl.ds(i * STACK, STACK)
        hid[:, columns] = tok[:, columns].astype(wide) + nn(att[...], wo[:, columns]) + bias_o[:, columns]

    @pl.loop(0, blocks)
    def _(i):
        span = aligned(i, ROWS)
        norm(hid[span, :], gain2, shift2, hat2, inv2, a2, span)

    for made in loads[3:]:
        made.wait()

    parts = []
    for i, kind in enumerate(KINDS):
        order = ORDERS[kind]
        scratch = take(len(order) + 1)
        parts.append(Part(link, grads.at[i], sums.at[i], sums_hbm.at[i], order, scratch[:-1], scratch[-1],
                          store_sems.at[i]))
    scratch = take(len(VECTOR_ORDER) + 1)
    vectors = Vectors(link, vec, scratch[:-1], scratch[-1])
    flows = parts + [vectors]
    stores = [pltpu.make_async_copy(a, b, store_sems.at[len(parts) + i])
              for i, (a, b) in enumerate(((out_ref, out_hbm), (dx_ref, dx_hbm)))]

    plan = iter(PLAN)

    def turn():
        for i in next(plan):
            if i < FINISH:
                flows[i].start()
            else:
                flows[i - FINISH].finish()

    vec[0] = jnp.zeros(vec.shape[1:], wide)
    per_row = width // STACK
    for j in range(ff // STACK):
        columns = pl.ds(j * STACK, STACK)
        spot = pl.ds((j % 2) * STACK, STACK)
        pre[...] = nn(a2[...], w1[:, columns]) + bias_1[:, columns]
        dact[...] = nt(cot[...], w2[columns, :])
        turn()

        def gelu(i, total):
            span = aligned(i, 32)
            x = pre[span, :]
            cdf = 0.5 + 0.5 * lax.erf(x * SQRT_HALF)
            act[span, columns] = (x * cdf).astype(low)
            slope = cdf + x * (jnp.exp(x * x * (-0.5)) * DENSITY)
            made = (dact[span, :] * slope).astype(low)
            dpre[span, columns] = made
            return total + jnp.sum(made.astype(wide).reshape(4, 8, STACK), axis=0)

        total = lax.fori_loop(0, tokens // 32, gelu, jnp.zeros((8, STACK), wide), unroll=True)
        vec[0, 5 + j // per_row : 6 + j // per_row, pl.ds((j % per_row) * STACK, STACK)] = column_sum(total)
        turn()
        grads[j // 2 * 2, spot, :] = tn(act[:, columns], cot[...]).astype(low)
        grads[j // 2 * 2 + 1, :, spot] = tn(a2[...], dpre[:, columns]).astype(low)
        turn()
    for i in range(2):
        columns = pl.ds(i * STACK, STACK)
        outacc[:, columns] = nn(act[...], w2[:, columns])
        turn()
    for i in range(2):
        columns = pl.ds(i * STACK, STACK)
        da[:, columns] = nt(dpre[...], w1[columns, :])
        turn()

    def norm_back(incoming, hat_ref, inv_ref, gain, span):
        hat = hat_ref[span, :]
        scaled = incoming * gain[...]
        bracket = scaled - row_mean(scaled) - hat * row_mean(scaled * hat)
        return inv_ref[span, :] * bracket, hat

    def fold(values):
        return jnp.sum(values.reshape(values.shape[0] // 8, 8, values.shape[1]), axis=0)

    def second_back(i, totals):
        span = aligned(i, ROWS)
        incoming = da[span, :]
        part, hat = norm_back(incoming, hat2, inv2, gain2, span)
        up = cot[span, :].astype(wide)
        state = up + part
        dhid[span, :] = state
        rounded = state.astype(low)
        db[span, :] = rounded
        out_ref[span, :] = (hid[span, :] + outacc[span, :] + bias_2[...]).astype(low)
        added = (rounded.astype(wide), incoming * hat, incoming, up)
        return tuple(t + fold(a) for t, a in zip(totals, added))

    zero = jnp.zeros((8, width), wide)
    totals = lax.fori_loop(0, blocks // 2, second_back, (zero,) * 4)
    turn()
    totals = lax.fori_loop(blocks // 2, blocks, second_back, totals)
    for at, total in zip((2, 3, 4, 9), totals):
        vec[0, at : at + 1, :] = column_sum(total)

    stores[0].start()
    turn()
    dout[...] = nt(db[...], wo[...]).astype(low)
    made = tn(att[...], db[...]).astype(low)
    for g in range(groups):
        grads[8 + g, :, 3 * GROUP :] = made[:, g * GROUP : (g + 1) * GROUP]
    turn()

    dkv[...] = jnp.zeros(dkv.shape, wide)

    def attention_back(g):
        lanes = pl.ds(g * GROUP, GROUP)

        def one(i):
            span = aligned(i, ROWS)
            keys = pl.ds(i * ROWS if isinstance(i, int) else pl.multiple_of(i * ROWS, ROWS), KEYS)
            stacked_out = stack_heads(dout[span, lanes])
            stacked_query = stack_heads(q[span, lanes])
            weights = prob[i * groups + g]
            slopes = nt(kv[1, keys, lanes], stacked_out)
            centre = column_sum(weights * slopes)
            ds = (weights * (slopes - centre)).astype(low)
            dkv[0, keys, lanes] += nn(ds, stacked_query) * scale
            dkv[1, keys, lanes] += nn(weights.astype(low), stacked_out)
            dqkv[span, lanes] = (pick_heads(tn(ds, kv[0, keys, lanes])) * scale).astype(low)

        for i in range(blocks):
            one(i)
            turn()

    def rim_copies(g):
        return [remote(rim_send.at[g, side], rim_box.at[g, side], rim_sems, 4 + 2 * g + side, device)
                for side, device in ((0, left), (1, right))]

    def rim_start(g):
        lanes = pl.ds(g * GROUP, GROUP)
        rim_send[g, 0] = dkv[:, 0:LON, lanes].astype(low)
        rim_send[g, 1] = dkv[:, edge : edge + LON, lanes].astype(low)
        for copy in rim_copies(g):
            copy.start()

    def rim_finish(g):
        for copy in rim_copies(g):
            copy.wait()
        lanes = pl.ds(g * GROUP, GROUP)
        dkv[:, tokens : tokens + LON, lanes] += rim_box[g, 0].astype(wide)
        dkv[:, LON : 2 * LON, lanes] += rim_box[g, 1].astype(wide)

    def triple_products(g):
        for which in range(2):
            columns = pl.ds((which + 1) * width + g * GROUP, GROUP)
            dqkv[:, columns] = dkv[which, LON : LON + tokens, pl.ds(g * GROUP, GROUP)].astype(low)
        joined = jnp.concatenate(
            [dqkv[:, pl.ds(which * width + g * GROUP, GROUP)] for which in range(3)], axis=1)
        grads[8 + g, :, : 3 * GROUP] = tn(a1[...], joined).astype(low)
        turn()

    for g in range(groups):
        attention_back(g)
        if g:
            rim_finish(g - 1)
        rim_start(g)
        if g:
            triple_products(g - 1)
    rim_finish(groups - 1)
    triple_products(groups - 1)

    da[...] = nt(dqkv[...], wqkv[...])
    turn()

    def first_back(i, totals):
        span = aligned(i, ROWS)
        incoming = da[span, :]
        part, hat = norm_back(incoming, hat1, inv1, gain1, span)
        dx_ref[span, :] = (dhid[span, :] + part).astype(low)
        return totals[0] + fold(incoming * hat), totals[1] + fold(incoming)

    totals = lax.fori_loop(0, blocks, first_back, (zero,) * 2)
    for at, total in zip((0, 1), totals):
        vec[0, at : at + 1, :] = column_sum(total)
    stores[1].start()
    turn()
    turn()
    vec_out[...] = vec[len(VECTOR_ORDER)]
    for store in stores:
        store.wait()
    for part in parts:
        part.settle()


def run_layer(arrays, dp_count, row_count):
    (tokens, cotangent, wqkv, wo, w1, w2, seg, *vectors) = arrays
    count, width = tokens.shape
    ff = w1.shape[1]
    sizes = link_sizes(dp_count, row_count)
    low, wide = jnp.bfloat16, jnp.float32
    keys = count + 2 * LON
    blocks = count // ROWS
    vm = pltpu.VMEM
    square = (count, width)
    vec_shape = (16, width)
    scratch = [vm(square, low), vm(square, low), vm(wqkv.shape, low), vm(wo.shape, low), vm(w1.shape, low),
               vm(w2.shape, low), pltpu.SemaphoreType.DMA((14,))]
    scratch += [vm(v.shape, v.dtype) for v in (seg, *vectors)]
    scratch += [vm(square, low), vm(square, wide), vm((count, 1), wide), vm(square, low), vm((2, keys, width), low),
                vm((blocks * width // GROUP, KEYS, STACK), wide), vm(square, low), vm(square, wide),
                vm(square, wide), vm((count, 1), wide), vm(square, low)]
    scratch += [vm((count, STACK), wide), vm((count, STACK), wide), vm((count, ff), low), vm((count, ff), low),
                vm(square, wide), vm(square, wide), vm(square, wide), vm(square, low), vm(square, low),
                vm((2, keys, width), wide), vm((count, 3 * width), low)]
    count_parts = len(KINDS)
    slabs = (count_parts, width, width)
    scratch += [vm(slabs, low), vm(slabs, low), vm(square, low), vm(square, low), vm((5,) + vec_shape, wide),
                vm((STACK, GROUP), low)]
    rims = (width // GROUP, 2, 2, LON, GROUP)
    scratch += [vm((2,) + seg.shape, jnp.int32), vm(rims, low), vm(rims, low),
                pltpu.SemaphoreType.DMA((2, 12)), pltpu.SemaphoreType.DMA((count_parts + 2,))]
    for kind in KINDS:
        scratch += part_scratch((width, width), ORDERS[kind], sizes)
    scratch += vector_scratch(vec_shape, sizes)
    shapes = [(square, low), (square, low), (slabs, low), (vec_shape, wide)]
    vmem = pl.BlockSpec(memory_space=pltpu.VMEM)
    anywhere = pl.BlockSpec(memory_space=pl.ANY)
    return pl.pallas_call(
        partial(layer_kernel, sizes, row_count, width, ff),
        out_shape=[jax.ShapeDtypeStruct(s, t) for s, t in shapes],
        in_specs=[anywhere] * 14,
        out_specs=[anywhere] * 3 + [vmem],
        scratch_shapes=scratch,
        compiler_params=pltpu.CompilerParams(collective_id=1, has_side_effects=True, vmem_limit_bytes=60 << 20),
        name="layer",
    )(*arrays)


def widen_kernel(factor, width, out_in, dx_in, sums_hbm, vec_ref, out_hbm, dx_hbm, triple_hbm, output_hbm,
                 expand_hbm, reduce_hbm, *refs):
    vector_outs, (slabs, triple, output, expand, reduce, passing, in_sems, out_sems) = refs[:7], refs[7:]
    wide = jnp.float32
    count = slabs.shape[0]
    sources = [pltpu.make_async_copy(sums_hbm.at[i], slabs.at[i], in_sems.at[i]) for i in range(count)]
    order = list(range(8, count)) + list(range(8))
    for i in order[:4]:
        sources[i].start()
    passed = [pltpu.make_async_copy(source, passing.at[i], in_sems.at[count + i])
              for i, source in enumerate((out_in, dx_in))]
    for made in passed:
        made.start()
    for i in order[4:]:
        sources[i].start()
    moves = []

    def send(source, target):
        moves.append(pltpu.make_async_copy(source, target, out_sems.at[len(moves)]))
        moves[-1].start()

    def convert(i, store):
        sources[i].wait()

        @pl.loop(0, width // 32)
        def _(at):
            span = pl.ds(pl.multiple_of(at * 32, 32), 32)
            store(span, slabs[i, span, :].astype(wide) * factor)

    for g in range(count - 8):

        def store(span, made):
            for which in range(3):
                triple[span, pl.ds(which * width + g * GROUP, GROUP)] = made[:, which * GROUP : (which + 1) * GROUP]
            output[span, pl.ds(g * GROUP, GROUP)] = made[:, 3 * GROUP :]

        convert(8 + g, store)
    send(triple, triple_hbm)
    send(output, output_hbm)
    for i, target in enumerate((out_hbm, dx_hbm)):
        passed[i].wait()
        send(passing.at[i], target)
    for i in range(4):

        def store_reduce(span, made):
            reduce[i, span, :] = made

        def store_expand(span, made):
            expand[i, span, :] = made

        convert(2 * i, store_reduce)
        send(reduce.at[i], reduce_hbm.at[i])
        convert(2 * i + 1, store_expand)
        send(expand.at[i], expand_hbm.at[:, pl.ds(i * width, width)])
    values = vec_ref[...] * factor
    for at, ref in zip((0, 1, 2, 3, 4, 9), vector_outs[:5] + vector_outs[6:]):
        ref[...] = values[at : at + 1]
    for i in range(vector_outs[5].shape[1] // width):
        vector_outs[5][:, i * width : (i + 1) * width] = values[5 + i : 6 + i]
    for move in moves:
        move.wait()


def widen(layer_out, input_grad, sums, vec, factor):
    count, width, _ = sums.shape
    ff = 4 * width
    square = layer_out.shape
    big = [(width, 3 * width), (width, width), (width, ff), (4, width, width)]
    small = [(1, width)] * 5 + [(1, ff), (1, width)]
    wide = jnp.float32
    vm = pltpu.VMEM
    anywhere = pl.BlockSpec(memory_space=pl.ANY)
    vmem = pl.BlockSpec(memory_space=pltpu.VMEM)
    made = pl.pallas_call(
        partial(widen_kernel, factor, width),
        out_shape=[jax.ShapeDtypeStruct(square, layer_out.dtype)] * 2
        + [jax.ShapeDtypeStruct(s, wide) for s in big + small],
        in_specs=[anywhere] * 3 + [vmem],
        out_specs=[anywhere] * 6 + [vmem] * 7,
        scratch_shapes=[vm(sums.shape, sums.dtype), vm(big[0], wide), vm(big[1], wide), vm(big[3], wide),
                        vm(big[3], wide), vm((2,) + square, layer_out.dtype), pltpu.SemaphoreType.DMA((count + 2,)),
                        pltpu.SemaphoreType.DMA((12,))],
        compiler_params=pltpu.CompilerParams(vmem_limit_bytes=60 << 20),
        name="widen",
    )(layer_out, input_grad, sums, vec)
    return (*made[:5], made[5].reshape(ff, width), *made[6:])


def body(
    tokens,
    segment_ids,
    first_gain,
    first_shift,
    triple_weight,
    output_weight,
    output_bias,
    second_gain,
    second_shift,
    expand_weight,
    expand_bias,
    reduce_weight,
    reduce_bias,
    cotangent,
):
    dp_count, row_count = lax.axis_size("dp"), lax.axis_size("rows")
    flat = [
        v.reshape(1, -1)
        for v in (segment_ids, first_gain, first_shift, output_bias, second_gain, second_shift, expand_bias, reduce_bias)
    ]
    made = run_layer(
        (tokens, cotangent, triple_weight, output_weight, expand_weight, reduce_weight, *flat), dp_count, row_count)
    factor = (tokens.shape[0] * dp_count * row_count) ** (-0.5)
    layer_out, input_grad, triple, output, expand, reduce, *small = widen(*made, factor)
    small = [v.reshape(-1) for v in small]
    return (
        layer_out, input_grad, small[0], small[1], triple, output, small[2], small[3], small[4],
        expand, small[5], reduce, small[6],
    )


def solution(mesh):
    placed = (
        P(("dp", "rows"), None),
        P(("dp", "rows")),
        P(),
        P(),
        P(),
        P(),
        P(),
        P(),
        P(),
        P(),
        P(),
        P(),
        P(),
        P(("dp", "rows"), None),
    )
    return jax.shard_map(
        body,
        mesh=mesh,
        in_specs=placed,
        out_specs=(
            P(("dp", "rows"), None),
            P(("dp", "rows"), None),
            P(),
            P(),
            P(),
            P(),
            P(),
            P(),
            P(),
            P(),
            P(),
            P(),
            P(),
        ),
        check_vma=False,
    )
```

```python
from functools import partial

import jax
import jax.numpy as jnp
from jax import lax
from jax.experimental import pallas as pl
from jax.experimental.pallas import tpu as pltpu
from jax.sharding import PartitionSpec as P

HEAD_DIM = 32
LON = 16
EPSILON = 1e-06
NEGATIVE = -1e30

MESH_ID = pl.DeviceIdType.MESH


def span_of(start, size, unit):
    if isinstance(start, int):
        return pl.ds(start, size)
    return pl.ds(pl.multiple_of(start, unit), size)


class Link:
    def __init__(self, dp_count, row_count):
        self.dp, self.row = lax.axis_index("dp"), lax.axis_index("rows")
        self.sizes = link_sizes(dp_count, row_count)
        z = self.row // 4
        self.place = {
            "core": self.row % 2, "x": self.dp, "y": (self.row // 2) % 2, "z": z, "zl": z % 2, "zh": z // 2,
            "yz": self.row // 2, "xz": z * dp_count + self.dp}
        self.row_count = row_count

    def peer(self, dim, step):
        n, here = self.sizes[dim], self.place[dim]
        there = lax.rem(here + step, n)
        if dim == "x":
            return (there, self.row)
        if dim == "xz":
            wide = self.sizes["x"]
            return (lax.rem(there, wide), self.row + (there // wide - here // wide) * 4)
        if dim == "yz":
            return (self.dp, self.row + (there - here) * 2)
        stride = {"core": 1, "y": 2, "z": 4, "zl": 4, "zh": 8}[dim]
        return (self.dp, self.row + (there - here) * stride)

    def beside(self, step):
        return (self.dp, lax.rem(self.row + step + self.row_count, self.row_count))

    def peers(self):
        found = [self.peer(d, s) for d in ("core", "x", "yz", "xz") for s in range(1, self.sizes[d])]
        return found + [self.beside(1), self.beside(-1)]

    def signal(self):
        barrier = pltpu.get_barrier_semaphore()
        for device in self.peers():
            pl.semaphore_signal(barrier, inc=1, device_id=device, device_id_type=MESH_ID)

    def await_all(self):
        pl.semaphore_wait(pltpu.get_barrier_semaphore(), len(self.peers()))


def link_sizes(dp_count, row_count):
    deep = row_count // 4
    return {"core": 2, "x": dp_count, "y": 2, "z": deep, "zl": 2, "zh": deep // 2,
            "yz": 2 * deep, "xz": dp_count * deep}


def remote(source, target, sems, i, device):
    return pltpu.make_async_remote_copy(
        src_ref=source, dst_ref=target, send_sem=sems.at[0, i], recv_sem=sems.at[1, i],
        device_id=device, device_id_type=MESH_ID)


def piece_grid(dim, n, columns):
    if "z" not in dim or dim == "zl":
        return n, 1
    across = min(n, columns // 128)
    return n // across, across


def phase_shapes(shape, order, sizes):
    shapes, (rows, columns) = [], shape
    for dim in order:
        down, across = piece_grid(dim, sizes[dim], columns)
        rows, columns = rows // down, columns // across
        shapes.append((sizes[dim] - 1, rows, columns))
    return shapes


class Part:
    def __init__(self, link, source, result, order, boxes, sems):
        self.link, self.source, self.result, self.order = link, source, result, order
        self.boxes, self.sems = boxes, sems
        self.step = 0
        top, left = 0, 0
        rows, columns = source.shape
        self.cuts, self.regions, self.first_sem = [], [], []
        used = 0
        for dim in order:
            n, here = link.sizes[dim], link.place[dim]
            down, across = piece_grid(dim, n, columns)
            rows, columns = rows // down, columns // across
            places = []
            for step in range(n):
                which = lax.rem(here + step, n)
                if across == 1:
                    places.append((which * rows, rows, 0, columns))
                else:
                    places.append(((which // across) * rows, rows, lax.rem(which, across) * columns, columns))
            self.cuts.append(places)
            top, left = top + places[0][0], left + places[0][2]
            self.regions.append((top, rows, left, columns))
            self.first_sem.append(used)
            used += n - 1
        self.spread_sem = used

    @property
    def last(self):
        return 2 * len(self.order)

    def view(self, ref, place):
        top, height, left, width = place
        rows = span_of(top, height, 16)
        if width == ref.shape[1]:
            return ref.at[rows, :]
        return ref.at[rows, span_of(left, width, 128)]

    def input_of(self, phase):
        return self.source if phase == 0 else self.boxes[phase - 1].at[0]

    def scatter(self, phase):
        dim = self.order[phase]
        return [
            remote(self.view(self.input_of(phase), self.cuts[phase][step]), self.boxes[phase].at[step - 1],
                   self.sems, self.first_sem[phase] + step - 1, self.link.peer(dim, step))
            for step in range(1, self.link.sizes[dim])
        ]

    def spread(self, phase):
        dim = self.order[phase]
        where = self.view(self.result, self.regions[phase])
        return [
            remote(where, where, self.sems, self.spread_sem + self.first_sem[phase] + step - 1,
                   self.link.peer(dim, step))
            for step in range(1, self.link.sizes[dim])
        ]

    def gain(self, phase):
        box = self.boxes[phase]
        _, height, _, _ = self.cuts[phase][0]
        mine = self.view(self.input_of(phase), self.cuts[phase][0])
        if phase == len(self.order) - 1:
            target = self.view(self.result, self.regions[phase])
        else:
            target = box.at[0]
        rows = min(height, 32)

        @pl.loop(0, height // rows)
        def _(i):
            span = pl.ds(pl.multiple_of(i * rows, rows), rows)
            if box.shape[0] == 1:
                target[span, :] = mine[span, :] + box[0, span, :]
            else:
                total = mine[span, :].astype(jnp.float32)
                for slot in range(box.shape[0]):
                    total += box[slot, span, :].astype(jnp.float32)
                target[span, :] = total.astype(jnp.bfloat16)

    def moves(self, step):
        depth = len(self.order)
        return self.scatter(step) if step < depth else self.spread(2 * depth - 1 - step)

    def start(self):
        for move in self.moves(self.step):
            move.start()
        self.step += 1

    def settle(self):
        for step in range(2 * len(self.order)):
            for move in self.moves(step):
                move.wait_send()

    def finish(self):
        for move in self.moves(self.step - 1):
            move.wait_recv()
        if self.step <= len(self.order):
            self.gain(self.step - 1)


def part_scratch(shape, order, sizes):
    copies = 2 * sum(sizes[d] - 1 for d in order)
    boxes = [pltpu.VMEM(s, jnp.bfloat16) for s in phase_shapes(shape, order, sizes)]
    return boxes + [pltpu.SemaphoreType.DMA((2, copies))]


VECTOR_ORDER = ("core", "x", "y", "z")


def vector_scratch(shape, sizes):
    boxes = [pltpu.VMEM((sizes[d] - 1,) + shape, jnp.float32) for d in VECTOR_ORDER]
    copies = sum(sizes[d] - 1 for d in VECTOR_ORDER)
    return boxes + [pltpu.SemaphoreType.DMA((2, copies))]


class Vectors:
    def __init__(self, link, work, boxes, sems):
        self.link, self.work, self.boxes, self.sems = link, work, boxes, sems
        self.step = 0
        self.last = len(VECTOR_ORDER)

    def moves(self, phase):
        dim = VECTOR_ORDER[phase]
        first = sum(self.link.sizes[d] - 1 for d in VECTOR_ORDER[:phase])
        return [
            remote(self.work.at[phase], self.boxes[phase].at[step - 1], self.sems, first + step - 1,
                   self.link.peer(dim, step))
            for step in range(1, self.link.sizes[dim])
        ]

    def start(self):
        for move in self.moves(self.step):
            move.start()
        self.step += 1

    def finish(self):
        for move in self.moves(self.step - 1):
            move.wait()
        total = self.work[self.step - 1]
        for slot in range(self.boxes[self.step - 1].shape[0]):
            total = total + self.boxes[self.step - 1][slot]
        self.work[self.step] = total


def nn(left, right):
    return lax.dot_general(left, right, (((1,), (0,)), ((), ())), preferred_element_type=jnp.float32)


def nt(left, right):
    return lax.dot_general(left, right, (((1,), (1,)), ((), ())), preferred_element_type=jnp.float32)


def tn(left, right):
    return lax.dot_general(left, right, (((0,), (0,)), ((), ())), preferred_element_type=jnp.float32)


def aligned(index, size):
    if isinstance(index, int):
        return pl.ds(index * size, size)
    return pl.ds(pl.multiple_of(index * size, size), size)


def column_sum(values):
    return jnp.sum(values, axis=0, keepdims=True)


def row_mean(values):
    return jnp.mean(values, axis=-1, keepdims=True)


ROWS = 64
KEYS = 96
GROUP = 128
STACK = 256
SQRT_HALF = 0.5 ** 0.5
DENSITY = (2.0 * 3.141592653589793) ** (-0.5)


ORDERS = (
    ("core", "x", "y", "z"),
    ("core", "y", "x", "z"),
    ("core", "zl", "x", "y", "zh"),
    ("core", "zl", "y", "x", "zh"),
    ("core", "x", "yz"),
    ("core", "y", "xz"),
)
FINISH = 100
KINDS = (2, 3, 0, 1, 3, 2, 0, 1, 0, 1, 0, 1)
PLAN = (
    (),
    (),
    (),
    (),
    (),
    (1, 0),
    (),
    (),
    (),
    (),
    (),
    (3, 2, 101, 1, 100, 0),
    (),
    (),
    (),
    (),
    (),
    (5, 4, 103, 3, 102, 2),
    (),
    (),
    (),
    (),
    (),
    (7, 6, 105, 104),
    (5, 4),
    (),
    (),
    (107, 7, 106, 6),
    (103, 101, 1, 102, 100),
    (),
    (3,),
    (),
    (),
    (),
    (),
    (),
    (),
    (),
    (0, 2, 106, 6),
    (),
    (),
    (),
    (),
    (),
    (),
    (),
    (105, 5, 104, 4, 107, 101, 103, 3),
    (8, 100, 1, 0),
    (),
    (),
    (),
    (),
    (),
    (),
    (),
    (7, 102, 2, 106, 6, 108, 105, 5, 103, 104, 101, 100),
    (9, 8),
    (),
    (),
    (),
    (),
    (),
    (),
    (),
    (1, 3, 109, 9, 4, 105, 107, 102, 106),
    (5, 7, 10),
    (11, 0, 6, 108, 8, 101, 110, 10, 104, 103),
    (1, 4, 105, 111, 11, 107, 109),
    (9, 5, 7, 12, 100, 106, 6, 108),
    (101, 104, 8, 112, 110, 1, 10, 4, 3, 105, 0, 5, 2, 111, 109, 9, 11, 107, 101, 1, 108, 8, 104, 106, 4, 100, 0, 103, 7, 3, 110, 10, 105, 102, 2, 111, 11, 5, 109, 9, 104, 101, 108, 6, 100, 1, 107, 110, 8, 10, 105, 4, 111, 0, 109, 102, 11, 7, 9, 103, 3, 106, 6, 110, 10, 5, 12, 108, 103, 100, 0, 8, 106, 104, 111, 109, 101, 1, 9, 112, 11, 12, 101, 110, 4, 2, 108, 8, 107, 7, 105, 5, 111, 11, 112, 12, 108, 107, 10, 100, 0, 105, 109, 9, 100, 102, 2, 109, 102, 104, 4, 111, 11, 112, 110, 10, 104, 111, 110),
)


def layer_kernel(sizes, row_count, width, ff, *refs):
    refs = list(refs)

    def take(n):
        taken = refs[:n]
        del refs[:n]
        return taken

    (tok_hbm, cot_hbm, wqkv_hbm, wo_hbm, w1_hbm, w2_hbm) = take(6)
    small_hbm = take(8)
    (out_ref, dx_ref, sums, vec_out) = take(4)
    (tok, cot, wqkv, wo, w1, w2, load_sems) = take(7)
    small = take(8)
    (seg_ref, gain1, shift1, bias_o, gain2, shift2, bias_1, bias_2) = small
    (a1, hat1, inv1, q, kv, prob, att, hid, hat2, inv2, a2) = take(11)
    (pre, dact, act, dpre, outacc, da, dhid, db, dout, dkv, dqkv) = take(11)
    (grads, vec, head_mask) = take(3)
    (seg_box, rim_send, rim_box, rim_sems) = take(4)
    low = jnp.bfloat16
    wide = jnp.float32
    tokens = tok.shape[0]
    rows_here = seg_ref.shape[1]
    blocks = tokens // ROWS
    groups = width // GROUP
    scale = HEAD_DIM ** (-0.5)

    link = Link(sizes["x"], row_count)
    link.signal()
    loads = [
        pltpu.make_async_copy(source, target, load_sems.at[i])
        for i, (source, target) in enumerate(
            ((tok_hbm, tok), (wqkv_hbm, wqkv), (wo_hbm, wo), (cot_hbm, cot), (w1_hbm, w1), (w2_hbm, w2)))
    ]
    small_loads = [
        pltpu.make_async_copy(source, target, load_sems.at[6 + i])
        for i, (source, target) in enumerate(zip(small_hbm, small))
    ]
    loads[0].start()
    for made in small_loads:
        made.start()
    loads[1].start()

    lane = lax.broadcasted_iota(jnp.int32, (ROWS, GROUP), 1) // HEAD_DIM
    for h in range(4):
        head_mask[pl.ds(h * ROWS, ROWS), :] = jnp.where(lane == h, 1.0, 0.0).astype(low)

    def stack_heads(block):
        return jnp.concatenate([block] * 4, axis=0) * head_mask[...]

    def pick_heads(stacked):
        picked = stacked[3 * ROWS :]
        for h in (2, 1, 0):
            picked = jnp.where(lane == h, stacked[h * ROWS : (h + 1) * ROWS], picked)
        return picked

    loads[0].wait()
    for made in small_loads:
        made.wait()

    def norm(values, gain, shift, hat_ref, inv_ref, out, span):
        centred = values - row_mean(values)
        inv = lax.rsqrt(row_mean(centred * centred) + EPSILON)
        hat = centred * inv
        hat_ref[span, :] = hat
        inv_ref[span, :] = inv
        out[span, :] = (hat * gain[...] + shift[...]).astype(low)

    @pl.loop(0, blocks)
    def _(i):
        span = aligned(i, ROWS)
        norm(tok[span, :].astype(wide), gain1, shift1, hat1, inv1, a1, span)

    loads[1].wait()
    for made in loads[2:]:
        made.start()
    for which in range(2):

        @pl.loop(0, 2)
        def _(i):
            columns = aligned(i, STACK)
            source = pl.ds(pl.multiple_of((which + 1) * width + i * STACK, STACK), STACK)
            kv[which, LON : LON + tokens, columns] = nn(a1[...], wqkv[:, source]).astype(low)

    link.await_all()
    edge = LON + tokens
    left, right = link.beside(-1), link.beside(1)
    halo = [
        remote(source, target, rim_sems, i, device)
        for i, (source, target, device) in enumerate(
            (
                (kv.at[:, pl.ds(LON, LON), :], kv.at[:, pl.ds(edge, LON), :], left),
                (kv.at[:, pl.ds(tokens, LON), :], kv.at[:, pl.ds(0, LON), :], right),
                (seg_ref, seg_box.at[1], left),
                (seg_ref, seg_box.at[0], right),
            )
        )
    ]
    for made in halo:
        made.start()

    @pl.loop(0, 2)
    def _(i):
        columns = aligned(i, STACK)
        q[:, columns] = nn(a1[...], wqkv[:, columns]).astype(low)

    tall = rows_here + 8
    slot = lax.broadcasted_iota(jnp.int32, (tall, rows_here), 0)
    place = lax.broadcasted_iota(jnp.int32, (tall, rows_here), 1)
    own = jnp.broadcast_to(seg_ref[...].astype(wide), (tall, rows_here))
    inner_seg = jnp.sum(jnp.where(slot == place + 1, own, 0.0), axis=1, keepdims=True)
    slot = lax.broadcasted_iota(jnp.int32, (tall, 1), 0)
    key = lax.broadcasted_iota(jnp.int32, (KEYS, STACK), 0)
    query = lax.broadcasted_iota(jnp.int32, (KEYS, STACK), 1) % ROWS
    gap = (query - key + 2 * LON) % LON
    near = (jnp.abs(key // LON - query // LON - 1) <= 1) & (jnp.minimum(gap, LON - gap) <= 2)
    spread_slot = lax.broadcasted_iota(jnp.int32, (tall, STACK), 0)
    spread_query = (lax.broadcasted_iota(jnp.int32, (tall, STACK), 1) % ROWS) // LON
    key_slot = key // LON

    def mask(i, seg_column):
        first = i * (ROWS // LON)
        query_seg = jnp.sum(
            jnp.where(spread_slot == spread_query + (first + 1), seg_column, 0.0), axis=0, keepdims=True)
        key_seg = jnp.zeros((KEYS, STACK), wide)
        for r in range(KEYS // LON):
            row_seg = jnp.sum(jnp.where(slot == first + r, seg_column, 0.0), axis=0, keepdims=True)
            key_seg = jnp.where(key_slot == r, row_seg, key_seg)
        return jnp.where(near & (key_seg == query_seg), 0.0, NEGATIVE)

    def attend(i, seg_column):
        span = aligned(i, ROWS)
        keys = pl.ds(i * ROWS if isinstance(i, int) else pl.multiple_of(i * ROWS, ROWS), KEYS)
        bias = mask(i, seg_column)
        for g in range(groups):
            lanes = pl.ds(g * GROUP, GROUP)
            scores = nt(kv[0, keys, lanes], stack_heads(q[span, lanes])) * scale + bias
            raised = jnp.exp(scores - jnp.max(scores, axis=0, keepdims=True))
            weights = raised * (1.0 / column_sum(raised))
            prob[i * groups + g] = weights
            mixed = tn(weights.astype(low), kv[1, keys, lanes])
            att[span, lanes] = pick_heads(mixed).astype(low)

    @pl.loop(0, (blocks - 2) // 2)
    def _(i):
        attend(2 * i + 1, inner_seg)
        attend(2 * i + 2, inner_seg)

    for made in halo:
        made.wait()
    before = jnp.where(link.row > 0, seg_box[0, :, rows_here - 1 : rows_here], -1)
    after = jnp.where(link.row < row_count - 1, seg_box[1, :, 0:1], -1)
    outer_seg = jnp.where(slot == 0, before.astype(wide), inner_seg)
    outer_seg = jnp.where(slot == rows_here + 1, after.astype(wide), outer_seg)
    attend(0, outer_seg)
    attend(blocks - 1, outer_seg)

    loads[2].wait()
    for i in range(2):
        columns = pl.ds(i * STACK, STACK)
        hid[:, columns] = tok[:, columns].astype(wide) + nn(att[...], wo[:, columns]) + bias_o[:, columns]

    @pl.loop(0, blocks)
    def _(i):
        span = aligned(i, ROWS)
        norm(hid[span, :], gain2, shift2, hat2, inv2, a2, span)

    for made in loads[3:]:
        made.wait()

    parts = []
    for i, kind in enumerate(KINDS):
        order = ORDERS[kind]
        scratch = take(len(order) + 1)
        parts.append(Part(link, grads.at[i], sums.at[i], order, scratch[:-1], scratch[-1]))
    scratch = take(len(VECTOR_ORDER) + 1)
    vectors = Vectors(link, vec, scratch[:-1], scratch[-1])
    flows = parts + [vectors]
    plan = iter(PLAN)

    def turn():
        for i in next(plan):
            if i < FINISH:
                flows[i].start()
            else:
                flows[i - FINISH].finish()

    vec[0] = jnp.zeros(vec.shape[1:], wide)
    per_row = width // STACK
    for j in range(ff // STACK):
        columns = pl.ds(j * STACK, STACK)
        spot = pl.ds((j % 2) * STACK, STACK)
        pre[...] = nn(a2[...], w1[:, columns]) + bias_1[:, columns]
        dact[...] = nt(cot[...], w2[columns, :])
        turn()

        def gelu(i, total):
            span = aligned(i, 32)
            x = pre[span, :]
            cdf = 0.5 + 0.5 * lax.erf(x * SQRT_HALF)
            act[span, columns] = (x * cdf).astype(low)
            slope = cdf + x * (jnp.exp(x * x * (-0.5)) * DENSITY)
            made = (dact[span, :] * slope).astype(low)
            dpre[span, columns] = made
            return total + jnp.sum(made.astype(wide).reshape(4, 8, STACK), axis=0)

        total = lax.fori_loop(0, tokens // 32, gelu, jnp.zeros((8, STACK), wide), unroll=True)
        vec[0, 5 + j // per_row : 6 + j // per_row, pl.ds((j % per_row) * STACK, STACK)] = column_sum(total)
        turn()
        grads[j // 2 * 2, spot, :] = tn(act[:, columns], cot[...]).astype(low)
        grads[j // 2 * 2 + 1, :, spot] = tn(a2[...], dpre[:, columns]).astype(low)
        turn()
    for i in range(2):
        columns = pl.ds(i * STACK, STACK)
        outacc[:, columns] = nn(act[...], w2[:, columns])
        turn()
    for i in range(2):
        columns = pl.ds(i * STACK, STACK)
        da[:, columns] = nt(dpre[...], w1[columns, :])
        turn()

    def norm_back(incoming, hat_ref, inv_ref, gain, span):
        hat = hat_ref[span, :]
        scaled = incoming * gain[...]
        bracket = scaled - row_mean(scaled) - hat * row_mean(scaled * hat)
        return inv_ref[span, :] * bracket, hat

    def fold(values):
        return jnp.sum(values.reshape(values.shape[0] // 8, 8, values.shape[1]), axis=0)

    def second_back(i, totals):
        span = aligned(i, ROWS)
        incoming = da[span, :]
        part, hat = norm_back(incoming, hat2, inv2, gain2, span)
        up = cot[span, :].astype(wide)
        state = up + part
        dhid[span, :] = state
        rounded = state.astype(low)
        db[span, :] = rounded
        out_ref[span, :] = (hid[span, :] + outacc[span, :] + bias_2[...]).astype(low)
        added = (rounded.astype(wide), incoming * hat, incoming, up)
        return tuple(t + fold(a) for t, a in zip(totals, added))

    zero = jnp.zeros((8, width), wide)
    totals = lax.fori_loop(0, blocks // 2, second_back, (zero,) * 4)
    turn()
    totals = lax.fori_loop(blocks // 2, blocks, second_back, totals)
    for at, total in zip((2, 3, 4, 9), totals):
        vec[0, at : at + 1, :] = column_sum(total)

    turn()
    dout[...] = nt(db[...], wo[...]).astype(low)
    made = tn(att[...], db[...]).astype(low)
    for g in range(groups):
        grads[8 + g, :, 3 * GROUP :] = made[:, g * GROUP : (g + 1) * GROUP]
    turn()

    dkv[...] = jnp.zeros(dkv.shape, wide)

    def attention_back(g):
        lanes = pl.ds(g * GROUP, GROUP)

        def one(i):
            span = aligned(i, ROWS)
            keys = pl.ds(i * ROWS if isinstance(i, int) else pl.multiple_of(i * ROWS, ROWS), KEYS)
            stacked_out = stack_heads(dout[span, lanes])
            stacked_query = stack_heads(q[span, lanes])
            weights = prob[i * groups + g]
            slopes = nt(kv[1, keys, lanes], stacked_out)
            centre = column_sum(weights * slopes)
            ds = (weights * (slopes - centre)).astype(low)
            dkv[0, keys, lanes] += nn(ds, stacked_query) * scale
            dkv[1, keys, lanes] += nn(weights.astype(low), stacked_out)
            dqkv[span, lanes] = (pick_heads(tn(ds, kv[0, keys, lanes])) * scale).astype(low)

        for i in range(blocks):
            one(i)
            turn()

    def rim_copies(g):
        return [remote(rim_send.at[g, side], rim_box.at[g, side], rim_sems, 4 + 2 * g + side, device)
                for side, device in ((0, left), (1, right))]

    def rim_start(g):
        lanes = pl.ds(g * GROUP, GROUP)
        rim_send[g, 0] = dkv[:, 0:LON, lanes].astype(low)
        rim_send[g, 1] = dkv[:, edge : edge + LON, lanes].astype(low)
        for copy in rim_copies(g):
            copy.start()

    def rim_finish(g):
        for copy in rim_copies(g):
            copy.wait()
        lanes = pl.ds(g * GROUP, GROUP)
        dkv[:, tokens : tokens + LON, lanes] += rim_box[g, 0].astype(wide)
        dkv[:, LON : 2 * LON, lanes] += rim_box[g, 1].astype(wide)

    def triple_products(g):
        for which in range(2):
            columns = pl.ds((which + 1) * width + g * GROUP, GROUP)
            dqkv[:, columns] = dkv[which, LON : LON + tokens, pl.ds(g * GROUP, GROUP)].astype(low)
        joined = jnp.concatenate(
            [dqkv[:, pl.ds(which * width + g * GROUP, GROUP)] for which in range(3)], axis=1)
        grads[8 + g, :, : 3 * GROUP] = tn(a1[...], joined).astype(low)
        turn()

    for g in range(groups):
        attention_back(g)
        if g:
            rim_finish(g - 1)
        rim_start(g)
        if g:
            triple_products(g - 1)
    rim_finish(groups - 1)
    triple_products(groups - 1)

    da[...] = nt(dqkv[...], wqkv[...])
    turn()

    def first_back(i, totals):
        span = aligned(i, ROWS)
        incoming = da[span, :]
        part, hat = norm_back(incoming, hat1, inv1, gain1, span)
        dx_ref[span, :] = (dhid[span, :] + part).astype(low)
        return totals[0] + fold(incoming * hat), totals[1] + fold(incoming)

    totals = lax.fori_loop(0, blocks, first_back, (zero,) * 2)
    for at, total in zip((0, 1), totals):
        vec[0, at : at + 1, :] = column_sum(total)
    turn()
    turn()
    vec_out[...] = vec[len(VECTOR_ORDER)]
    for part in parts:
        part.settle()


def run_layer(arrays, dp_count, row_count):
    (tokens, cotangent, wqkv, wo, w1, w2, seg, *vectors) = arrays
    count, width = tokens.shape
    ff = w1.shape[1]
    sizes = link_sizes(dp_count, row_count)
    low, wide = jnp.bfloat16, jnp.float32
    keys = count + 2 * LON
    blocks = count // ROWS
    vm = pltpu.VMEM
    square = (count, width)
    vec_shape = (16, width)
    scratch = [vm(square, low), vm(square, low), vm(wqkv.shape, low), vm(wo.shape, low), vm(w1.shape, low),
               vm(w2.shape, low), pltpu.SemaphoreType.DMA((14,))]
    scratch += [vm(v.shape, v.dtype) for v in (seg, *vectors)]
    scratch += [vm(square, low), vm(square, wide), vm((count, 1), wide), vm(square, low), vm((2, keys, width), low),
                vm((blocks * width // GROUP, KEYS, STACK), wide), vm(square, low), vm(square, wide),
                vm(square, wide), vm((count, 1), wide), vm(square, low)]
    scratch += [vm((count, STACK), wide), vm((count, STACK), wide), vm((count, ff), low), vm((count, ff), low),
                vm(square, wide), vm(square, wide), vm(square, wide), vm(square, low), vm(square, low),
                vm((2, keys, width), wide), vm((count, 3 * width), low)]
    count_parts = len(KINDS)
    slabs = (count_parts, width, width)
    scratch += [vm(slabs, low), vm((5,) + vec_shape, wide),
                vm((STACK, GROUP), low)]
    rims = (width // GROUP, 2, 2, LON, GROUP)
    scratch += [vm((2,) + seg.shape, jnp.int32), vm(rims, low), vm(rims, low),
                pltpu.SemaphoreType.DMA((2, 12))]
    for kind in KINDS:
        scratch += part_scratch((width, width), ORDERS[kind], sizes)
    scratch += vector_scratch(vec_shape, sizes)
    shapes = [(square, low), (square, low), (slabs, low), (vec_shape, wide)]
    vmem = pl.BlockSpec(memory_space=pltpu.VMEM)
    anywhere = pl.BlockSpec(memory_space=pl.ANY)
    return pl.pallas_call(
        partial(layer_kernel, sizes, row_count, width, ff),
        out_shape=[vm(*s) for s in shapes],
        in_specs=[pl.BlockSpec(memory_space=pltpu.HBM)] * 14,
        out_specs=[vmem] * 4,
        scratch_shapes=scratch,
        compiler_params=pltpu.CompilerParams(collective_id=1, has_side_effects=True, vmem_limit_bytes=54 << 20),
        name="layer",
    )(*arrays)


def widen_kernel(factor, width, out_in, dx_in, slabs, vec_ref, out_hbm, dx_hbm, triple_hbm, output_hbm,
                 expand_hbm, reduce_hbm, *refs):
    vector_outs, (triple, output, expand, reduce, out_sems) = refs[:7], refs[7:]
    wide = jnp.float32
    count = slabs.shape[0]
    moves = []

    def send(source, target):
        moves.append(pltpu.make_async_copy(source, target, out_sems.at[len(moves)]))
        moves[-1].start()

    send(out_in, out_hbm)
    send(dx_in, dx_hbm)

    def convert(i, store):
        @pl.loop(0, width // 32)
        def _(at):
            span = pl.ds(pl.multiple_of(at * 32, 32), 32)
            store(span, slabs[i, span, :].astype(wide) * factor)

    for g in range(count - 8):

        def store(span, made):
            for which in range(3):
                triple[span, pl.ds(which * width + g * GROUP, GROUP)] = made[:, which * GROUP : (which + 1) * GROUP]
            output[span, pl.ds(g * GROUP, GROUP)] = made[:, 3 * GROUP :]

        convert(8 + g, store)
    send(triple, triple_hbm)
    send(output, output_hbm)
    for i in range(4):

        def store_reduce(span, made):
            reduce[i, span, :] = made

        def store_expand(span, made):
            expand[i, span, :] = made

        convert(2 * i, store_reduce)
        send(reduce.at[i], reduce_hbm.at[i])
        convert(2 * i + 1, store_expand)
        send(expand.at[i], expand_hbm.at[:, pl.ds(i * width, width)])
    values = vec_ref[...] * factor
    for at, ref in zip((0, 1, 2, 3, 4, 9), vector_outs[:5] + vector_outs[6:]):
        ref[...] = values[at : at + 1]
    for i in range(vector_outs[5].shape[1] // width):
        vector_outs[5][:, i * width : (i + 1) * width] = values[5 + i : 6 + i]
    for move in moves:
        move.wait()


def widen(layer_out, input_grad, sums, vec, factor):
    count, width, _ = sums.shape
    ff = 4 * width
    square = layer_out.shape
    big = [(width, 3 * width), (width, width), (width, ff), (4, width, width)]
    small = [(1, width)] * 5 + [(1, ff), (1, width)]
    wide = jnp.float32
    vm = pltpu.VMEM
    anywhere = pl.BlockSpec(memory_space=pl.ANY)
    vmem = pl.BlockSpec(memory_space=pltpu.VMEM)
    made = pl.pallas_call(
        partial(widen_kernel, factor, width),
        out_shape=[jax.ShapeDtypeStruct(square, layer_out.dtype)] * 2
        + [jax.ShapeDtypeStruct(s, wide) for s in big + small],
        in_specs=[vmem] * 4,
        out_specs=[anywhere] * 6 + [vmem] * 7,
        scratch_shapes=[vm(big[0], wide), vm(big[1], wide), vm(big[3], wide),
                        vm(big[3], wide),
                        pltpu.SemaphoreType.DMA((12,))],
        compiler_params=pltpu.CompilerParams(vmem_limit_bytes=40 << 20),
        name="widen",
    )(layer_out, input_grad, sums, vec)
    return (*made[:5], made[5].reshape(ff, width), *made[6:])


def body(
    tokens,
    segment_ids,
    first_gain,
    first_shift,
    triple_weight,
    output_weight,
    output_bias,
    second_gain,
    second_shift,
    expand_weight,
    expand_bias,
    reduce_weight,
    reduce_bias,
    cotangent,
):
    dp_count, row_count = lax.axis_size("dp"), lax.axis_size("rows")
    flat = [
        v.reshape(1, -1)
        for v in (segment_ids, first_gain, first_shift, output_bias, second_gain, second_shift, expand_bias, reduce_bias)
    ]
    made = run_layer(
        (tokens, cotangent, triple_weight, output_weight, expand_weight, reduce_weight, *flat), dp_count, row_count)
    factor = (tokens.shape[0] * dp_count * row_count) ** (-0.5)
    layer_out, input_grad, triple, output, expand, reduce, *small = widen(*made, factor)
    small = [v.reshape(-1) for v in small]
    return (
        layer_out, input_grad, small[0], small[1], triple, output, small[2], small[3], small[4],
        expand, small[5], reduce, small[6],
    )


def solution(mesh):
    placed = (
        P(("dp", "rows"), None),
        P(("dp", "rows")),
        P(),
        P(),
        P(),
        P(),
        P(),
        P(),
        P(),
        P(),
        P(),
        P(),
        P(),
        P(("dp", "rows"), None),
    )
    return jax.shard_map(
        body,
        mesh=mesh,
        in_specs=placed,
        out_specs=(
            P(("dp", "rows"), None),
            P(("dp", "rows"), None),
            P(),
            P(),
            P(),
            P(),
            P(),
            P(),
            P(),
            P(),
            P(),
            P(),
            P(),
        ),
        check_vma=False,
    )
```

```python
from functools import partial

import jax
import jax.numpy as jnp
from jax import lax
from jax.experimental import pallas as pl
from jax.experimental.pallas import tpu as pltpu
from jax.sharding import PartitionSpec as P

HEAD_DIM = 32
LON = 16
EPSILON = 1e-06
NEGATIVE = -1e30

MESH_ID = pl.DeviceIdType.MESH


def span_of(start, size, unit):
    if isinstance(start, int):
        return pl.ds(start, size)
    return pl.ds(pl.multiple_of(start, unit), size)


class Link:
    def __init__(self, dp_count, row_count):
        self.dp, self.row = lax.axis_index("dp"), lax.axis_index("rows")
        self.sizes = link_sizes(dp_count, row_count)
        z = self.row // 4
        self.place = {
            "core": self.row % 2, "x": self.dp, "y": (self.row // 2) % 2, "z": z, "zl": z % 2, "zh": z // 2,
            "yz": self.row // 2, "xz": z * dp_count + self.dp}
        self.row_count = row_count

    def peer(self, dim, step):
        n, here = self.sizes[dim], self.place[dim]
        there = lax.rem(here + step, n)
        if dim == "x":
            return (there, self.row)
        if dim == "xz":
            wide = self.sizes["x"]
            return (lax.rem(there, wide), self.row + (there // wide - here // wide) * 4)
        if dim == "yz":
            return (self.dp, self.row + (there - here) * 2)
        stride = {"core": 1, "y": 2, "z": 4, "zl": 4, "zh": 8}[dim]
        return (self.dp, self.row + (there - here) * stride)

    def beside(self, step):
        return (self.dp, lax.rem(self.row + step + self.row_count, self.row_count))

    def peers(self):
        found = [self.peer(d, s) for d in ("core", "x", "yz", "xz") for s in range(1, self.sizes[d])]
        return found + [self.beside(1), self.beside(-1)]

    def signal(self):
        barrier = pltpu.get_barrier_semaphore()
        for device in self.peers():
            pl.semaphore_signal(barrier, inc=1, device_id=device, device_id_type=MESH_ID)

    def await_all(self):
        pl.semaphore_wait(pltpu.get_barrier_semaphore(), len(self.peers()))


def link_sizes(dp_count, row_count):
    deep = row_count // 4
    return {"core": 2, "x": dp_count, "y": 2, "z": deep, "zl": 2, "zh": deep // 2,
            "yz": 2 * deep, "xz": dp_count * deep}


def remote(source, target, sems, i, device):
    return pltpu.make_async_remote_copy(
        src_ref=source, dst_ref=target, send_sem=sems.at[0, i], recv_sem=sems.at[1, i],
        device_id=device, device_id_type=MESH_ID)


def piece_grid(dim, n, columns):
    if "z" not in dim or dim == "zl":
        return n, 1
    across = min(n, columns // 128)
    return n // across, across


def phase_shapes(shape, order, sizes):
    shapes, (rows, columns) = [], shape
    for dim in order:
        down, across = piece_grid(dim, sizes[dim], columns)
        rows, columns = rows // down, columns // across
        shapes.append((sizes[dim] - 1, rows, columns))
    return shapes


class Part:
    def __init__(self, link, source, result, order, boxes, sems):
        self.link, self.source, self.result, self.order = link, source, result, order
        self.boxes, self.sems = boxes, sems
        self.step = 0
        top, left = 0, 0
        rows, columns = source.shape
        self.cuts, self.regions, self.first_sem = [], [], []
        used = 0
        for dim in order:
            n, here = link.sizes[dim], link.place[dim]
            down, across = piece_grid(dim, n, columns)
            rows, columns = rows // down, columns // across
            places = []
            for step in range(n):
                which = lax.rem(here + step, n)
                if across == 1:
                    places.append((which * rows, rows, 0, columns))
                else:
                    places.append(((which // across) * rows, rows, lax.rem(which, across) * columns, columns))
            self.cuts.append(places)
            top, left = top + places[0][0], left + places[0][2]
            self.regions.append((top, rows, left, columns))
            self.first_sem.append(used)
            used += n - 1
        self.spread_sem = used

    @property
    def last(self):
        return 2 * len(self.order)

    def view(self, ref, place):
        top, height, left, width = place
        rows = span_of(top, height, 16)
        if width == ref.shape[1]:
            return ref.at[rows, :]
        return ref.at[rows, span_of(left, width, 128)]

    def input_of(self, phase):
        return self.source if phase == 0 else self.boxes[phase - 1].at[0]

    def scatter(self, phase):
        dim = self.order[phase]
        return [
            remote(self.view(self.input_of(phase), self.cuts[phase][step]), self.boxes[phase].at[step - 1],
                   self.sems, self.first_sem[phase] + step - 1, self.link.peer(dim, step))
            for step in range(1, self.link.sizes[dim])
        ]

    def spread(self, phase):
        dim = self.order[phase]
        where = self.view(self.result, self.regions[phase])
        return [
            remote(where, where, self.sems, self.spread_sem + self.first_sem[phase] + step - 1,
                   self.link.peer(dim, step))
            for step in range(1, self.link.sizes[dim])
        ]

    def gain(self, phase):
        box = self.boxes[phase]
        _, height, _, _ = self.cuts[phase][0]
        mine = self.view(self.input_of(phase), self.cuts[phase][0])
        if phase == len(self.order) - 1:
            target = self.view(self.result, self.regions[phase])
        else:
            target = box.at[0]
        rows = min(height, 32)

        @pl.loop(0, height // rows)
        def _(i):
            span = pl.ds(pl.multiple_of(i * rows, rows), rows)
            if box.shape[0] == 1:
                target[span, :] = mine[span, :] + box[0, span, :]
            else:
                total = mine[span, :].astype(jnp.float32)
                for slot in range(box.shape[0]):
                    total += box[slot, span, :].astype(jnp.float32)
                target[span, :] = total.astype(jnp.bfloat16)

    def moves(self, step):
        depth = len(self.order)
        return self.scatter(step) if step < depth else self.spread(2 * depth - 1 - step)

    def start(self):
        for move in self.moves(self.step):
            move.start()
        self.step += 1

    def settle(self):
        for step in range(2 * len(self.order)):
            for move in self.moves(step):
                move.wait_send()

    def finish(self):
        for move in self.moves(self.step - 1):
            move.wait_recv()
        if self.step <= len(self.order):
            self.gain(self.step - 1)


def part_scratch(shape, order, sizes):
    copies = 2 * sum(sizes[d] - 1 for d in order)
    boxes = [pltpu.VMEM(s, jnp.bfloat16) for s in phase_shapes(shape, order, sizes)]
    return boxes + [pltpu.SemaphoreType.DMA((2, copies))]


VECTOR_ORDER = ("core", "x", "y", "z")


def vector_scratch(shape, sizes):
    boxes = [pltpu.VMEM((sizes[d] - 1,) + shape, jnp.float32) for d in VECTOR_ORDER]
    copies = sum(sizes[d] - 1 for d in VECTOR_ORDER)
    return boxes + [pltpu.SemaphoreType.DMA((2, copies))]


class Vectors:
    def __init__(self, link, work, boxes, sems):
        self.link, self.work, self.boxes, self.sems = link, work, boxes, sems
        self.step = 0
        self.last = len(VECTOR_ORDER)

    def moves(self, phase):
        dim = VECTOR_ORDER[phase]
        first = sum(self.link.sizes[d] - 1 for d in VECTOR_ORDER[:phase])
        return [
            remote(self.work.at[phase], self.boxes[phase].at[step - 1], self.sems, first + step - 1,
                   self.link.peer(dim, step))
            for step in range(1, self.link.sizes[dim])
        ]

    def start(self):
        for move in self.moves(self.step):
            move.start()
        self.step += 1

    def finish(self):
        for move in self.moves(self.step - 1):
            move.wait()
        total = self.work[self.step - 1]
        for slot in range(self.boxes[self.step - 1].shape[0]):
            total = total + self.boxes[self.step - 1][slot]
        self.work[self.step] = total


def nn(left, right):
    return lax.dot_general(left, right, (((1,), (0,)), ((), ())), preferred_element_type=jnp.float32)


def nt(left, right):
    return lax.dot_general(left, right, (((1,), (1,)), ((), ())), preferred_element_type=jnp.float32)


def tn(left, right):
    return lax.dot_general(left, right, (((0,), (0,)), ((), ())), preferred_element_type=jnp.float32)


def aligned(index, size):
    if isinstance(index, int):
        return pl.ds(index * size, size)
    return pl.ds(pl.multiple_of(index * size, size), size)


def column_sum(values):
    return jnp.sum(values, axis=0, keepdims=True)


def row_mean(values):
    return jnp.mean(values, axis=-1, keepdims=True)


ROWS = 64
KEYS = 96
GROUP = 128
STACK = 256
SQRT_HALF = 0.5 ** 0.5
DENSITY = (2.0 * 3.141592653589793) ** (-0.5)


ORDERS = (
    ("core", "x", "y", "z"),
    ("core", "y", "x", "z"),
    ("core", "zl", "x", "y", "zh"),
    ("core", "zl", "y", "x", "zh"),
    ("core", "x", "yz"),
    ("core", "y", "xz"),
)
FINISH = 100
KINDS = (2, 0, 1, 3, 3, 1, 2, 0, 1, 0, 0, 1)
PLAN = (
    (),
    (),
    (),
    (),
    (),
    (0, 1),
    (),
    (),
    (),
    (),
    (),
    (3, 2),
    (),
    (),
    (100, 0, 101, 1),
    (),
    (),
    (5, 4),
    (),
    (),
    (103, 3, 102, 2),
    (),
    (),
    (6, 7),
    (105, 104, 4),
    (),
    (5,),
    (101, 106, 6, 107, 7, 100),
    (),
    (1, 102),
    (),
    (),
    (),
    (),
    (),
    (),
    (),
    (),
    (0, 103, 3, 105),
    (),
    (),
    (),
    (),
    (),
    (),
    (),
    (5, 107, 7, 101, 1, 104, 106),
    (8, 100, 6, 103, 4),
    (),
    (),
    (),
    (),
    (),
    (),
    (),
    (0, 3, 108, 101, 1, 105, 5, 107, 7),
    (9, 8, 2, 106, 104),
    (),
    (),
    (),
    (),
    (),
    (),
    (),
    (6, 4, 100, 0, 109, 103, 3),
    (9, 10),
    (11, 102, 2, 101, 1, 105, 5, 107, 7, 108, 110, 100, 106, 10, 104, 103),
    (111, 11),
    (8, 6, 4, 0, 12, 109, 101),
    (102, 3, 9, 2, 105, 112, 107, 5, 110, 10, 12, 106, 6, 111, 104, 4, 100, 108, 8, 11, 103, 0, 109, 9, 7, 102, 105, 3, 112, 106, 2, 110, 10, 5, 104, 100, 111, 11, 4, 108, 8, 103, 0, 109, 9, 107, 6, 110, 102, 7, 10, 3, 104, 105, 5, 4, 100, 0, 111, 11, 106, 108, 6, 105, 2, 109, 103, 3, 110, 8, 107, 7, 104, 4, 1, 9, 107, 106, 111, 10, 108, 102, 2, 11, 8, 6, 109, 102, 9, 101, 1, 110, 100, 0, 12, 111, 101, 11, 100, 10, 108, 8, 103, 3, 112, 12, 109, 9, 104, 4, 108, 103, 106, 6, 109, 104, 111, 11, 110, 10, 106, 112, 111, 110),
)


def layer_kernel(sizes, row_count, width, ff, *refs):
    refs = list(refs)

    def take(n):
        taken = refs[:n]
        del refs[:n]
        return taken

    (tok_hbm, cot_hbm, wqkv_hbm, wo_hbm, w1_hbm, w2_hbm) = take(6)
    small_hbm = take(8)
    (out_ref, dx_ref, sums, vec_out) = take(4)
    (tok, cot, wqkv, wo, w1, w2, load_sems) = take(7)
    small = take(8)
    (seg_ref, gain1, shift1, bias_o, gain2, shift2, bias_1, bias_2) = small
    (a1, hat1, inv1, q, kv, prob, att, hid, hat2, inv2, a2) = take(11)
    (pre, dact, act, dpre, outacc, da, dhid, db, dout, dkv, dqkv) = take(11)
    (grads, vec, head_mask) = take(3)
    (seg_box, rim_send, rim_box, rim_sems) = take(4)
    low = jnp.bfloat16
    wide = jnp.float32
    tokens = tok.shape[0]
    rows_here = seg_ref.shape[1]
    blocks = tokens // ROWS
    groups = width // GROUP
    scale = HEAD_DIM ** (-0.5)

    link = Link(sizes["x"], row_count)
    link.signal()
    loads = [
        pltpu.make_async_copy(source, target, load_sems.at[i])
        for i, (source, target) in enumerate(
            ((tok_hbm, tok), (wqkv_hbm, wqkv), (wo_hbm, wo), (cot_hbm, cot), (w1_hbm, w1), (w2_hbm, w2)))
    ]
    small_loads = [
        pltpu.make_async_copy(source, target, load_sems.at[6 + i])
        for i, (source, target) in enumerate(zip(small_hbm, small))
    ]
    loads[0].start()
    for made in small_loads:
        made.start()
    loads[1].start()

    lane = lax.broadcasted_iota(jnp.int32, (ROWS, GROUP), 1) // HEAD_DIM
    for h in range(4):
        head_mask[pl.ds(h * ROWS, ROWS), :] = jnp.where(lane == h, 1.0, 0.0).astype(low)

    def stack_heads(block):
        return jnp.concatenate([block] * 4, axis=0) * head_mask[...]

    def pick_heads(stacked):
        picked = stacked[3 * ROWS :]
        for h in (2, 1, 0):
            picked = jnp.where(lane == h, stacked[h * ROWS : (h + 1) * ROWS], picked)
        return picked

    loads[0].wait()
    for made in small_loads:
        made.wait()

    def norm(values, gain, shift, hat_ref, inv_ref, out, span):
        centred = values - row_mean(values)
        inv = lax.rsqrt(row_mean(centred * centred) + EPSILON)
        hat = centred * inv
        hat_ref[span, :] = hat
        inv_ref[span, :] = inv
        out[span, :] = (hat * gain[...] + shift[...]).astype(low)

    @pl.loop(0, blocks)
    def _(i):
        span = aligned(i, ROWS)
        norm(tok[span, :].astype(wide), gain1, shift1, hat1, inv1, a1, span)

    loads[1].wait()
    for made in loads[2:]:
        made.start()
    for which in range(2):

        @pl.loop(0, 2)
        def _(i):
            columns = aligned(i, STACK)
            source = pl.ds(pl.multiple_of((which + 1) * width + i * STACK, STACK), STACK)
            kv[which, LON : LON + tokens, columns] = nn(a1[...], wqkv[:, source]).astype(low)

    link.await_all()
    edge = LON + tokens
    left, right = link.beside(-1), link.beside(1)
    halo = [
        remote(source, target, rim_sems, i, device)
        for i, (source, target, device) in enumerate(
            (
                (kv.at[:, pl.ds(LON, LON), :], kv.at[:, pl.ds(edge, LON), :], left),
                (kv.at[:, pl.ds(tokens, LON), :], kv.at[:, pl.ds(0, LON), :], right),
                (seg_ref, seg_box.at[1], left),
                (seg_ref, seg_box.at[0], right),
            )
        )
    ]
    for made in halo:
        made.start()

    @pl.loop(0, 2)
    def _(i):
        columns = aligned(i, STACK)
        q[:, columns] = nn(a1[...], wqkv[:, columns]).astype(low)

    tall = rows_here + 8
    slot = lax.broadcasted_iota(jnp.int32, (tall, rows_here), 0)
    place = lax.broadcasted_iota(jnp.int32, (tall, rows_here), 1)
    own = jnp.broadcast_to(seg_ref[...].astype(wide), (tall, rows_here))
    inner_seg = jnp.sum(jnp.where(slot == place + 1, own, 0.0), axis=1, keepdims=True)
    slot = lax.broadcasted_iota(jnp.int32, (tall, 1), 0)
    key = lax.broadcasted_iota(jnp.int32, (KEYS, STACK), 0)
    query = lax.broadcasted_iota(jnp.int32, (KEYS, STACK), 1) % ROWS
    gap = (query - key + 2 * LON) % LON
    near = (jnp.abs(key // LON - query // LON - 1) <= 1) & (jnp.minimum(gap, LON - gap) <= 2)
    spread_slot = lax.broadcasted_iota(jnp.int32, (tall, STACK), 0)
    spread_query = (lax.broadcasted_iota(jnp.int32, (tall, STACK), 1) % ROWS) // LON
    key_slot = key // LON

    def mask(i, seg_column):
        first = i * (ROWS // LON)
        query_seg = jnp.sum(
            jnp.where(spread_slot == spread_query + (first + 1), seg_column, 0.0), axis=0, keepdims=True)
        key_seg = jnp.zeros((KEYS, STACK), wide)
        for r in range(KEYS // LON):
            row_seg = jnp.sum(jnp.where(slot == first + r, seg_column, 0.0), axis=0, keepdims=True)
            key_seg = jnp.where(key_slot == r, row_seg, key_seg)
        return jnp.where(near & (key_seg == query_seg), 0.0, NEGATIVE)

    def attend(i, seg_column):
        span = aligned(i, ROWS)
        keys = pl.ds(i * ROWS if isinstance(i, int) else pl.multiple_of(i * ROWS, ROWS), KEYS)
        bias = mask(i, seg_column)
        for g in range(groups):
            lanes = pl.ds(g * GROUP, GROUP)
            scores = nt(kv[0, keys, lanes], stack_heads(q[span, lanes])) * scale + bias
            raised = jnp.exp(scores - jnp.max(scores, axis=0, keepdims=True))
            weights = raised * (1.0 / column_sum(raised))
            prob[i * groups + g] = weights
            mixed = tn(weights.astype(low), kv[1, keys, lanes])
            att[span, lanes] = pick_heads(mixed).astype(low)

    @pl.loop(0, (blocks - 2) // 2)
    def _(i):
        attend(2 * i + 1, inner_seg)
        attend(2 * i + 2, inner_seg)

    for made in halo:
        made.wait()
    before = jnp.where(link.row > 0, seg_box[0, :, rows_here - 1 : rows_here], -1)
    after = jnp.where(link.row < row_count - 1, seg_box[1, :, 0:1], -1)
    outer_seg = jnp.where(slot == 0, before.astype(wide), inner_seg)
    outer_seg = jnp.where(slot == rows_here + 1, after.astype(wide), outer_seg)
    attend(0, outer_seg)
    attend(blocks - 1, outer_seg)

    loads[2].wait()
    for i in range(2):
        columns = pl.ds(i * STACK, STACK)
        hid[:, columns] = tok[:, columns].astype(wide) + nn(att[...], wo[:, columns]) + bias_o[:, columns]

    @pl.loop(0, blocks)
    def _(i):
        span = aligned(i, ROWS)
        norm(hid[span, :], gain2, shift2, hat2, inv2, a2, span)

    for made in loads[3:]:
        made.wait()

    parts = []
    for i, kind in enumerate(KINDS):
        order = ORDERS[kind]
        scratch = take(len(order) + 1)
        parts.append(Part(link, grads.at[i], sums.at[i], order, scratch[:-1], scratch[-1]))
    scratch = take(len(VECTOR_ORDER) + 1)
    vectors = Vectors(link, vec, scratch[:-1], scratch[-1])
    flows = parts + [vectors]
    plan = iter(PLAN)

    def turn():
        for i in next(plan):
            if i < FINISH:
                flows[i].start()
            else:
                flows[i - FINISH].finish()

    vec[0] = jnp.zeros(vec.shape[1:], wide)
    per_row = width // STACK
    for j in range(ff // STACK):
        columns = pl.ds(j * STACK, STACK)
        spot = pl.ds((j % 2) * STACK, STACK)
        pre[...] = nn(a2[...], w1[:, columns]) + bias_1[:, columns]
        dact[...] = nt(cot[...], w2[columns, :])
        turn()

        def gelu(i, total):
            span = aligned(i, 32)
            x = pre[span, :]
            cdf = 0.5 + 0.5 * lax.erf(x * SQRT_HALF)
            act[span, columns] = (x * cdf).astype(low)
            slope = cdf + x * (jnp.exp(x * x * (-0.5)) * DENSITY)
            made = (dact[span, :] * slope).astype(low)
            dpre[span, columns] = made
            return total + jnp.sum(made.astype(wide).reshape(4, 8, STACK), axis=0)

        total = lax.fori_loop(0, tokens // 32, gelu, jnp.zeros((8, STACK), wide), unroll=True)
        vec[0, 5 + j // per_row : 6 + j // per_row, pl.ds((j % per_row) * STACK, STACK)] = column_sum(total)
        turn()
        grads[j // 2 * 2, spot, :] = tn(act[:, columns], cot[...]).astype(low)
        grads[j // 2 * 2 + 1, :, spot] = tn(a2[...], dpre[:, columns]).astype(low)
        turn()
    for i in range(2):
        columns = pl.ds(i * STACK, STACK)
        outacc[:, columns] = nn(act[...], w2[:, columns])
        turn()
    for i in range(2):
        columns = pl.ds(i * STACK, STACK)
        da[:, columns] = nt(dpre[...], w1[columns, :])
        turn()

    def norm_back(incoming, hat_ref, inv_ref, gain, span):
        hat = hat_ref[span, :]
        scaled = incoming * gain[...]
        bracket = scaled - row_mean(scaled) - hat * row_mean(scaled * hat)
        return inv_ref[span, :] * bracket, hat

    def fold(values):
        return jnp.sum(values.reshape(values.shape[0] // 8, 8, values.shape[1]), axis=0)

    def second_back(i, totals):
        span = aligned(i, ROWS)
        incoming = da[span, :]
        part, hat = norm_back(incoming, hat2, inv2, gain2, span)
        up = cot[span, :].astype(wide)
        state = up + part
        dhid[span, :] = state
        rounded = state.astype(low)
        db[span, :] = rounded
        out_ref[span, :] = (hid[span, :] + outacc[span, :] + bias_2[...]).astype(low)
        added = (rounded.astype(wide), incoming * hat, incoming, up)
        return tuple(t + fold(a) for t, a in zip(totals, added))

    zero = jnp.zeros((8, width), wide)
    totals = lax.fori_loop(0, blocks // 2, second_back, (zero,) * 4)
    turn()
    totals = lax.fori_loop(blocks // 2, blocks, second_back, totals)
    for at, total in zip((2, 3, 4, 9), totals):
        vec[0, at : at + 1, :] = column_sum(total)

    turn()
    dout[...] = nt(db[...], wo[...]).astype(low)
    made = tn(att[...], db[...]).astype(low)
    for g in range(groups):
        grads[8 + g, :, 3 * GROUP :] = made[:, g * GROUP : (g + 1) * GROUP]
    turn()

    dkv[...] = jnp.zeros(dkv.shape, wide)

    def attention_back(g):
        lanes = pl.ds(g * GROUP, GROUP)

        def one(i):
            span = aligned(i, ROWS)
            keys = pl.ds(i * ROWS if isinstance(i, int) else pl.multiple_of(i * ROWS, ROWS), KEYS)
            stacked_out = stack_heads(dout[span, lanes])
            stacked_query = stack_heads(q[span, lanes])
            weights = prob[i * groups + g]
            slopes = nt(kv[1, keys, lanes], stacked_out)
            centre = column_sum(weights * slopes)
            ds = (weights * (slopes - centre)).astype(low)
            dkv[0, keys, lanes] += nn(ds, stacked_query) * scale
            dkv[1, keys, lanes] += nn(weights.astype(low), stacked_out)
            dqkv[span, lanes] = (pick_heads(tn(ds, kv[0, keys, lanes])) * scale).astype(low)

        for i in range(blocks):
            one(i)
            turn()

    def rim_copies(g):
        return [remote(rim_send.at[g, side], rim_box.at[g, side], rim_sems, 4 + 2 * g + side, device)
                for side, device in ((0, left), (1, right))]

    def rim_start(g):
        lanes = pl.ds(g * GROUP, GROUP)
        rim_send[g, 0] = dkv[:, 0:LON, lanes].astype(low)
        rim_send[g, 1] = dkv[:, edge : edge + LON, lanes].astype(low)
        for copy in rim_copies(g):
            copy.start()

    def rim_finish(g):
        for copy in rim_copies(g):
            copy.wait()
        lanes = pl.ds(g * GROUP, GROUP)
        dkv[:, tokens : tokens + LON, lanes] += rim_box[g, 0].astype(wide)
        dkv[:, LON : 2 * LON, lanes] += rim_box[g, 1].astype(wide)

    def triple_products(g):
        for which in range(2):
            columns = pl.ds((which + 1) * width + g * GROUP, GROUP)
            dqkv[:, columns] = dkv[which, LON : LON + tokens, pl.ds(g * GROUP, GROUP)].astype(low)
        joined = jnp.concatenate(
            [dqkv[:, pl.ds(which * width + g * GROUP, GROUP)] for which in range(3)], axis=1)
        grads[8 + g, :, : 3 * GROUP] = tn(a1[...], joined).astype(low)
        turn()

    for g in range(groups):
        attention_back(g)
        if g:
            rim_finish(g - 1)
        rim_start(g)
        if g:
            triple_products(g - 1)
    rim_finish(groups - 1)
    triple_products(groups - 1)

    da[...] = nt(dqkv[...], wqkv[...])
    turn()

    def first_back(i, totals):
        span = aligned(i, ROWS)
        incoming = da[span, :]
        part, hat = norm_back(incoming, hat1, inv1, gain1, span)
        dx_ref[span, :] = (dhid[span, :] + part).astype(low)
        return totals[0] + fold(incoming * hat), totals[1] + fold(incoming)

    totals = lax.fori_loop(0, blocks, first_back, (zero,) * 2)
    for at, total in zip((0, 1), totals):
        vec[0, at : at + 1, :] = column_sum(total)
    turn()
    turn()
    vec_out[...] = vec[len(VECTOR_ORDER)]
    for part in parts:
        part.settle()


def run_layer(arrays, dp_count, row_count):
    (tokens, cotangent, wqkv, wo, w1, w2, seg, *vectors) = arrays
    count, width = tokens.shape
    ff = w1.shape[1]
    sizes = link_sizes(dp_count, row_count)
    low, wide = jnp.bfloat16, jnp.float32
    keys = count + 2 * LON
    blocks = count // ROWS
    vm = pltpu.VMEM
    square = (count, width)
    vec_shape = (16, width)
    scratch = [vm(square, low), vm(square, low), vm(wqkv.shape, low), vm(wo.shape, low), vm(w1.shape, low),
               vm(w2.shape, low), pltpu.SemaphoreType.DMA((14,))]
    scratch += [vm(v.shape, v.dtype) for v in (seg, *vectors)]
    scratch += [vm(square, low), vm(square, wide), vm((count, 1), wide), vm(square, low), vm((2, keys, width), low),
                vm((blocks * width // GROUP, KEYS, STACK), wide), vm(square, low), vm(square, wide),
                vm(square, wide), vm((count, 1), wide), vm(square, low)]
    scratch += [vm((count, STACK), wide), vm((count, STACK), wide), vm((count, ff), low), vm((count, ff), low),
                vm(square, wide), vm(square, wide), vm(square, wide), vm(square, low), vm(square, low),
                vm((2, keys, width), wide), vm((count, 3 * width), low)]
    count_parts = len(KINDS)
    slabs = (count_parts, width, width)
    scratch += [vm(slabs, low), vm((5,) + vec_shape, wide),
                vm((STACK, GROUP), low)]
    rims = (width // GROUP, 2, 2, LON, GROUP)
    scratch += [vm((2,) + seg.shape, jnp.int32), vm(rims, low), vm(rims, low),
                pltpu.SemaphoreType.DMA((2, 12))]
    for kind in KINDS:
        scratch += part_scratch((width, width), ORDERS[kind], sizes)
    scratch += vector_scratch(vec_shape, sizes)
    shapes = [(square, low), (square, low), (slabs, low), (vec_shape, wide)]
    vmem = pl.BlockSpec(memory_space=pltpu.VMEM)
    anywhere = pl.BlockSpec(memory_space=pl.ANY)
    return pl.pallas_call(
        partial(layer_kernel, sizes, row_count, width, ff),
        out_shape=[vm(*s) for s in shapes],
        in_specs=[pl.BlockSpec(memory_space=pltpu.HBM)] * 14,
        out_specs=[vmem] * 4,
        scratch_shapes=scratch,
        compiler_params=pltpu.CompilerParams(collective_id=1, has_side_effects=True, vmem_limit_bytes=54 << 20),
        name="layer",
    )(*arrays)


def widen_kernel(factor, width, out_in, dx_in, slabs, vec_ref, out_hbm, dx_hbm, triple_hbm, output_hbm,
                 expand_hbm, reduce_hbm, *refs):
    vector_outs, (triple, output, expand, reduce, out_sems) = refs[:7], refs[7:]
    wide = jnp.float32
    count = slabs.shape[0]
    moves = []

    def send(source, target):
        moves.append(pltpu.make_async_copy(source, target, out_sems.at[len(moves)]))
        moves[-1].start()

    send(out_in, out_hbm)
    send(dx_in, dx_hbm)

    def convert(i, store):
        @pl.loop(0, width // 32)
        def _(at):
            span = pl.ds(pl.multiple_of(at * 32, 32), 32)
            store(span, slabs[i, span, :].astype(wide) * factor)

    def store_reduce(i, span, made):
        reduce[i, span, :] = made

    def store_expand(i, span, made):
        expand[i, span, :] = made

    def store_group(g, span, made):
        for which in range(3):
            triple[span, pl.ds(which * width + g * GROUP, GROUP)] = made[:, which * GROUP : (which + 1) * GROUP]
        output[span, pl.ds(g * GROUP, GROUP)] = made[:, 3 * GROUP :]

    for i in range(4):
        convert(2 * i, partial(store_reduce, i))
        send(reduce.at[i], reduce_hbm.at[i])
        convert(2 * i + 1, partial(store_expand, i))
        send(expand.at[i], expand_hbm.at[:, pl.ds(i * width, width)])
        if i == 1:
            for g in range(count - 8):
                convert(8 + g, partial(store_group, g))
            send(triple, triple_hbm)
            send(output, output_hbm)
    values = vec_ref[...] * factor
    for at, ref in zip((0, 1, 2, 3, 4, 9), vector_outs[:5] + vector_outs[6:]):
        ref[...] = values[at : at + 1]
    for i in range(vector_outs[5].shape[1] // width):
        vector_outs[5][:, i * width : (i + 1) * width] = values[5 + i : 6 + i]
    for move in moves:
        move.wait()


def widen(layer_out, input_grad, sums, vec, factor):
    count, width, _ = sums.shape
    ff = 4 * width
    square = layer_out.shape
    big = [(width, 3 * width), (width, width), (width, ff), (4, width, width)]
    small = [(1, width)] * 5 + [(1, ff), (1, width)]
    wide = jnp.float32
    vm = pltpu.VMEM
    anywhere = pl.BlockSpec(memory_space=pl.ANY)
    vmem = pl.BlockSpec(memory_space=pltpu.VMEM)
    made = pl.pallas_call(
        partial(widen_kernel, factor, width),
        out_shape=[jax.ShapeDtypeStruct(square, layer_out.dtype)] * 2
        + [jax.ShapeDtypeStruct(s, wide) for s in big + small],
        in_specs=[vmem] * 4,
        out_specs=[anywhere] * 6 + [vmem] * 7,
        scratch_shapes=[vm(big[0], wide), vm(big[1], wide), vm(big[3], wide),
                        vm(big[3], wide),
                        pltpu.SemaphoreType.DMA((12,))],
        compiler_params=pltpu.CompilerParams(vmem_limit_bytes=40 << 20),
        name="widen",
    )(layer_out, input_grad, sums, vec)
    return (*made[:5], made[5].reshape(ff, width), *made[6:])


def body(
    tokens,
    segment_ids,
    first_gain,
    first_shift,
    triple_weight,
    output_weight,
    output_bias,
    second_gain,
    second_shift,
    expand_weight,
    expand_bias,
    reduce_weight,
    reduce_bias,
    cotangent,
):
    dp_count, row_count = lax.axis_size("dp"), lax.axis_size("rows")
    flat = [
        v.reshape(1, -1)
        for v in (segment_ids, first_gain, first_shift, output_bias, second_gain, second_shift, expand_bias, reduce_bias)
    ]
    made = run_layer(
        (tokens, cotangent, triple_weight, output_weight, expand_weight, reduce_weight, *flat), dp_count, row_count)
    factor = (tokens.shape[0] * dp_count * row_count) ** (-0.5)
    layer_out, input_grad, triple, output, expand, reduce, *small = widen(*made, factor)
    small = [v.reshape(-1) for v in small]
    return (
        layer_out, input_grad, small[0], small[1], triple, output, small[2], small[3], small[4],
        expand, small[5], reduce, small[6],
    )


def solution(mesh):
    placed = (
        P(("dp", "rows"), None),
        P(("dp", "rows")),
        P(),
        P(),
        P(),
        P(),
        P(),
        P(),
        P(),
        P(),
        P(),
        P(),
        P(),
        P(("dp", "rows"), None),
    )
    return jax.shard_map(
        body,
        mesh=mesh,
        in_specs=placed,
        out_specs=(
            P(("dp", "rows"), None),
            P(("dp", "rows"), None),
            P(),
            P(),
            P(),
            P(),
            P(),
            P(),
            P(),
            P(),
            P(),
            P(),
            P(),
        ),
        check_vma=False,
    )
```

```python
from functools import partial

import jax
import jax.numpy as jnp
from jax import lax
from jax.experimental import pallas as pl
from jax.experimental.pallas import tpu as pltpu
from jax.sharding import PartitionSpec as P

HEAD_DIM = 32
LON = 16
EPSILON = 1e-06
NEGATIVE = -1e30

MESH_ID = pl.DeviceIdType.MESH


def span_of(start, size, unit):
    if isinstance(start, int):
        return pl.ds(start, size)
    return pl.ds(pl.multiple_of(start, unit), size)


class Link:
    def __init__(self, dp_count, row_count):
        self.dp, self.row = lax.axis_index("dp"), lax.axis_index("rows")
        self.sizes = link_sizes(dp_count, row_count)
        z = self.row // 4
        self.place = {
            "core": self.row % 2, "x": self.dp, "y": (self.row // 2) % 2, "z": z, "zl": z % 2, "zh": z // 2,
            "yz": self.row // 2, "xz": z * dp_count + self.dp}
        self.row_count = row_count

    def peer(self, dim, step):
        n, here = self.sizes[dim], self.place[dim]
        there = lax.rem(here + step, n)
        if dim == "x":
            return (there, self.row)
        if dim == "xz":
            wide = self.sizes["x"]
            return (lax.rem(there, wide), self.row + (there // wide - here // wide) * 4)
        if dim == "yz":
            return (self.dp, self.row + (there - here) * 2)
        stride = {"core": 1, "y": 2, "z": 4, "zl": 4, "zh": 8}[dim]
        return (self.dp, self.row + (there - here) * stride)

    def beside(self, step):
        return (self.dp, lax.rem(self.row + step + self.row_count, self.row_count))

    def peers(self):
        found = [self.peer(d, s) for d in ("core", "x", "yz", "xz") for s in range(1, self.sizes[d])]
        return found + [self.beside(1), self.beside(-1)]

    def signal(self):
        barrier = pltpu.get_barrier_semaphore()
        for device in self.peers():
            pl.semaphore_signal(barrier, inc=1, device_id=device, device_id_type=MESH_ID)

    def await_all(self):
        pl.semaphore_wait(pltpu.get_barrier_semaphore(), len(self.peers()))


def link_sizes(dp_count, row_count):
    deep = row_count // 4
    return {"core": 2, "x": dp_count, "y": 2, "z": deep, "zl": 2, "zh": deep // 2,
            "yz": 2 * deep, "xz": dp_count * deep}


def remote(source, target, sems, i, device):
    return pltpu.make_async_remote_copy(
        src_ref=source, dst_ref=target, send_sem=sems.at[0, i], recv_sem=sems.at[1, i],
        device_id=device, device_id_type=MESH_ID)


def piece_grid(dim, n, columns):
    if "z" not in dim or dim == "zl":
        return n, 1
    across = min(n, columns // 128)
    return n // across, across


def phase_shapes(shape, order, sizes):
    shapes, (rows, columns) = [], shape
    for dim in order:
        down, across = piece_grid(dim, sizes[dim], columns)
        rows, columns = rows // down, columns // across
        shapes.append((sizes[dim] - 1, rows, columns))
    return shapes


class Part:
    def __init__(self, link, source, result, order, boxes, sems):
        self.link, self.source, self.result, self.order = link, source, result, order
        self.boxes, self.sems = boxes, sems
        self.step = 0
        top, left = 0, 0
        rows, columns = source.shape
        self.cuts, self.regions, self.first_sem = [], [], []
        used = 0
        for dim in order:
            n, here = link.sizes[dim], link.place[dim]
            down, across = piece_grid(dim, n, columns)
            rows, columns = rows // down, columns // across
            places = []
            for step in range(n):
                which = lax.rem(here + step, n)
                if across == 1:
                    places.append((which * rows, rows, 0, columns))
                else:
                    places.append(((which // across) * rows, rows, lax.rem(which, across) * columns, columns))
            self.cuts.append(places)
            top, left = top + places[0][0], left + places[0][2]
            self.regions.append((top, rows, left, columns))
            self.first_sem.append(used)
            used += n - 1
        self.spread_sem = used

    @property
    def last(self):
        return 2 * len(self.order)

    def view(self, ref, place):
        top, height, left, width = place
        rows = span_of(top, height, 16)
        if width == ref.shape[1]:
            return ref.at[rows, :]
        return ref.at[rows, span_of(left, width, 128)]

    def input_of(self, phase):
        return self.source if phase == 0 else self.boxes[phase - 1].at[0]

    def scatter(self, phase):
        dim = self.order[phase]
        return [
            remote(self.view(self.input_of(phase), self.cuts[phase][step]), self.boxes[phase].at[step - 1],
                   self.sems, self.first_sem[phase] + step - 1, self.link.peer(dim, step))
            for step in range(1, self.link.sizes[dim])
        ]

    def spread(self, phase):
        dim = self.order[phase]
        where = self.view(self.result, self.regions[phase])
        return [
            remote(where, where, self.sems, self.spread_sem + self.first_sem[phase] + step - 1,
                   self.link.peer(dim, step))
            for step in range(1, self.link.sizes[dim])
        ]

    def gain(self, phase):
        box = self.boxes[phase]
        _, height, _, _ = self.cuts[phase][0]
        mine = self.view(self.input_of(phase), self.cuts[phase][0])
        if phase == len(self.order) - 1:
            target = self.view(self.result, self.regions[phase])
        else:
            target = box.at[0]
        rows = min(height, 32)

        @pl.loop(0, height // rows)
        def _(i):
            span = pl.ds(pl.multiple_of(i * rows, rows), rows)
            if box.shape[0] == 1:
                target[span, :] = mine[span, :] + box[0, span, :]
            else:
                total = mine[span, :].astype(jnp.float32)
                for slot in range(box.shape[0]):
                    total += box[slot, span, :].astype(jnp.float32)
                target[span, :] = total.astype(jnp.bfloat16)

    def moves(self, step):
        depth = len(self.order)
        return self.scatter(step) if step < depth else self.spread(2 * depth - 1 - step)

    def start(self):
        for move in self.moves(self.step):
            move.start()
        self.step += 1

    def settle(self):
        for step in range(2 * len(self.order)):
            for move in self.moves(step):
                move.wait_send()

    def finish(self):
        for move in self.moves(self.step - 1):
            move.wait_recv()
        if self.step <= len(self.order):
            self.gain(self.step - 1)


def part_scratch(shape, order, sizes):
    copies = 2 * sum(sizes[d] - 1 for d in order)
    boxes = [pltpu.VMEM(s, jnp.bfloat16) for s in phase_shapes(shape, order, sizes)]
    return boxes + [pltpu.SemaphoreType.DMA((2, copies))]


VECTOR_ORDER = ("core", "x", "y", "z")


def vector_scratch(shape, sizes):
    boxes = [pltpu.VMEM((sizes[d] - 1,) + shape, jnp.float32) for d in VECTOR_ORDER]
    copies = sum(sizes[d] - 1 for d in VECTOR_ORDER)
    return boxes + [pltpu.SemaphoreType.DMA((2, copies))]


class Vectors:
    def __init__(self, link, work, boxes, sems):
        self.link, self.work, self.boxes, self.sems = link, work, boxes, sems
        self.step = 0
        self.last = len(VECTOR_ORDER)

    def moves(self, phase):
        dim = VECTOR_ORDER[phase]
        first = sum(self.link.sizes[d] - 1 for d in VECTOR_ORDER[:phase])
        return [
            remote(self.work.at[phase], self.boxes[phase].at[step - 1], self.sems, first + step - 1,
                   self.link.peer(dim, step))
            for step in range(1, self.link.sizes[dim])
        ]

    def start(self):
        for move in self.moves(self.step):
            move.start()
        self.step += 1

    def finish(self):
        for move in self.moves(self.step - 1):
            move.wait()
        total = self.work[self.step - 1]
        for slot in range(self.boxes[self.step - 1].shape[0]):
            total = total + self.boxes[self.step - 1][slot]
        self.work[self.step] = total


def nn(left, right):
    return lax.dot_general(left, right, (((1,), (0,)), ((), ())), preferred_element_type=jnp.float32)


def nt(left, right):
    return lax.dot_general(left, right, (((1,), (1,)), ((), ())), preferred_element_type=jnp.float32)


def tn(left, right):
    return lax.dot_general(left, right, (((0,), (0,)), ((), ())), preferred_element_type=jnp.float32)


def aligned(index, size):
    if isinstance(index, int):
        return pl.ds(index * size, size)
    return pl.ds(pl.multiple_of(index * size, size), size)


def column_sum(values):
    return jnp.sum(values, axis=0, keepdims=True)


def row_mean(values):
    return jnp.mean(values, axis=-1, keepdims=True)


ROWS = 64
KEYS = 96
GROUP = 128
STACK = 256
SQRT_HALF = 0.5 ** 0.5
DENSITY = (2.0 * 3.141592653589793) ** (-0.5)


ORDERS = (
    ("core", "x", "y", "z"),
    ("core", "y", "x", "z"),
    ("core", "zl", "x", "y", "zh"),
    ("core", "zl", "y", "x", "zh"),
    ("core", "x", "yz"),
    ("core", "y", "xz"),
)
FINISH = 100
KINDS = (2, 0, 1, 3, 3, 1, 2, 0, 1, 0, 0, 1)
PLAN = (
    (),
    (),
    (),
    (),
    (),
    (0, 1),
    (),
    (),
    (),
    (),
    (),
    (3, 2),
    (),
    (),
    (100, 0, 101, 1),
    (),
    (),
    (4, 5),
    (),
    (),
    (103, 3, 102, 2),
    (),
    (),
    (6, 7),
    (104, 4, 105),
    (),
    (5,),
    (101, 106, 6, 107, 7, 100),
    (),
    (1, 102),
    (),
    (),
    (),
    (),
    (),
    (),
    (),
    (),
    (0, 103, 3, 105),
    (),
    (),
    (),
    (),
    (),
    (),
    (),
    (5, 107, 7, 101, 1, 104, 106),
    (8, 100, 6, 103, 4),
    (),
    (),
    (),
    (),
    (),
    (),
    (),
    (0, 3, 108, 101, 1, 105, 5, 107, 7),
    (9, 8, 2, 106, 104),
    (),
    (),
    (),
    (),
    (),
    (),
    (),
    (4, 6, 100, 0, 109, 103, 3),
    (10, 9),
    (11, 102, 2, 101, 1, 105, 5, 107, 7, 108, 110, 100, 104, 106, 10, 103),
    (111, 11),
    (8, 4, 6, 0, 12, 109, 101),
    (102, 3, 9, 2, 105, 112, 107, 5, 110, 10, 12, 104, 4, 111, 106, 6, 100, 108, 8, 11, 103, 0, 109, 9, 7, 102, 105, 3, 112, 104, 4, 110, 10, 5, 106, 2, 100, 111, 11, 108, 8, 103, 0, 109, 9, 107, 104, 6, 110, 7, 4, 10, 102, 105, 5, 3, 100, 0, 106, 111, 11, 108, 8, 105, 2, 109, 104, 4, 110, 6, 107, 7, 103, 3, 1, 10, 108, 107, 111, 9, 106, 102, 2, 11, 8, 6, 110, 102, 10, 101, 1, 109, 100, 0, 12, 111, 101, 11, 100, 9, 108, 8, 104, 4, 112, 12, 110, 10, 103, 3, 108, 104, 106, 6, 110, 103, 111, 11, 109, 9, 106, 112, 111, 109),
)


def layer_kernel(sizes, row_count, width, ff, *refs):
    refs = list(refs)

    def take(n):
        taken = refs[:n]
        del refs[:n]
        return taken

    (tok_hbm, cot_hbm, wqkv_hbm, wo_hbm, w1_hbm, w2_hbm) = take(6)
    small_hbm = take(8)
    (out_ref, dx_ref, sums, vec_out) = take(4)
    (tok, cot, wqkv, wo, w1, w2, load_sems) = take(7)
    small = take(8)
    (seg_ref, gain1, shift1, bias_o, gain2, shift2, bias_1, bias_2) = small
    (a1, hat1, inv1, q, kv, prob, att, hid, hat2, inv2, a2) = take(11)
    (pre, dact, act, dpre, outacc, da, dhid, db, dout, dkv, dqkv) = take(11)
    (grads, vec, head_mask) = take(3)
    (seg_box, rim_send, rim_box, rim_sems) = take(4)
    low = jnp.bfloat16
    wide = jnp.float32
    tokens = tok.shape[0]
    rows_here = seg_ref.shape[1]
    blocks = tokens // ROWS
    groups = width // GROUP
    scale = HEAD_DIM ** (-0.5)

    link = Link(sizes["x"], row_count)
    link.signal()
    loads = [
        pltpu.make_async_copy(source, target, load_sems.at[i])
        for i, (source, target) in enumerate(
            ((tok_hbm, tok), (wqkv_hbm, wqkv), (wo_hbm, wo), (cot_hbm, cot), (w1_hbm, w1), (w2_hbm, w2)))
    ]
    small_loads = [
        pltpu.make_async_copy(source, target, load_sems.at[6 + i])
        for i, (source, target) in enumerate(zip(small_hbm, small))
    ]
    loads[0].start()
    for made in small_loads:
        made.start()
    loads[1].start()

    lane = lax.broadcasted_iota(jnp.int32, (ROWS, GROUP), 1) // HEAD_DIM
    for h in range(4):
        head_mask[pl.ds(h * ROWS, ROWS), :] = jnp.where(lane == h, 1.0, 0.0).astype(low)

    def stack_heads(block):
        return jnp.concatenate([block] * 4, axis=0) * head_mask[...]

    def pick_heads(stacked):
        picked = stacked[3 * ROWS :]
        for h in (2, 1, 0):
            picked = jnp.where(lane == h, stacked[h * ROWS : (h + 1) * ROWS], picked)
        return picked

    loads[0].wait()
    for made in small_loads:
        made.wait()

    def norm(values, gain, shift, hat_ref, inv_ref, out, span):
        centred = values - row_mean(values)
        inv = lax.rsqrt(row_mean(centred * centred) + EPSILON)
        hat = centred * inv
        hat_ref[span, :] = hat
        inv_ref[span, :] = inv
        out[span, :] = (hat * gain[...] + shift[...]).astype(low)

    @pl.loop(0, blocks)
    def _(i):
        span = aligned(i, ROWS)
        norm(tok[span, :].astype(wide), gain1, shift1, hat1, inv1, a1, span)

    loads[1].wait()
    for made in loads[2:]:
        made.start()
    for which in range(2):

        @pl.loop(0, 2)
        def _(i):
            columns = aligned(i, STACK)
            source = pl.ds(pl.multiple_of((which + 1) * width + i * STACK, STACK), STACK)
            kv[which, LON : LON + tokens, columns] = nn(a1[...], wqkv[:, source]).astype(low)

    link.await_all()
    edge = LON + tokens
    left, right = link.beside(-1), link.beside(1)
    halo = [
        remote(source, target, rim_sems, i, device)
        for i, (source, target, device) in enumerate(
            (
                (kv.at[:, pl.ds(LON, LON), :], kv.at[:, pl.ds(edge, LON), :], left),
                (kv.at[:, pl.ds(tokens, LON), :], kv.at[:, pl.ds(0, LON), :], right),
                (seg_ref, seg_box.at[1], left),
                (seg_ref, seg_box.at[0], right),
            )
        )
    ]
    for made in halo:
        made.start()

    @pl.loop(0, 2)
    def _(i):
        columns = aligned(i, STACK)
        q[:, columns] = nn(a1[...], wqkv[:, columns]).astype(low)

    tall = rows_here + 8
    slot = lax.broadcasted_iota(jnp.int32, (tall, rows_here), 0)
    place = lax.broadcasted_iota(jnp.int32, (tall, rows_here), 1)
    own = jnp.broadcast_to(seg_ref[...].astype(wide), (tall, rows_here))
    inner_seg = jnp.sum(jnp.where(slot == place + 1, own, 0.0), axis=1, keepdims=True)
    slot = lax.broadcasted_iota(jnp.int32, (tall, 1), 0)
    key = lax.broadcasted_iota(jnp.int32, (KEYS, STACK), 0)
    query = lax.broadcasted_iota(jnp.int32, (KEYS, STACK), 1) % ROWS
    gap = (query - key + 2 * LON) % LON
    near = (jnp.abs(key // LON - query // LON - 1) <= 1) & (jnp.minimum(gap, LON - gap) <= 2)
    spread_slot = lax.broadcasted_iota(jnp.int32, (tall, STACK), 0)
    spread_query = (lax.broadcasted_iota(jnp.int32, (tall, STACK), 1) % ROWS) // LON
    key_slot = key // LON

    def mask(i, seg_column):
        first = i * (ROWS // LON)
        query_seg = jnp.sum(
            jnp.where(spread_slot == spread_query + (first + 1), seg_column, 0.0), axis=0, keepdims=True)
        key_seg = jnp.zeros((KEYS, STACK), wide)
        for r in range(KEYS // LON):
            row_seg = jnp.sum(jnp.where(slot == first + r, seg_column, 0.0), axis=0, keepdims=True)
            key_seg = jnp.where(key_slot == r, row_seg, key_seg)
        return jnp.where(near & (key_seg == query_seg), 0.0, NEGATIVE)

    def attend(i, seg_column):
        span = aligned(i, ROWS)
        keys = pl.ds(i * ROWS if isinstance(i, int) else pl.multiple_of(i * ROWS, ROWS), KEYS)
        bias = mask(i, seg_column)
        for g in range(groups):
            lanes = pl.ds(g * GROUP, GROUP)
            scores = nt(kv[0, keys, lanes], stack_heads(q[span, lanes])) * scale + bias
            raised = jnp.exp(scores - jnp.max(scores, axis=0, keepdims=True))
            weights = raised * (1.0 / column_sum(raised))
            prob[i * groups + g] = weights
            mixed = tn(weights.astype(low), kv[1, keys, lanes])
            att[span, lanes] = pick_heads(mixed).astype(low)

    @pl.loop(0, (blocks - 2) // 2)
    def _(i):
        attend(2 * i + 1, inner_seg)
        attend(2 * i + 2, inner_seg)

    for made in halo:
        made.wait()
    before = jnp.where(link.row > 0, seg_box[0, :, rows_here - 1 : rows_here], -1)
    after = jnp.where(link.row < row_count - 1, seg_box[1, :, 0:1], -1)
    outer_seg = jnp.where(slot == 0, before.astype(wide), inner_seg)
    outer_seg = jnp.where(slot == rows_here + 1, after.astype(wide), outer_seg)
    attend(0, outer_seg)
    attend(blocks - 1, outer_seg)

    loads[2].wait()
    for i in range(2):
        columns = pl.ds(i * STACK, STACK)
        hid[:, columns] = tok[:, columns].astype(wide) + nn(att[...], wo[:, columns]) + bias_o[:, columns]

    @pl.loop(0, blocks)
    def _(i):
        span = aligned(i, ROWS)
        norm(hid[span, :], gain2, shift2, hat2, inv2, a2, span)

    for made in loads[3:]:
        made.wait()

    parts = []
    for i, kind in enumerate(KINDS):
        order = ORDERS[kind]
        scratch = take(len(order) + 1)
        parts.append(Part(link, grads.at[i], sums.at[i], order, scratch[:-1], scratch[-1]))
    scratch = take(len(VECTOR_ORDER) + 1)
    vectors = Vectors(link, vec, scratch[:-1], scratch[-1])
    flows = parts + [vectors]
    plan = iter(PLAN)

    def turn():
        for i in next(plan):
            if i < FINISH:
                flows[i].start()
            else:
                flows[i - FINISH].finish()

    vec[0] = jnp.zeros(vec.shape[1:], wide)
    per_row = width // STACK
    for j in range(ff // STACK):
        columns = pl.ds(j * STACK, STACK)
        spot = pl.ds((j % 2) * STACK, STACK)
        pre[...] = nn(a2[...], w1[:, columns]) + bias_1[:, columns]
        dact[...] = nt(cot[...], w2[columns, :])
        turn()

        def gelu(i, total):
            span = aligned(i, 32)
            x = pre[span, :]
            cdf = 0.5 + 0.5 * lax.erf(x * SQRT_HALF)
            act[span, columns] = (x * cdf).astype(low)
            slope = cdf + x * (jnp.exp(x * x * (-0.5)) * DENSITY)
            made = (dact[span, :] * slope).astype(low)
            dpre[span, columns] = made
            return total + jnp.sum(made.astype(wide).reshape(4, 8, STACK), axis=0)

        total = lax.fori_loop(0, tokens // 32, gelu, jnp.zeros((8, STACK), wide), unroll=True)
        vec[0, 5 + j // per_row : 6 + j // per_row, pl.ds((j % per_row) * STACK, STACK)] = column_sum(total)
        turn()
        grads[j // 2 * 2, spot, :] = tn(act[:, columns], cot[...]).astype(low)
        grads[j // 2 * 2 + 1, :, spot] = tn(a2[...], dpre[:, columns]).astype(low)
        turn()
    for i in range(2):
        columns = pl.ds(i * STACK, STACK)
        outacc[:, columns] = nn(act[...], w2[:, columns])
        turn()
    for i in range(2):
        columns = pl.ds(i * STACK, STACK)
        da[:, columns] = nt(dpre[...], w1[columns, :])
        turn()

    def norm_back(incoming, hat_ref, inv_ref, gain, span):
        hat = hat_ref[span, :]
        scaled = incoming * gain[...]
        bracket = scaled - row_mean(scaled) - hat * row_mean(scaled * hat)
        return inv_ref[span, :] * bracket, hat

    def fold(values):
        return jnp.sum(values.reshape(values.shape[0] // 8, 8, values.shape[1]), axis=0)

    def second_back(i, totals):
        span = aligned(i, ROWS)
        incoming = da[span, :]
        part, hat = norm_back(incoming, hat2, inv2, gain2, span)
        up = cot[span, :].astype(wide)
        state = up + part
        dhid[span, :] = state
        rounded = state.astype(low)
        db[span, :] = rounded
        out_ref[span, :] = (hid[span, :] + outacc[span, :] + bias_2[...]).astype(low)
        added = (rounded.astype(wide), incoming * hat, incoming, up)
        return tuple(t + fold(a) for t, a in zip(totals, added))

    zero = jnp.zeros((8, width), wide)
    totals = lax.fori_loop(0, blocks // 2, second_back, (zero,) * 4)
    turn()
    totals = lax.fori_loop(blocks // 2, blocks, second_back, totals)
    for at, total in zip((2, 3, 4, 9), totals):
        vec[0, at : at + 1, :] = column_sum(total)

    turn()
    dout[...] = nt(db[...], wo[...]).astype(low)
    made = tn(att[...], db[...]).astype(low)
    for g in range(groups):
        grads[8 + g, :, 3 * GROUP :] = made[:, g * GROUP : (g + 1) * GROUP]
    turn()

    dkv[...] = jnp.zeros(dkv.shape, wide)

    def attention_back(g):
        lanes = pl.ds(g * GROUP, GROUP)

        def one(i):
            span = aligned(i, ROWS)
            keys = pl.ds(i * ROWS if isinstance(i, int) else pl.multiple_of(i * ROWS, ROWS), KEYS)
            stacked_out = stack_heads(dout[span, lanes])
            stacked_query = stack_heads(q[span, lanes])
            weights = prob[i * groups + g]
            slopes = nt(kv[1, keys, lanes], stacked_out)
            centre = column_sum(weights * slopes)
            ds = (weights * (slopes - centre)).astype(low)
            dkv[0, keys, lanes] += nn(ds, stacked_query) * scale
            dkv[1, keys, lanes] += nn(weights.astype(low), stacked_out)
            dqkv[span, lanes] = (pick_heads(tn(ds, kv[0, keys, lanes])) * scale).astype(low)

        for i in range(blocks):
            one(i)
            turn()

    def rim_copies(g):
        return [remote(rim_send.at[g, side], rim_box.at[g, side], rim_sems, 4 + 2 * g + side, device)
                for side, device in ((0, left), (1, right))]

    def rim_start(g):
        lanes = pl.ds(g * GROUP, GROUP)
        rim_send[g, 0] = dkv[:, 0:LON, lanes].astype(low)
        rim_send[g, 1] = dkv[:, edge : edge + LON, lanes].astype(low)
        for copy in rim_copies(g):
            copy.start()

    def rim_finish(g):
        for copy in rim_copies(g):
            copy.wait()
        lanes = pl.ds(g * GROUP, GROUP)
        dkv[:, tokens : tokens + LON, lanes] += rim_box[g, 0].astype(wide)
        dkv[:, LON : 2 * LON, lanes] += rim_box[g, 1].astype(wide)

    def triple_products(g):
        for which in range(2):
            columns = pl.ds((which + 1) * width + g * GROUP, GROUP)
            dqkv[:, columns] = dkv[which, LON : LON + tokens, pl.ds(g * GROUP, GROUP)].astype(low)
        joined = jnp.concatenate(
            [dqkv[:, pl.ds(which * width + g * GROUP, GROUP)] for which in range(3)], axis=1)
        grads[8 + g, :, : 3 * GROUP] = tn(a1[...], joined).astype(low)
        turn()

    for g in range(groups):
        attention_back(g)
        if g:
            rim_finish(g - 1)
        rim_start(g)
        if g:
            triple_products(g - 1)
    da[...] = nt(dqkv[:, :width], wqkv[:, :width])
    rim_finish(groups - 1)
    triple_products(groups - 1)

    da[...] += nt(dqkv[:, width:], wqkv[:, width:])
    turn()

    def first_back(i, totals):
        span = aligned(i, ROWS)
        incoming = da[span, :]
        part, hat = norm_back(incoming, hat1, inv1, gain1, span)
        dx_ref[span, :] = (dhid[span, :] + part).astype(low)
        return totals[0] + fold(incoming * hat), totals[1] + fold(incoming)

    totals = lax.fori_loop(0, blocks, first_back, (zero,) * 2)
    for at, total in zip((0, 1), totals):
        vec[0, at : at + 1, :] = column_sum(total)
    turn()
    turn()
    vec_out[...] = vec[len(VECTOR_ORDER)]
    for part in parts:
        part.settle()


def run_layer(arrays, dp_count, row_count):
    (tokens, cotangent, wqkv, wo, w1, w2, seg, *vectors) = arrays
    count, width = tokens.shape
    ff = w1.shape[1]
    sizes = link_sizes(dp_count, row_count)
    low, wide = jnp.bfloat16, jnp.float32
    keys = count + 2 * LON
    blocks = count // ROWS
    vm = pltpu.VMEM
    square = (count, width)
    vec_shape = (16, width)
    scratch = [vm(square, low), vm(square, low), vm(wqkv.shape, low), vm(wo.shape, low), vm(w1.shape, low),
               vm(w2.shape, low), pltpu.SemaphoreType.DMA((14,))]
    scratch += [vm(v.shape, v.dtype) for v in (seg, *vectors)]
    scratch += [vm(square, low), vm(square, wide), vm((count, 1), wide), vm(square, low), vm((2, keys, width), low),
                vm((blocks * width // GROUP, KEYS, STACK), wide), vm(square, low), vm(square, wide),
                vm(square, wide), vm((count, 1), wide), vm(square, low)]
    scratch += [vm((count, STACK), wide), vm((count, STACK), wide), vm((count, ff), low), vm((count, ff), low),
                vm(square, wide), vm(square, wide), vm(square, wide), vm(square, low), vm(square, low),
                vm((2, keys, width), wide), vm((count, 3 * width), low)]
    count_parts = len(KINDS)
    slabs = (count_parts, width, width)
    scratch += [vm(slabs, low), vm((5,) + vec_shape, wide),
                vm((STACK, GROUP), low)]
    rims = (width // GROUP, 2, 2, LON, GROUP)
    scratch += [vm((2,) + seg.shape, jnp.int32), vm(rims, low), vm(rims, low),
                pltpu.SemaphoreType.DMA((2, 12))]
    for kind in KINDS:
        scratch += part_scratch((width, width), ORDERS[kind], sizes)
    scratch += vector_scratch(vec_shape, sizes)
    shapes = [(square, low), (square, low), (slabs, low), (vec_shape, wide)]
    vmem = pl.BlockSpec(memory_space=pltpu.VMEM)
    anywhere = pl.BlockSpec(memory_space=pl.ANY)
    return pl.pallas_call(
        partial(layer_kernel, sizes, row_count, width, ff),
        out_shape=[vm(*s) for s in shapes],
        in_specs=[pl.BlockSpec(memory_space=pltpu.HBM)] * 14,
        out_specs=[vmem] * 4,
        scratch_shapes=scratch,
        compiler_params=pltpu.CompilerParams(collective_id=1, has_side_effects=True, vmem_limit_bytes=54 << 20),
        name="layer",
    )(*arrays)


def widen_kernel(factor, width, out_in, dx_in, slabs, vec_ref, out_hbm, dx_hbm, triple_hbm, output_hbm,
                 expand_hbm, reduce_hbm, *refs):
    vector_outs, (triple, output, expand, reduce, out_sems) = refs[:7], refs[7:]
    wide = jnp.float32
    count = slabs.shape[0]
    moves = []

    def send(source, target):
        moves.append(pltpu.make_async_copy(source, target, out_sems.at[len(moves)]))
        moves[-1].start()

    send(out_in, out_hbm)
    send(dx_in, dx_hbm)

    def convert(i, store):
        @pl.loop(0, width // 32)
        def _(at):
            span = pl.ds(pl.multiple_of(at * 32, 32), 32)
            store(span, slabs[i, span, :].astype(wide) * factor)

    def store_reduce(i, span, made):
        reduce[i, span, :] = made

    def store_expand(i, span, made):
        expand[i, span, :] = made

    def store_group(g, span, made):
        for which in range(3):
            triple[span, pl.ds(which * width + g * GROUP, GROUP)] = made[:, which * GROUP : (which + 1) * GROUP]
        output[span, pl.ds(g * GROUP, GROUP)] = made[:, 3 * GROUP :]

    for i in range(4):
        convert(2 * i, partial(store_reduce, i))
        send(reduce.at[i], reduce_hbm.at[i])
        convert(2 * i + 1, partial(store_expand, i))
        send(expand.at[i], expand_hbm.at[:, pl.ds(i * width, width)])
        if i == 1:
            for g in range(count - 8):
                convert(8 + g, partial(store_group, g))
            send(triple, triple_hbm)
            send(output, output_hbm)
    values = vec_ref[...] * factor
    for at, ref in zip((0, 1, 2, 3, 4, 9), vector_outs[:5] + vector_outs[6:]):
        ref[...] = values[at : at + 1]
    for i in range(vector_outs[5].shape[1] // width):
        vector_outs[5][:, i * width : (i + 1) * width] = values[5 + i : 6 + i]
    for move in moves:
        move.wait()


def widen(layer_out, input_grad, sums, vec, factor):
    count, width, _ = sums.shape
    ff = 4 * width
    square = layer_out.shape
    big = [(width, 3 * width), (width, width), (width, ff), (4, width, width)]
    small = [(1, width)] * 5 + [(1, ff), (1, width)]
    wide = jnp.float32
    vm = pltpu.VMEM
    anywhere = pl.BlockSpec(memory_space=pl.ANY)
    vmem = pl.BlockSpec(memory_space=pltpu.VMEM)
    made = pl.pallas_call(
        partial(widen_kernel, factor, width),
        out_shape=[jax.ShapeDtypeStruct(square, layer_out.dtype)] * 2
        + [jax.ShapeDtypeStruct(s, wide) for s in big + small],
        in_specs=[vmem] * 4,
        out_specs=[anywhere] * 6 + [vmem] * 7,
        scratch_shapes=[vm(big[0], wide), vm(big[1], wide), vm(big[3], wide),
                        vm(big[3], wide),
                        pltpu.SemaphoreType.DMA((12,))],
        compiler_params=pltpu.CompilerParams(vmem_limit_bytes=40 << 20),
        name="widen",
    )(layer_out, input_grad, sums, vec)
    return (*made[:5], made[5].reshape(ff, width), *made[6:])


def body(
    tokens,
    segment_ids,
    first_gain,
    first_shift,
    triple_weight,
    output_weight,
    output_bias,
    second_gain,
    second_shift,
    expand_weight,
    expand_bias,
    reduce_weight,
    reduce_bias,
    cotangent,
):
    dp_count, row_count = lax.axis_size("dp"), lax.axis_size("rows")
    flat = [
        v.reshape(1, -1)
        for v in (segment_ids, first_gain, first_shift, output_bias, second_gain, second_shift, expand_bias, reduce_bias)
    ]
    made = run_layer(
        (tokens, cotangent, triple_weight, output_weight, expand_weight, reduce_weight, *flat), dp_count, row_count)
    factor = (tokens.shape[0] * dp_count * row_count) ** (-0.5)
    layer_out, input_grad, triple, output, expand, reduce, *small = widen(*made, factor)
    small = [v.reshape(-1) for v in small]
    return (
        layer_out, input_grad, small[0], small[1], triple, output, small[2], small[3], small[4],
        expand, small[5], reduce, small[6],
    )


def solution(mesh):
    placed = (
        P(("dp", "rows"), None),
        P(("dp", "rows")),
        P(),
        P(),
        P(),
        P(),
        P(),
        P(),
        P(),
        P(),
        P(),
        P(),
        P(),
        P(("dp", "rows"), None),
    )
    return jax.shard_map(
        body,
        mesh=mesh,
        in_specs=placed,
        out_specs=(
            P(("dp", "rows"), None),
            P(("dp", "rows"), None),
            P(),
            P(),
            P(),
            P(),
            P(),
            P(),
            P(),
            P(),
            P(),
            P(),
            P(),
        ),
        check_vma=False,
    )
```
